32 devices in a mesh: tm: 8 (over z, y), chan: 4 (over x, core).
Axes of the slice: x: 2, y: 2, z: 4, core: 2. Of those that a mesh axis runs over, the one named last changes fastest.
Arguments:
- series_value: bfloat16 [4096, 1024], P('tm', 'chan'), may hold values from -6 to 6
- series_gate: bfloat16 [4096, 1024], P('tm', 'chan'), may hold values from -6 to 6
- long_filter: bfloat16 [4096, 1024], P('tm', 'chan'), may hold values from -2 to 2
- step_table: float32 [200, 1024], P(None, 'chan'), may hold values from -3 to 3
- diffusion_step: int32 [1], replicated, may hold values from 0 to 199
- mask_embed: float32 [1024], P('chan'), may hold values from -3 to 3
- block_flags: int32 [64], P('tm'), may hold values 0 or 1
- skip_gain: float32 [1024], P('chan'), may hold values from 0.5 to 1.5
- norm_gain: float32 [1024], replicated, may hold values from 0.5 to 2
- w_gate: bfloat16 [1024, 2048], P(None, 'chan'), may hold values from -0.1875 to 0.1875
- w_up: bfloat16 [1024, 2048], P(None, 'chan'), may hold values from -0.1875 to 0.1875
- w_down: bfloat16 [2048, 1024], P('chan'), may hold values from -0.125 to 0.125
Outputs:
- layer_out: bfloat16 [4096, 1024], P('tm', 'chan')
The draws below stay inside these ranges and needn't reach their ends.
All inputs are finite; a program needn't handle non-finite values. No bound on the sum of `block_flags` on one device may be relied on, other than what follows from the above.
Results may differ from the reference program's by a relative error of at most 0.014.
Values may be sent and summed in bfloat16 or wider, within the bound.
No kernel may reach another device: no remote copies, remote signals or barrier semaphores. Data moves between devices by JAX's collectives and lax.ppermute only.
A program may use at most 128 MiB of HBM per device.

```python
import math
import jax
import jax.numpy as jnp
from jax import lax

C = 1024
FF = 2048
FLAGBLK = 64
STEPS = 200
LENGTH = 4096
FLAGS = 64


def draw_long_filter(key, part):
    key_noise, key_kind, key_slow, key_fast = jax.random.split(key, 4)
    lag_steps = jnp.arange(LENGTH, dtype=jnp.float32)[:, None]
    noise = jax.random.normal(key_noise, (LENGTH, C), jnp.float32)
    slow_mask = jax.random.bernoulli(key_kind, 0.5, (1, C))
    slow_rate = jax.random.uniform(key_slow, (1, C), jnp.float32, 0.2, 1.0) / LENGTH
    fast_rate = 1.0 / jax.random.uniform(key_fast, (1, C), jnp.float32, 30.0, 50.0)
    decay_rate = jnp.where(slow_mask, slow_rate, fast_rate)
    return (noise * jnp.sqrt(2.0 * decay_rate) * jnp.exp(-decay_rate * lag_steps)).astype(jnp.bfloat16)


def place_ends(values, own_key, low, top_value):
    shape = values.shape
    index_at = [jax.random.randint(jax.random.fold_in(own_key, axis), (), 0, shape[axis]) for axis in range(len(shape))]
    values = values.at[tuple(index_at)].set(low)
    longest = shape.index(max(shape))
    index_at[longest] = (index_at[longest] + 1) % shape[longest]
    return values.at[tuple(index_at)].set(top_value)


def steps_of(stream_key, shape, cuts, smallest, high):
    def one(axis_at, shards_of):
        draws = jax.random.uniform(jax.random.fold_in(jax.random.fold_in(stream_key, 6), axis_at), (shards_of,), jnp.float32, smallest / len(cuts), high / len(cuts))
        return jnp.repeat(jnp.exp(draws), shape[axis_at] // shards_of).reshape((-1,) + (1,) * (len(shape) - axis_at - 1))

    factor_of = one(*cuts[0])
    for cut in cuts[1:]:
        factor_of = factor_of * one(*cut)
    return factor_of


def gaussian(rng, dims, width, reach, cuts=(), kind=jnp.bfloat16):
    level = steps_of(rng, dims, cuts, -0.22, 0.18) if cuts else 1.0
    result = jax.random.normal(rng, dims, jnp.float32) * width * level
    return jnp.minimum(jnp.maximum(result, -reach), reach).astype(kind)


def setup_inputs(seed: int = 0) -> dict:
    key_of = jax.random.split(jax.random.key(seed), 13)
    return {
        "series_value": gaussian(key_of[0], (LENGTH, C), 1.0, 6.0, ((0, 8), (1, 4))),
        "series_gate": gaussian(key_of[1], (LENGTH, C), 1.0, 6.0, ((0, 8), (1, 4))),
        "long_filter": draw_long_filter(jax.random.fold_in(key_of[12], 71), 0),
        "step_table": gaussian(key_of[3], (STEPS, C), 0.5, 3.0, ((1, 4),), jnp.float32),
        "diffusion_step": jax.random.randint(key_of[4], (1,), 0, STEPS).astype(jnp.int32),
        "mask_embed": gaussian(key_of[5], (C,), 0.5, 3.0, ((0, 4),), jnp.float32),
        "block_flags": place_ends((jax.random.randint(key_of[6], (FLAGS,), 0, 2) < 1).astype(jnp.int32), jax.random.fold_in(key_of[6], 1), 0, 1),
        "skip_gain": jnp.clip(0.5 + 1.0 * jax.random.uniform(key_of[7], (C,), jnp.float32) ** steps_of(key_of[7], (C,), ((0, 4),), -0.2, 0.2), 0.5, 1.5),
        "norm_gain": jnp.clip(jnp.exp(jax.random.uniform(key_of[8], (C,), jnp.float32, math.log(0.5), math.log(2.0))), 0.5, 2.0),
        "w_gate": gaussian(key_of[9], (C, FF), C ** -0.5, 0.1875, ((1, 4),)),
        "w_up": gaussian(key_of[10], (C, FF), C ** -0.5, 0.1875, ((1, 4),)),
        "w_down": gaussian(key_of[11], (FF, C), FF ** -0.5, 0.125, ((0, 4),)),
    }


def convolve_block(both):
    signal_spec = jnp.fft.rfft(both[0], n=2 * LENGTH, axis=0)
    filter_spec = jnp.fft.rfft(both[1], n=2 * LENGTH, axis=0)
    return jnp.fft.irfft(signal_spec * filter_spec, n=2 * LENGTH, axis=0)[:LENGTH]

def reference(series_value, series_gate, long_filter, step_table, diffusion_step, mask_embed, block_flags, skip_gain, norm_gain, w_gate, w_up, w_down):
    embed = step_table[diffusion_step[0]]
    flags = jnp.broadcast_to(block_flags[:, None], (FLAGS, FLAGBLK)).reshape(LENGTH).astype(jnp.float32)
    summed = series_value.astype(jnp.float32) + embed[None, :] + flags[:, None] * mask_embed[None, :]
    inputs_low = summed.astype(jnp.bfloat16)
    inputs = inputs_low.astype(jnp.float32)
    filter_wide = long_filter.astype(jnp.float32)
    block = math.gcd(C, 128)
    split_in = inputs.reshape(LENGTH, C // block, block).transpose(1, 0, 2)
    split_filter = filter_wide.reshape(LENGTH, C // block, block).transpose(1, 0, 2)
    convolved = lax.map(convolve_block, (split_in, split_filter))
    convolved = convolved.transpose(1, 0, 2).reshape(LENGTH, C).astype(inputs.dtype)
    mixed = (series_gate.astype(jnp.float32) * (convolved + skip_gain[None, :] * inputs)).astype(jnp.bfloat16)
    mixed_wide = mixed.astype(jnp.float32)
    square_mean = lax.optimization_barrier(jnp.mean(mixed_wide * mixed_wide, axis=-1, keepdims=True))
    normed = (mixed_wide * lax.rsqrt(square_mean + 1e-06) * norm_gain[None, :]).astype(jnp.bfloat16)
    gate_proj = jnp.dot(normed, w_gate, preferred_element_type=jnp.float32)
    up_proj = jnp.dot(normed, w_up, preferred_element_type=jnp.float32)
    hidden = (jax.nn.silu(gate_proj) * up_proj).astype(jnp.bfloat16)
    down_proj = jnp.dot(hidden, w_down, preferred_element_type=jnp.float32)
    return (mixed_wide + down_proj).astype(jnp.bfloat16)
```

```python
import math

import jax
import jax.numpy as jnp
import numpy as np
from jax import lax
from jax.experimental import pallas as pl
from jax.experimental.pallas import tpu as pltpu
from jax.sharding import PartitionSpec as P

FLAGBLK = 64
bf16 = jnp.bfloat16
f32 = jnp.float32


def split_table(table):
    high = table.astype(bf16)
    low = (table - high.astype(np.float64)).astype(bf16)
    return high, low


def block_tables(block):
    freq = np.concatenate([np.arange(0, block, 2), np.arange(1, block, 2)])
    time = np.arange(block)
    turn = np.pi * ((2 * freq[None, :] + 1) * time[:, None] % (4 * block)) / (2 * block)
    forward = np.concatenate([np.cos(turn), -np.sin(turn)], axis=1)
    turn = np.pi * ((2 * freq[:, None] + 1) * (block + time[None, :]) % (4 * block)) / (2 * block)
    inverse = np.concatenate([np.cos(turn), -np.sin(turn)], axis=0) / block
    return split_table(forward) + split_table(inverse)


def dot(left, right):
    return jnp.dot(left, right, preferred_element_type=f32)


def prepare_kernel(step_ref, flags_ref, value_ref, filter_ref, table_ref, mask_ref, out_ref):
    embed = table_ref[pl.ds(step_ref[0], 1), :]
    mask = mask_ref[...]
    parts = []
    for at in range(value_ref.shape[0] // FLAGBLK):
        rows = value_ref[at * FLAGBLK : (at + 1) * FLAGBLK, :].astype(f32)
        parts.append((rows + embed + flags_ref[at].astype(f32) * mask).astype(bf16))
    inputs = jnp.concatenate(parts, axis=0)
    shape = (out_ref.shape[0], out_ref.shape[2], out_ref.shape[3])
    out_ref[:, 0] = inputs.T.reshape(shape)
    out_ref[:, 1] = filter_ref[...].T.reshape(shape)


def convolve_kernel(
    both_ref, fh_ref, fl_ref, gh_ref, gl_ref, skip_ref, out_ref, x_ref, h_ref, z_ref
):
    tm, _, chans, rows = both_ref.shape
    block = rows // 2
    half = block // 2
    nb = 2 * tm
    for which, dst in ((0, x_ref), (1, h_ref)):
        for part in range(2):
            data = both_ref[:, which, :, part * block : (part + 1) * block]
            data = data.reshape(tm * chans, block)
            spec = dot(data, fh_ref[...]) + dot(data, fl_ref[...])
            dst[:, part] = spec.reshape(tm, chans, 2 * block)

    def read(ref, at, sub, lanes):
        return ref[at // 2, at % 2, sub, lanes]

    def windows(at, sub, odd):
        re = slice(odd * half, (odd + 1) * half)
        im = slice(block + odd * half, block + (odd + 1) * half)
        return re, im

    def tile(step, carry):
        sub = pl.ds(pl.multiple_of(step * 8, 8), 8)
        for odd in range(2):
            for low in range(0, half, 128):
                width = min(128, half)
                re = slice(odd * half + low, odd * half + low + width)
                im = slice(block + odd * half + low, block + odd * half + low + width)
                if nb <= 16:
                    hr, hi = [], []
                    for d in range(nb):
                        cur_re, cur_im = read(h_ref, d, sub, re), read(h_ref, d, sub, im)
                        if d == 0:
                            wr, wi = (-cur_im, cur_re) if odd else (cur_im, -cur_re)
                        elif odd:
                            wr, wi = prev_re - cur_im, prev_im + cur_re
                        else:
                            wr, wi = prev_re + cur_im, prev_im - cur_re
                        prev_re, prev_im = cur_re, cur_im
                        hr.append(wr)
                        hi.append(wi)
                    for a in range(nb):
                        zr, zi = None, None
                        for d in range(a + 1):
                            xr, xi = read(x_ref, a - d, sub, re), read(x_ref, a - d, sub, im)
                            tr = xr * hr[d] - xi * hi[d]
                            ti = xr * hi[d] + xi * hr[d]
                            zr, zi = (tr, ti) if zr is None else (zr + tr, zi + ti)
                        z_ref[a // 2, a % 2, sub, re] = zr
                        z_ref[a // 2, a % 2, sub, im] = zi
                else:

                    def out_block(a, carry):
                        def pair(d, acc):
                            before = jnp.maximum(d - 1, 0)
                            keep = (d > 0).astype(f32)
                            pr = keep * read(h_ref, before, sub, re)
                            pi = keep * read(h_ref, before, sub, im)
                            cr, ci = read(h_ref, d, sub, re), read(h_ref, d, sub, im)
                            wr, wi = (pr - ci, pi + cr) if odd else (pr + ci, pi - cr)
                            xr, xi = read(x_ref, a - d, sub, re), read(x_ref, a - d, sub, im)
                            return (
                                acc[0] + xr * wr - xi * wi,
                                acc[1] + xr * wi + xi * wr,
                            )

                        zero = jnp.zeros((8, width), f32)
                        zr, zi = lax.fori_loop(0, a + 1, pair, (zero, zero))
                        z_ref[a // 2, a % 2, sub, re] = zr
                        z_ref[a // 2, a % 2, sub, im] = zi
                        return carry

                    lax.fori_loop(0, nb, out_block, 0)
        return carry

    lax.fori_loop(0, chans // 8, tile, 0)
    skip = skip_ref[...]
    for part in range(2):
        spec = z_ref[:, part].reshape(tm * chans, 2 * block)
        high = spec.astype(bf16)
        low = (spec - high.astype(f32)).astype(bf16)
        conv = dot(high, gh_ref[...]) + dot(low, gh_ref[...]) + dot(high, gl_ref[...])
        inputs = both_ref[:, 0, :, part * block : (part + 1) * block].astype(f32)
        total = (conv.reshape(tm, chans, block) + skip[None] * inputs).astype(bf16)
        out_ref[:, 0, part] = total
        out_ref[:, 1, part] = total


def feed_forward_kernel(
    chan_ref,
    conv_ref,
    gate0_ref,
    gate1_ref,
    gate2_ref,
    gate3_ref,
    gain_ref,
    wg0_ref,
    wu0_ref,
    wd0_ref,
    wg1_ref,
    wu1_ref,
    wd1_ref,
    out0_ref,
    out1_ref,
    out2_ref,
    out3_ref,
    mixed_ref,
    normed_ref,
):
    here = chan_ref[0]
    rows, width = gate0_ref.shape
    total = gain_ref.shape[0] * width
    square = jnp.zeros((rows, 1), f32)
    for j, gate_ref in enumerate((gate0_ref, gate1_ref, gate2_ref, gate3_ref)):
        conv = conv_ref[here ^ j].T.astype(f32)
        mixed = (gate_ref[...].astype(f32) * conv).astype(bf16)
        mixed_ref[j] = mixed
        wide = mixed.astype(f32)
        square = square + jnp.sum(wide * wide, axis=-1, keepdims=True)
    scale = lax.rsqrt(square / total + 1e-06)
    for j in range(4):
        at = here ^ j
        normed = (mixed_ref[j].astype(f32) * scale * gain_ref[at]).astype(bf16)
        normed_ref[:, pl.ds(pl.multiple_of(at * width, width), width)] = normed
    normed = normed_ref[...]
    hidden = []
    for wg_ref, wu_ref in ((wg0_ref, wu0_ref), (wg1_ref, wu1_ref)):
        gate = dot(normed, wg_ref[...])
        up = dot(normed, wu_ref[...])
        hidden.append((gate / (1.0 + jnp.exp(-gate)) * up).astype(bf16))
    for j, out_ref in ((2, out2_ref), (3, out3_ref), (1, out1_ref), (0, out0_ref)):
        cols = pl.ds(pl.multiple_of((here ^ j) * width, width), width)
        part = dot(hidden[0], wd0_ref[:, cols]) + dot(hidden[1], wd1_ref[:, cols])
        if j < 2:
            part = part + mixed_ref[j].astype(f32)
        out_ref[...] = part.astype(bf16)


VMEM = pltpu.MemorySpace.VMEM
SMEM = pltpu.MemorySpace.SMEM


def whole(space=VMEM):
    return pl.BlockSpec(memory_space=space)


def params(mib):
    return pltpu.CompilerParams(vmem_limit_bytes=mib << 20)


def shards(
    series_value,
    series_gate,
    long_filter,
    step_table,
    diffusion_step,
    mask_embed,
    block_flags,
    skip_gain,
    norm_gain,
    w_gate,
    w_up,
    w_down,
):
    tm = lax.axis_size("tm")
    chan = lax.axis_size("chan")
    here = lax.axis_index("chan")
    rows, width = series_value.shape
    own = width // tm
    block = rows // 2
    core = here % 2

    def swap(values, bits):
        return lax.ppermute(values, "chan", [(at, at ^ bits) for at in range(chan)])

    direct = own % 16 == 0
    made = pl.pallas_call(
        prepare_kernel,
        out_shape=jax.ShapeDtypeStruct(
            (tm, 2, own, rows) if direct else (1, 2, width, rows), bf16
        ),
        in_specs=[whole(SMEM), whole(SMEM)] + [whole()] * 4,
        out_specs=whole(),
        compiler_params=params(32),
        name="prepare",
    )(
        diffusion_step,
        block_flags,
        series_value,
        long_filter,
        step_table,
        mask_embed.reshape(1, width),
    )
    if not direct:
        made = made.reshape(2, tm, own, rows).transpose(1, 0, 2, 3)
    both = lax.all_to_all(made, "tm", split_axis=0, concat_axis=0, tiled=True)

    gate_own = lax.dynamic_slice_in_dim(series_gate, core * block, block, 0)
    gate_other = lax.dynamic_slice_in_dim(series_gate, (1 - core) * block, block, 0)
    gates = (gate_own, swap(gate_other, 1), swap(gate_own, 2), swap(gate_other, 3))
    wg1, wu1, wd1 = swap(w_gate, 1), swap(w_up, 1), swap(w_down, 1)

    skip = lax.dynamic_slice_in_dim(skip_gain, lax.axis_index("tm") * own, own, 0)
    skip = skip.reshape(own, 1)
    held = own
    if not direct:
        held = -(-own // 16) * 16
        both = jnp.pad(both, ((0, 0), (0, 0), (0, held - own), (0, 0)))
        skip = jnp.pad(skip, ((0, held - own), (0, 0)))
    tables = [jnp.asarray(table) for table in block_tables(block)]
    conv = pl.pallas_call(
        convolve_kernel,
        out_shape=jax.ShapeDtypeStruct((tm, 2, 2, held, block), bf16),
        in_specs=[whole()] * 6,
        out_specs=whole(),
        scratch_shapes=[pltpu.VMEM((tm, 2, held, 2 * block), f32)] * 3,
        compiler_params=params(48),
        name="convolve",
    )(both, *tables, skip)
    if not direct:
        conv = conv[:, :, :, :own]
    conv = lax.all_to_all(
        conv.reshape(tm * chan, own, block), ("tm", "chan"), split_axis=0, concat_axis=0, tiled=True
    )
    conv = conv.reshape(tm, chan, own, block).transpose(1, 0, 2, 3).reshape(chan, width, block)

    outs = pl.pallas_call(
        feed_forward_kernel,
        out_shape=[jax.ShapeDtypeStruct((block, width), bf16)] * 4,
        in_specs=[whole(SMEM)] + [whole()] * 12,
        out_specs=[whole()] * 4,
        scratch_shapes=[
            pltpu.VMEM((4, block, width), bf16),
            pltpu.VMEM((block, 4 * width), bf16),
        ],
        compiler_params=params(48),
        name="feed_forward",
    )(
        here.reshape(1).astype(jnp.int32),
        conv,
        *gates,
        norm_gain.reshape(chan, 1, width),
        w_gate,
        w_up,
        w_down,
        wg1,
        wu1,
        wd1,
    )
    same = outs[0].astype(f32) + swap(outs[2], 2).astype(f32)
    other = swap(outs[1], 1).astype(f32) + swap(outs[3], 3).astype(f32)
    first = jnp.where(core == 0, same, other).astype(bf16)
    second = jnp.where(core == 0, other, same).astype(bf16)
    return jnp.concatenate([first, second], axis=0)


def solution(mesh):
    placed = (
        P("tm", "chan"),
        P("tm", "chan"),
        P("tm", "chan"),
        P(None, "chan"),
        P(),
        P("chan"),
        P("tm"),
        P("chan"),
        P(),
        P(None, "chan"),
        P(None, "chan"),
        P("chan", None),
    )
    return jax.shard_map(
        shards, mesh=mesh, in_specs=placed, out_specs=P("tm", "chan"), check_vma=False
    )
```

```python
import functools

import jax
import jax.numpy as jnp
import numpy as np
from jax import lax
from jax.experimental import pallas as pl
from jax.experimental.pallas import tpu as pltpu
from jax.sharding import PartitionSpec as P

FLAGBLK = 64
bf16 = jnp.bfloat16
f32 = jnp.float32


def split_table(table):
    high = table.astype(bf16)
    low = (table - high.astype(np.float64)).astype(bf16)
    return high, low


def block_tables(block):
    freq = np.concatenate([np.arange(0, block, 2), np.arange(1, block, 2)])
    time = np.arange(block)
    turn = np.pi * ((2 * freq[None, :] + 1) * time[:, None] % (4 * block)) / (2 * block)
    forward = np.concatenate([np.cos(turn), -np.sin(turn)], axis=1)
    turn = np.pi * ((2 * freq[:, None] + 1) * (block + time[None, :]) % (4 * block)) / (2 * block)
    inverse = np.concatenate([np.cos(turn), -np.sin(turn)], axis=0) / block
    return split_table(forward) + split_table(inverse)


def dot(left, right):
    return jnp.dot(left, right, preferred_element_type=f32)


def start_loads(pairs, sems):
    loads = [
        pltpu.make_async_copy(src, dst, sems.at[at]) for at, (src, dst) in enumerate(pairs)
    ]
    for load in loads:
        load.start()
    return loads


def prepare_kernel(
    step_ref,
    flags_hbm,
    value_hbm,
    filter_hbm,
    table_hbm,
    mask_hbm,
    out_hbm,
    flags_ref,
    value_ref,
    filter_ref,
    table_ref,
    mask_ref,
    out_ref,
    sems,
    out_sems,
):
    loads = start_loads(
        (
            (filter_hbm, filter_ref),
            (value_hbm, value_ref),
            (flags_hbm, flags_ref),
            (table_hbm, table_ref),
            (mask_hbm, mask_ref),
        ),
        sems,
    )
    rows, width = value_ref.shape
    groups = out_ref.shape[0]
    lanes = 128
    stores = []

    def store(which, low, values):
        share = groups * lanes // width
        first = groups * low // width
        part = out_ref.at[pl.ds(first, share), which]
        part[...] = values.T.reshape(part.shape)
        copy = pltpu.make_async_copy(
            part, out_hbm.at[pl.ds(first, share), which], out_sems.at[len(stores)]
        )
        copy.start()
        stores.append(copy)

    steps = width // lanes if groups * lanes % width == 0 else 1
    lanes = width // steps
    loads[0].wait()
    for low in range(0, width, lanes):
        store(1, low, filter_ref[:, low : low + lanes])
    for load in loads[1:]:
        load.wait()
    embed = table_ref[pl.ds(step_ref[0], 1), :]
    mask = mask_ref[...]
    for low in range(0, width, lanes):
        here = slice(low, low + lanes)
        parts = []
        for at in range(rows // FLAGBLK):
            values = value_ref[at * FLAGBLK : (at + 1) * FLAGBLK, here].astype(f32)
            flag = flags_ref[at].astype(f32)
            parts.append((values + embed[:, here] + flag * mask[:, here]).astype(bf16))
        store(0, low, jnp.concatenate(parts, axis=0))
    for copy in stores:
        copy.wait()


def convolve_kernel(
    both_ref, fh_hbm, fl_hbm, gh_hbm, gl_hbm, skip_ref, out_ref,
    x_ref, h_ref, z_ref, fh_ref, fl_ref, gh_ref, gl_ref, sems
):
    loads = start_loads(
        ((fh_hbm, fh_ref), (fl_hbm, fl_ref), (gh_hbm, gh_ref), (gl_hbm, gl_ref)), sems
    )
    tm, _, chans, rows = both_ref.shape
    block = rows // 2
    half = block // 2
    nb = 2 * tm
    loads[0].wait()
    loads[1].wait()
    for which, dst in ((0, x_ref), (1, h_ref)):
        for part in range(2):
            data = both_ref[:, which, :, part * block : (part + 1) * block]
            data = data.reshape(tm * chans, block)
            spec = dot(data, fh_ref[...]) + dot(data, fl_ref[...])
            dst[:, part] = spec.reshape(tm, chans, 2 * block)

    def read(ref, at, sub, lanes):
        return ref[at // 2, at % 2, sub, lanes]

    def windows(at, sub, odd):
        re = slice(odd * half, (odd + 1) * half)
        im = slice(block + odd * half, block + (odd + 1) * half)
        return re, im

    def tile(step, carry):
        sub = pl.ds(pl.multiple_of(step * 8, 8), 8)
        for odd in range(2):
            for low in range(0, half, 128):
                width = min(128, half)
                re = slice(odd * half + low, odd * half + low + width)
                im = slice(block + odd * half + low, block + odd * half + low + width)
                if nb <= 16:
                    hr, hi = [], []
                    for d in range(nb):
                        cur_re, cur_im = read(h_ref, d, sub, re), read(h_ref, d, sub, im)
                        if d == 0:
                            wr, wi = (-cur_im, cur_re) if odd else (cur_im, -cur_re)
                        elif odd:
                            wr, wi = prev_re - cur_im, prev_im + cur_re
                        else:
                            wr, wi = prev_re + cur_im, prev_im - cur_re
                        prev_re, prev_im = cur_re, cur_im
                        hr.append(wr)
                        hi.append(wi)
                    for a in range(nb):
                        zr, zi = None, None
                        for d in range(a + 1):
                            xr, xi = read(x_ref, a - d, sub, re), read(x_ref, a - d, sub, im)
                            tr = xr * hr[d] - xi * hi[d]
                            ti = xr * hi[d] + xi * hr[d]
                            zr, zi = (tr, ti) if zr is None else (zr + tr, zi + ti)
                        z_ref[a // 2, a % 2, sub, re] = zr
                        z_ref[a // 2, a % 2, sub, im] = zi
                else:

                    def out_block(a, carry):
                        def pair(d, acc):
                            before = jnp.maximum(d - 1, 0)
                            keep = (d > 0).astype(f32)
                            pr = keep * read(h_ref, before, sub, re)
                            pi = keep * read(h_ref, before, sub, im)
                            cr, ci = read(h_ref, d, sub, re), read(h_ref, d, sub, im)
                            wr, wi = (pr - ci, pi + cr) if odd else (pr + ci, pi - cr)
                            xr, xi = read(x_ref, a - d, sub, re), read(x_ref, a - d, sub, im)
                            return (
                                acc[0] + xr * wr - xi * wi,
                                acc[1] + xr * wi + xi * wr,
                            )

                        zero = jnp.zeros((8, width), f32)
                        zr, zi = lax.fori_loop(0, a + 1, pair, (zero, zero))
                        z_ref[a // 2, a % 2, sub, re] = zr
                        z_ref[a // 2, a % 2, sub, im] = zi
                        return carry

                    lax.fori_loop(0, nb, out_block, 0)
        return carry

    lax.fori_loop(0, chans // 8, tile, 0)
    loads[2].wait()
    loads[3].wait()
    skip = skip_ref[...]
    for part in range(2):
        spec = z_ref[:, part].reshape(tm * chans, 2 * block)
        high = spec.astype(bf16)
        low = (spec - high.astype(f32)).astype(bf16)
        conv = dot(high, gh_ref[...]) + dot(low, gh_ref[...]) + dot(high, gl_ref[...])
        inputs = both_ref[:, 0, :, part * block : (part + 1) * block].astype(f32)
        total = (conv.reshape(tm, chans, block) + skip[None] * inputs).astype(bf16)
        out_ref[:, 0, part] = total
        out_ref[:, 1, part] = total


def feed_forward_kernel(
    chan_ref,
    conv_ref,
    gate0_ref,
    gate1_ref,
    gate2_ref,
    gate3_ref,
    gain_hbm,
    wg0_hbm,
    wu0_hbm,
    wg1_hbm,
    wu1_hbm,
    wd0_hbm,
    wd1_hbm,
    out0_ref,
    out1_hbm,
    out2_hbm,
    out3_hbm,
    mixed_ref,
    normed_ref,
    part_ref,
    gain_ref,
    wg0_ref,
    wu0_ref,
    wg1_ref,
    wu1_ref,
    wd0_ref,
    wd1_ref,
    sems,
    load_sems,
):
    loads = start_loads(
        (
            (gain_hbm, gain_ref),
            (wg0_hbm, wg0_ref),
            (wu0_hbm, wu0_ref),
            (wg1_hbm, wg1_ref),
            (wu1_hbm, wu1_ref),
            (wd0_hbm, wd0_ref),
            (wd1_hbm, wd1_ref),
        ),
        load_sems,
    )
    here = chan_ref[0]
    rows, width = gate0_ref.shape
    total = gain_ref.shape[0] * width
    square = jnp.zeros((rows, 1), f32)
    for j, gate_ref in enumerate((gate0_ref, gate1_ref, gate2_ref, gate3_ref)):
        conv = conv_ref[:, here ^ j].reshape(width, rows).T.astype(f32)
        mixed = (gate_ref[...].astype(f32) * conv).astype(bf16)
        mixed_ref[j] = mixed
        wide = mixed.astype(f32)
        square = square + jnp.sum(wide * wide, axis=-1, keepdims=True)
    loads[0].wait()
    scale = lax.rsqrt(square / total + 1e-06)
    for j in range(4):
        at = here ^ j
        normed = (mixed_ref[j].astype(f32) * scale * gain_ref[at]).astype(bf16)
        normed_ref[:, pl.ds(pl.multiple_of(at * width, width), width)] = normed
    normed = normed_ref[...]
    hidden = []
    for at, (wg_ref, wu_ref) in enumerate(((wg0_ref, wu0_ref), (wg1_ref, wu1_ref))):
        loads[1 + 2 * at].wait()
        loads[2 + 2 * at].wait()
        gate = dot(normed, wg_ref[...])
        up = dot(normed, wu_ref[...])
        hidden.append((gate / (1.0 + jnp.exp(-gate)) * up).astype(bf16))
    loads[5].wait()
    loads[6].wait()
    sends = []
    for j, out_hbm in ((2, out2_hbm), (3, out3_hbm), (1, out1_hbm), (0, None)):
        cols = pl.ds(pl.multiple_of((here ^ j) * width, width), width)
        part = dot(hidden[0], wd0_ref[:, cols]) + dot(hidden[1], wd1_ref[:, cols])
        if j < 2:
            part = part + mixed_ref[j].astype(f32)
        if out_hbm is None:
            out0_ref[...] = part.astype(bf16)
        else:
            part_ref[j - 1] = part.astype(bf16)
            send = pltpu.make_async_copy(part_ref.at[j - 1], out_hbm, sems.at[j - 1])
            send.start()
            sends.append(send)
    for send in sends:
        send.wait()


def finish_kernel(core_ref, own_ref, side_ref, core1_ref, side1_ref, out_ref):
    block = own_ref.shape[0]
    same = pl.ds(pl.multiple_of(core_ref[0] * block, block), block)
    other = pl.ds(pl.multiple_of((1 - core_ref[0]) * block, block), block)
    out_ref[same, :] = (own_ref[...].astype(f32) + side_ref[...].astype(f32)).astype(bf16)
    out_ref[other, :] = (core1_ref[...].astype(f32) + side1_ref[...].astype(f32)).astype(bf16)


VMEM = pltpu.MemorySpace.VMEM
SMEM = pltpu.MemorySpace.SMEM
HBM = pltpu.MemorySpace.HBM


def whole(space=VMEM):
    return pl.BlockSpec(memory_space=space)


def stay(array):
    return pltpu.with_memory_space_constraint(array, HBM)


def params(mib):
    return pltpu.CompilerParams(vmem_limit_bytes=mib << 20)


def shards(
    series_value,
    series_gate,
    long_filter,
    step_table,
    diffusion_step,
    mask_embed,
    block_flags,
    skip_gain,
    norm_gain,
    w_gate,
    w_up,
    w_down,
):
    tm = lax.axis_size("tm")
    chan = lax.axis_size("chan")
    here = lax.axis_index("chan")
    rows, width = series_value.shape
    own = width // tm
    block = rows // 2
    core = here % 2

    def swap(values, bits):
        return lax.ppermute(values, "chan", [(at, at ^ bits) for at in range(chan)])

    direct = own % 16 == 0
    shape = (tm, 2, own, rows) if direct else (1, 2, width, rows)
    made = pl.pallas_call(
        prepare_kernel,
        out_shape=jax.ShapeDtypeStruct(shape, bf16),
        in_specs=[whole(SMEM)] + [whole(HBM)] * 5,
        out_specs=whole(HBM),
        scratch_shapes=[
            pltpu.SMEM(block_flags.shape, jnp.int32),
            pltpu.VMEM(series_value.shape, bf16),
            pltpu.VMEM(long_filter.shape, bf16),
            pltpu.VMEM(step_table.shape, f32),
            pltpu.VMEM((1, width), f32),
            pltpu.VMEM(shape, bf16),
            pltpu.SemaphoreType.DMA((5,)),
            pltpu.SemaphoreType.DMA((2 * max(1, width // 128),)),
        ],
        compiler_params=params(32),
        name="prepare",
    )(
        diffusion_step,
        *map(stay, (block_flags, series_value, long_filter, step_table)),
        stay(mask_embed.reshape(1, width)),
    )
    if not direct:
        made = made.reshape(2, tm, own, rows).transpose(1, 0, 2, 3)
    both = lax.all_to_all(made, "tm", split_axis=0, concat_axis=0, tiled=True)

    gate_own = lax.dynamic_slice_in_dim(series_gate, core * block, block, 0)
    gate_other = lax.dynamic_slice_in_dim(series_gate, (1 - core) * block, block, 0)
    gates = (gate_own, swap(gate_other, 1), swap(gate_own, 2), swap(gate_other, 3))
    wg1, wu1, wd1 = swap(w_gate, 1), swap(w_up, 1), swap(w_down, 1)

    skip = lax.dynamic_slice_in_dim(skip_gain, lax.axis_index("tm") * own, own, 0)
    skip = skip.reshape(own, 1)
    held = own
    if not direct:
        held = -(-own // 16) * 16
        both = jnp.pad(both, ((0, 0), (0, 0), (0, held - own), (0, 0)))
        skip = jnp.pad(skip, ((0, held - own), (0, 0)))
    both, gates = lax.optimization_barrier((both, gates))
    tables = [stay(jnp.asarray(table)) for table in block_tables(block)]
    conv = pl.pallas_call(
        convolve_kernel,
        out_shape=jax.ShapeDtypeStruct((tm, 2, 2, held, block), bf16),
        in_specs=[whole()] + [whole(HBM)] * 4 + [whole()],
        out_specs=whole(),
        scratch_shapes=[pltpu.VMEM((tm, 2, held, 2 * block), f32)] * 3
        + [pltpu.VMEM(table.shape, bf16) for table in tables]
        + [pltpu.SemaphoreType.DMA((4,))],
        compiler_params=params(48),
        name="convolve",
    )(both, *tables, skip)
    if not direct:
        conv = conv[:, :, :, :own]
    conv = lax.all_to_all(
        conv.reshape(tm * chan, own, block), ("tm", "chan"), split_axis=0, concat_axis=0, tiled=True
    )
    conv = conv.reshape(tm, chan, own, block)
    if not direct:
        conv = conv.transpose(1, 0, 2, 3).reshape(1, chan, width, block)

    gain = norm_gain.reshape(chan, 1, width)
    outs = pl.pallas_call(
        feed_forward_kernel,
        out_shape=[jax.ShapeDtypeStruct((block, width), bf16)] * 4,
        in_specs=[whole(SMEM)] + [whole()] * 5 + [whole(HBM)] * 7,
        out_specs=[whole()] + [whole(HBM)] * 3,
        scratch_shapes=[
            pltpu.VMEM((4, block, width), bf16),
            pltpu.VMEM((block, 4 * width), bf16),
            pltpu.VMEM((3, block, width), bf16),
            pltpu.VMEM(gain.shape, f32),
            pltpu.VMEM(w_gate.shape, bf16),
            pltpu.VMEM(w_up.shape, bf16),
            pltpu.VMEM(w_gate.shape, bf16),
            pltpu.VMEM(w_up.shape, bf16),
            pltpu.VMEM(w_down.shape, bf16),
            pltpu.VMEM(w_down.shape, bf16),
            pltpu.SemaphoreType.DMA((3,)),
            pltpu.SemaphoreType.DMA((7,)),
        ],
        compiler_params=params(48),
        name="feed_forward",
    )(here.reshape(1).astype(jnp.int32), conv, *gates, *map(stay, (gain, w_gate, w_up, wg1, wu1, w_down, wd1)))
    return pl.pallas_call(
        finish_kernel,
        out_shape=jax.ShapeDtypeStruct((rows, width), bf16),
        in_specs=[whole(SMEM)] + [whole()] * 4,
        out_specs=whole(),
        compiler_params=params(8),
        name="finish",
    )(
        core.reshape(1).astype(jnp.int32),
        outs[0],
        swap(outs[2], 2),
        swap(outs[1], 1),
        swap(outs[3], 3),
    )


def solution(mesh):
    placed = (
        P("tm", "chan"),
        P("tm", "chan"),
        P("tm", "chan"),
        P(None, "chan"),
        P(),
        P("chan"),
        P("tm"),
        P("chan"),
        P(),
        P(None, "chan"),
        P(None, "chan"),
        P("chan", None),
    )
    return jax.shard_map(
        shards, mesh=mesh, in_specs=placed, out_specs=P("tm", "chan"), check_vma=False
    )
```

```python
import functools

import jax
import jax.numpy as jnp
import numpy as np
from jax import lax
from jax.experimental import pallas as pl
from jax.experimental.pallas import tpu as pltpu
from jax.sharding import PartitionSpec as P

FLAGBLK = 64
bf16 = jnp.bfloat16
f32 = jnp.float32


def split_table(table):
    high = table.astype(bf16)
    low = (table - high.astype(np.float64)).astype(bf16)
    return high, low


def block_tables(block):
    freq = np.concatenate([np.arange(0, block, 2), np.arange(1, block, 2)])
    time = np.arange(block)
    turn = np.pi * ((2 * freq[None, :] + 1) * time[:, None] % (4 * block)) / (2 * block)
    forward = np.concatenate([np.cos(turn), -np.sin(turn)], axis=1)
    turn = np.pi * ((2 * freq[:, None] + 1) * (block + time[None, :]) % (4 * block)) / (2 * block)
    inverse = np.concatenate([np.cos(turn), -np.sin(turn)], axis=0) / block
    return split_table(forward) + split_table(inverse)


def dot(left, right):
    return jnp.dot(left, right, preferred_element_type=f32)


def start_loads(pairs, sems):
    loads = [
        pltpu.make_async_copy(src, dst, sems.at[at]) for at, (src, dst) in enumerate(pairs)
    ]
    for load in loads:
        load.start()
    return loads


def prepare_kernel(
    step_ref,
    flags_hbm,
    value_hbm,
    filter_hbm,
    table_hbm,
    mask_hbm,
    out_hbm,
    flags_ref,
    value_ref,
    filter_ref,
    table_ref,
    mask_ref,
    out_ref,
    sems,
    out_sems,
):
    loads = start_loads(
        (
            (filter_hbm, filter_ref),
            (value_hbm, value_ref),
            (flags_hbm, flags_ref),
            (table_hbm, table_ref),
            (mask_hbm, mask_ref),
        ),
        sems,
    )
    rows, width = value_ref.shape
    groups = out_ref.shape[0]
    lanes = 128
    stores = []

    def store(which, low, values):
        share = groups * lanes // width
        first = groups * low // width
        part = out_ref.at[pl.ds(first, share), which]
        part[...] = values.T.reshape(part.shape)
        copy = pltpu.make_async_copy(
            part, out_hbm.at[pl.ds(first, share), which], out_sems.at[len(stores)]
        )
        copy.start()
        stores.append(copy)

    steps = width // lanes if groups * lanes % width == 0 else 1
    lanes = width // steps
    loads[0].wait()
    for low in range(0, width, lanes):
        store(1, low, filter_ref[:, low : low + lanes])
    for load in loads[1:]:
        load.wait()
    embed = table_ref[pl.ds(step_ref[0], 1), :]
    mask = mask_ref[...]
    for low in range(0, width, lanes):
        here = slice(low, low + lanes)
        parts = []
        for at in range(rows // FLAGBLK):
            values = value_ref[at * FLAGBLK : (at + 1) * FLAGBLK, here].astype(f32)
            flag = flags_ref[at].astype(f32)
            parts.append((values + embed[:, here] + flag * mask[:, here]).astype(bf16))
        store(0, low, jnp.concatenate(parts, axis=0))
    for copy in stores:
        copy.wait()


def convolve_kernel(
    both_ref,
    fh_hbm,
    fl_hbm,
    gh_hbm,
    gl_hbm,
    skip_ref,
    out_hbm,
    x_ref,
    h_ref,
    z_ref,
    fh_ref,
    fl_ref,
    gh_ref,
    gl_ref,
    out_ref,
    sems,
    out_sems,
):
    loads = start_loads(
        ((fh_hbm, fh_ref), (fl_hbm, fl_ref), (gh_hbm, gh_ref), (gl_hbm, gl_ref)), sems
    )
    tm, _, chans, rows = both_ref.shape
    block = rows // 2
    half = block // 2
    nb = 2 * tm
    loads[0].wait()
    loads[1].wait()
    for which, dst in ((0, x_ref), (1, h_ref)):
        for part in range(2):
            data = both_ref[:, which, :, part * block : (part + 1) * block]
            data = data.reshape(tm * chans, block)
            spec = dot(data, fh_ref[...]) + dot(data, fl_ref[...])
            dst[:, part] = spec.reshape(tm, chans, 2 * block)

    def read(ref, at, sub, lanes):
        return ref[at // 2, at % 2, sub, lanes]

    def window(prev_re, prev_im, cur_re, cur_im, odd):
        if odd:
            return prev_re - cur_im, prev_im + cur_re
        return prev_re + cur_im, prev_im - cur_re

    def tile(step, carry):
        sub = pl.ds(pl.multiple_of(step * 8, 8), 8)
        width = min(128, half)
        for odd in range(2):
            for low in range(odd * half, (odd + 1) * half, width):
                re = slice(low, low + width)
                im = slice(block + low, block + low + width)
                zero = jnp.zeros((8, width), f32)

                def put(a, acc):
                    z_ref[a // 2, a % 2, sub, re] = acc[0] - acc[1]
                    z_ref[a // 2, a % 2, sub, im] = acc[2] - acc[0] - acc[1]

                def load(at):
                    xr, xi = read(x_ref, at, sub, re), read(x_ref, at, sub, im)
                    return xr, xi, xr + xi

                if nb <= 16:
                    taps = []
                    prev = (zero, zero)
                    for d in range(nb):
                        cur = read(h_ref, d, sub, re), read(h_ref, d, sub, im)
                        wr, wi = window(*prev, *cur, odd)
                        taps.append((wr, wi, wr + wi))
                        prev = cur
                    values = [load(at) for at in range(nb)]
                    for a in range(nb):
                        acc = None
                        for d in range(a + 1):
                            terms = [v * t for v, t in zip(values[a - d], taps[d])]
                            acc = terms if acc is None else [p + q for p, q in zip(acc, terms)]
                        put(a, acc)
                else:

                    def out_block(a, carry):
                        def pair(d, acc):
                            before = jnp.maximum(d - 1, 0)
                            keep = (d > 0).astype(f32)
                            wr, wi = window(
                                keep * read(h_ref, before, sub, re),
                                keep * read(h_ref, before, sub, im),
                                read(h_ref, d, sub, re),
                                read(h_ref, d, sub, im),
                                odd,
                            )
                            terms = zip(acc, load(a - d), (wr, wi, wr + wi))
                            return tuple(p + v * t for p, v, t in terms)

                        put(a, lax.fori_loop(0, a + 1, pair, (zero, zero, zero)))
                        return carry

                    lax.fori_loop(0, nb, out_block, 0)
        return carry

    lax.fori_loop(0, chans // 8, tile, 0)
    loads[2].wait()
    loads[3].wait()
    skip = skip_ref[...]
    stores = []
    for part in range(2):
        spec = z_ref[:, part].reshape(tm * chans, 2 * block)
        high = spec.astype(bf16)
        low = (spec - high.astype(f32)).astype(bf16)
        conv = dot(high, gh_ref[...]) + dot(low, gh_ref[...]) + dot(high, gl_ref[...])
        inputs = both_ref[:, 0, :, part * block : (part + 1) * block].astype(f32)
        out_ref[:, part] = (conv.reshape(tm, chans, block) + skip[None] * inputs).astype(bf16)
        store = pltpu.make_async_copy(
            out_ref.at[:, part], out_hbm.at[:, part], out_sems.at[part]
        )
        store.start()
        stores.append(store)
    for store in stores:
        store.wait()


def mix(conv_ref, gate_refs, place_ref, mixed_ref, ready_ref, gain_ref, square):
    chip, core = place_ref
    rows, width = gate_refs[0].shape
    for j, gate_ref in enumerate(gate_refs):
        at = core ^ j
        conv = conv_ref[:, at].reshape(width, rows).T.astype(f32)
        mixed = (gate_ref[...].astype(f32) * conv).astype(bf16)
        if mixed_ref is not None:
            mixed_ref[j] = mixed
        wide = mixed.astype(f32)
        square = square + jnp.sum(wide * wide, axis=-1, keepdims=True)
        lanes = pl.ds(pl.multiple_of(at * width, width), width)
        ready_ref[:, lanes] = (wide * gain_ref[2 * chip + at]).astype(bf16)
    return square


def feed_first_kernel(
    place_ref,
    conv_ref,
    gate0_ref,
    gate1_ref,
    gain_hbm,
    wg0_hbm,
    wu0_hbm,
    wg1_hbm,
    wu1_hbm,
    wd0_hbm,
    wd1_hbm,
    mixed_ref,
    square_ref,
    gain_ref,
    sums_ref,
    rest_ref,
    down_ref,
    ready_ref,
    now_ref,
    sems,
):
    chip, core = place_ref[0], place_ref[1]
    depth = now_ref.shape[1]
    hidden = wd0_hbm.shape[0]
    here = pl.ds(pl.multiple_of(chip * depth, depth), depth)
    there = pl.ds(pl.multiple_of((1 - chip) * depth, depth), depth)
    weights = (wg0_hbm, wu0_hbm, wg1_hbm, wu1_hbm)
    loads = start_loads(
        [(gain_hbm, gain_ref)]
        + [(weight.at[here], now_ref.at[at]) for at, weight in enumerate(weights)]
        + [(weight.at[there], rest_ref.at[at]) for at, weight in enumerate(weights)]
        + [
            (weight, down_ref.at[pl.ds(at * hidden, hidden)])
            for at, weight in enumerate((wd0_hbm, wd1_hbm))
        ],
        sems,
    )
    rows = gate0_ref.shape[0]
    loads[0].wait()
    square_ref[...] = mix(
        conv_ref,
        (gate0_ref, gate1_ref),
        (chip, core),
        mixed_ref,
        ready_ref,
        gain_ref,
        jnp.zeros((rows, 1), f32),
    )
    ready = ready_ref[...]
    for at in range(4):
        loads[1 + at].wait()
        sums_ref[at] = dot(ready, now_ref[at])
    for load in loads[5:]:
        load.wait()


def feed_second_kernel(
    place_ref,
    conv_ref,
    gate2_ref,
    gate3_ref,
    mixed_ref,
    square_ref,
    gain_ref,
    sums_ref,
    rest_ref,
    down_ref,
    out0_ref,
    out1_ref,
    out2_ref,
    out3_ref,
    ready_ref,
):
    chip, core = place_ref[0], place_ref[1]
    rows, width = gate2_ref.shape
    square = mix(
        conv_ref,
        (gate2_ref, gate3_ref),
        (1 - chip, core),
        None,
        ready_ref,
        gain_ref,
        square_ref[...],
    )
    scale = lax.rsqrt(square / (gain_ref.shape[0] * width) + 1e-06)
    ready = ready_ref[...]
    parts = []
    for at in range(2):
        gate = scale * (sums_ref[2 * at] + dot(ready, rest_ref[2 * at]))
        up = scale * (sums_ref[2 * at + 1] + dot(ready, rest_ref[2 * at + 1]))
        parts.append((gate / (1.0 + jnp.exp(-gate)) * up).astype(bf16))
    hidden = jnp.concatenate(parts, axis=1)
    for j, out_ref in ((2, out2_ref), (3, out3_ref), (1, out1_ref), (0, out0_ref)):
        at = (2 * chip + core) ^ j
        part = dot(hidden, down_ref[:, pl.ds(pl.multiple_of(at * width, width), width)])
        if j < 2:
            part = part + mixed_ref[j].astype(f32)
        out_ref[...] = part.astype(bf16)


def finish_kernel(place_ref, own_ref, side_ref, core1_ref, side1_ref, out_ref):
    block = own_ref.shape[0]
    same = pl.ds(pl.multiple_of(place_ref[1] * block, block), block)
    other = pl.ds(pl.multiple_of((1 - place_ref[1]) * block, block), block)
    out_ref[same, :] = (own_ref[...].astype(f32) + side_ref[...].astype(f32)).astype(bf16)
    out_ref[other, :] = (core1_ref[...].astype(f32) + side1_ref[...].astype(f32)).astype(bf16)


VMEM = pltpu.MemorySpace.VMEM
SMEM = pltpu.MemorySpace.SMEM
HBM = pltpu.MemorySpace.HBM


def whole(space=VMEM):
    return pl.BlockSpec(memory_space=space)


def stay(array):
    return pltpu.with_memory_space_constraint(array, HBM)


def params(mib):
    return pltpu.CompilerParams(vmem_limit_bytes=mib << 20)


def shards(
    series_value,
    series_gate,
    long_filter,
    step_table,
    diffusion_step,
    mask_embed,
    block_flags,
    skip_gain,
    norm_gain,
    w_gate,
    w_up,
    w_down,
):
    tm = lax.axis_size("tm")
    chip, core = lax.axis_index("x"), lax.axis_index("core")
    place = jnp.stack([chip, core]).astype(jnp.int32)
    rows, width = series_value.shape
    own = width // tm
    block = rows // 2
    depth = 2 * width

    def swap(values, bits):
        return lax.ppermute(values, ("x", "core"), [(at, at ^ bits) for at in range(4)])

    direct = own % 16 == 0
    shape = (tm, 2, own, rows) if direct else (1, 2, width, rows)
    made = pl.pallas_call(
        prepare_kernel,
        out_shape=jax.ShapeDtypeStruct(shape, bf16),
        in_specs=[whole(SMEM)] + [whole(HBM)] * 5,
        out_specs=whole(HBM),
        scratch_shapes=[
            pltpu.SMEM(block_flags.shape, jnp.int32),
            pltpu.VMEM(series_value.shape, bf16),
            pltpu.VMEM(long_filter.shape, bf16),
            pltpu.VMEM(step_table.shape, f32),
            pltpu.VMEM((1, width), f32),
            pltpu.VMEM(shape, bf16),
            pltpu.SemaphoreType.DMA((5,)),
            pltpu.SemaphoreType.DMA((2 * max(1, width // 128),)),
        ],
        compiler_params=params(32),
        name="prepare",
    )(
        diffusion_step,
        *map(stay, (block_flags, series_value, long_filter, step_table)),
        stay(mask_embed.reshape(1, width)),
    )
    if not direct:
        made = made.reshape(2, tm, own, rows).transpose(1, 0, 2, 3)
    both = lax.all_to_all(made, "tm", split_axis=0, concat_axis=0, tiled=True)

    gate_own = lax.dynamic_slice_in_dim(series_gate, core * block, block, 0)
    gate_other = lax.dynamic_slice_in_dim(series_gate, (1 - core) * block, block, 0)
    gates = (gate_own, swap(gate_other, 1), swap(gate_own, 2), swap(gate_other, 3))
    wg1, wu1, wd1 = swap(w_gate, 1), swap(w_up, 1), swap(w_down, 1)

    skip = lax.dynamic_slice_in_dim(skip_gain, lax.axis_index("tm") * own, own, 0)
    skip = skip.reshape(own, 1)
    held = own
    if not direct:
        held = -(-own // 16) * 16
        both = jnp.pad(both, ((0, 0), (0, 0), (0, held - own), (0, 0)))
        skip = jnp.pad(skip, ((0, held - own), (0, 0)))
    both, gates = lax.optimization_barrier((both, gates))
    tables = [stay(jnp.asarray(table)) for table in block_tables(block)]
    conv = pl.pallas_call(
        convolve_kernel,
        out_shape=jax.ShapeDtypeStruct((tm, 2, held, block), bf16),
        in_specs=[whole()] + [whole(HBM)] * 4 + [whole()],
        out_specs=whole(HBM),
        scratch_shapes=[pltpu.VMEM((tm, 2, held, 2 * block), f32)] * 3
        + [pltpu.VMEM(table.shape, bf16) for table in tables]
        + [pltpu.VMEM((tm, 2, held, block), bf16)]
        + [pltpu.SemaphoreType.DMA((4,)), pltpu.SemaphoreType.DMA((2,))],
        compiler_params=params(24),
        name="convolve",
    )(both, *tables, skip)
    if not direct:
        conv = conv[:, :, :own]

    conv = lax.all_to_all(
        conv.reshape(tm * 2, own, block), ("tm", "core"), split_axis=0, concat_axis=0, tiled=True
    )
    other = swap(conv, 2)

    def view(values):
        values = values.reshape(tm, 2, own, block)
        if not direct:
            values = values.transpose(1, 0, 2, 3).reshape(1, 2, width, block)
        return values

    gain = norm_gain.reshape(4, 1, width)
    held = [
        ((2, block, width), bf16),
        ((block, 1), f32),
        ((4, 1, width), f32),
        ((4, block, w_gate.shape[1]), f32),
        ((4, depth, w_gate.shape[1]), bf16),
        ((2 * w_down.shape[0], w_down.shape[1]), bf16),
    ]
    kept = pl.pallas_call(
        feed_first_kernel,
        out_shape=[jax.ShapeDtypeStruct(*spec) for spec in held],
        in_specs=[whole(SMEM)] + [whole()] * 3 + [whole(HBM)] * 7,
        out_specs=[whole()] * 6,
        scratch_shapes=[
            pltpu.VMEM((block, depth), bf16),
            pltpu.VMEM((4, depth, w_gate.shape[1]), bf16),
            pltpu.SemaphoreType.DMA((11,)),
        ],
        compiler_params=params(24),
        name="feed_first",
    )(place, view(conv), *gates[:2], *map(stay, (gain, w_gate, w_up, wg1, wu1, w_down, wd1)))
    outs = pl.pallas_call(
        feed_second_kernel,
        out_shape=[jax.ShapeDtypeStruct((block, width), bf16)] * 4,
        in_specs=[whole(SMEM)] + [whole()] * 9,
        out_specs=[whole()] * 4,
        scratch_shapes=[pltpu.VMEM((block, depth), bf16)],
        compiler_params=params(24),
        name="feed_second",
    )(place, view(other), *gates[2:], *kept)
    return pl.pallas_call(
        finish_kernel,
        out_shape=jax.ShapeDtypeStruct((rows, width), bf16),
        in_specs=[whole(SMEM)] + [whole()] * 4,
        out_specs=whole(),
        compiler_params=params(8),
        name="finish",
    )(place, outs[0], swap(outs[2], 2), swap(outs[1], 1), swap(outs[3], 3))


def solution(mesh):
    axes = mesh.devices.reshape(mesh.shape["tm"], mesh.shape["chan"] // 2, 2)
    mesh = jax.sharding.Mesh(axes, ("tm", "x", "core"))
    chan = ("x", "core")
    placed = (
        P("tm", chan),
        P("tm", chan),
        P("tm", chan),
        P(None, chan),
        P(),
        P(chan),
        P("tm"),
        P(chan),
        P(),
        P(None, chan),
        P(None, chan),
        P(chan, None),
    )
    return jax.shard_map(
        shards, mesh=mesh, in_specs=placed, out_specs=P("tm", chan), check_vma=False
    )
```

```python
import functools

import jax
import jax.numpy as jnp
import numpy as np
from jax import lax
from jax.experimental import pallas as pl
from jax.experimental.pallas import tpu as pltpu
from jax.sharding import PartitionSpec as P

FLAGBLK = 64
bf16 = jnp.bfloat16
f32 = jnp.float32


def split_table(table):
    high = table.astype(bf16)
    low = (table - high.astype(np.float64)).astype(bf16)
    return high, low


def block_tables(block):
    freq = np.concatenate([np.arange(0, block, 2), np.arange(1, block, 2)])
    time = np.arange(block)
    turn = np.pi * ((2 * freq[None, :] + 1) * time[:, None] % (4 * block)) / (2 * block)
    forward = np.concatenate([np.cos(turn), -np.sin(turn)], axis=1)
    turn = np.pi * ((2 * freq[:, None] + 1) * (block + time[None, :]) % (4 * block)) / (2 * block)
    inverse = np.concatenate([np.cos(turn), -np.sin(turn)], axis=0) / block
    return split_table(forward) + split_table(inverse)


def dot(left, right):
    return jnp.dot(left, right, preferred_element_type=f32)


def start_loads(pairs, sems):
    loads = [
        pltpu.make_async_copy(src, dst, sems.at[at]) for at, (src, dst) in enumerate(pairs)
    ]
    for load in loads:
        load.start()
    return loads


def prepare_kernel(
    step_ref,
    flags_hbm,
    value_hbm,
    filter_hbm,
    table_hbm,
    mask_hbm,
    out_hbm,
    flags_ref,
    value_ref,
    filter_ref,
    table_ref,
    mask_ref,
    out_ref,
    sems,
    out_sems,
):
    loads = start_loads(
        (
            (filter_hbm, filter_ref),
            (value_hbm, value_ref),
            (flags_hbm, flags_ref),
            (table_hbm, table_ref),
            (mask_hbm, mask_ref),
        ),
        sems,
    )
    rows, width = value_ref.shape
    groups = out_ref.shape[0]
    lanes = 128
    stores = []

    def store(which, low, values):
        share = groups * lanes // width
        first = groups * low // width
        part = out_ref.at[pl.ds(first, share), which]
        part[...] = values.T.reshape(part.shape)
        copy = pltpu.make_async_copy(
            part, out_hbm.at[pl.ds(first, share), which], out_sems.at[len(stores)]
        )
        copy.start()
        stores.append(copy)

    steps = width // lanes if groups * lanes % width == 0 else 1
    lanes = width // steps
    loads[0].wait()
    for low in range(0, width, lanes):
        store(1, low, filter_ref[:, low : low + lanes])
    for load in loads[1:]:
        load.wait()
    embed = table_ref[pl.ds(step_ref[0], 1), :]
    mask = mask_ref[...]
    for low in range(0, width, lanes):
        here = slice(low, low + lanes)
        parts = []
        for at in range(rows // FLAGBLK):
            values = value_ref[at * FLAGBLK : (at + 1) * FLAGBLK, here].astype(f32)
            flag = flags_ref[at].astype(f32)
            parts.append((values + embed[:, here] + flag * mask[:, here]).astype(bf16))
        store(0, low, jnp.concatenate(parts, axis=0))
    for copy in stores:
        copy.wait()


def convolve_kernel(
    both_ref,
    fh_hbm,
    fl_hbm,
    gh_hbm,
    gl_hbm,
    skip_ref,
    out_hbm,
    x_ref,
    h_ref,
    z_ref,
    fh_ref,
    fl_ref,
    gh_ref,
    gl_ref,
    out_ref,
    sems,
    out_sems,
):
    loads = start_loads(
        ((fh_hbm, fh_ref), (fl_hbm, fl_ref), (gh_hbm, gh_ref), (gl_hbm, gl_ref)), sems
    )
    tm, _, chans, rows = both_ref.shape
    block = rows // 2
    half = block // 2
    nb = 2 * tm
    loads[0].wait()
    loads[1].wait()
    for which, dst in ((0, x_ref), (1, h_ref)):
        for part in range(2):
            data = both_ref[:, which, :, part * block : (part + 1) * block]
            data = data.reshape(tm * chans, block)
            spec = dot(data, fh_ref[...]) + dot(data, fl_ref[...])
            dst[:, part] = spec.reshape(tm, chans, 2 * block)

    def read(ref, at, sub, lanes):
        return ref[at // 2, at % 2, sub, lanes]

    def window(prev_re, prev_im, cur_re, cur_im, odd):
        if odd:
            return prev_re - cur_im, prev_im + cur_re
        return prev_re + cur_im, prev_im - cur_re

    def tile(step, carry):
        sub = pl.ds(pl.multiple_of(step * 8, 8), 8)
        width = min(128, half)
        for odd in range(2):
            for low in range(odd * half, (odd + 1) * half, width):
                re = slice(low, low + width)
                im = slice(block + low, block + low + width)
                zero = jnp.zeros((8, width), f32)

                def put(a, acc):
                    z_ref[a // 2, a % 2, sub, re] = acc[0] - acc[1]
                    z_ref[a // 2, a % 2, sub, im] = acc[2] - acc[0] - acc[1]

                def load(at):
                    xr, xi = read(x_ref, at, sub, re), read(x_ref, at, sub, im)
                    return xr, xi, xr + xi

                if nb <= 16:
                    taps = []
                    prev = (zero, zero)
                    for d in range(nb):
                        cur = read(h_ref, d, sub, re), read(h_ref, d, sub, im)
                        wr, wi = window(*prev, *cur, odd)
                        taps.append((wr, wi, wr + wi))
                        prev = cur
                    values = [load(at) for at in range(nb)]
                    for a in range(nb):
                        acc = None
                        for d in range(a + 1):
                            terms = [v * t for v, t in zip(values[a - d], taps[d])]
                            acc = terms if acc is None else [p + q for p, q in zip(acc, terms)]
                        put(a, acc)
                else:

                    def out_block(a, carry):
                        def pair(d, acc):
                            before = jnp.maximum(d - 1, 0)
                            keep = (d > 0).astype(f32)
                            wr, wi = window(
                                keep * read(h_ref, before, sub, re),
                                keep * read(h_ref, before, sub, im),
                                read(h_ref, d, sub, re),
                                read(h_ref, d, sub, im),
                                odd,
                            )
                            terms = zip(acc, load(a - d), (wr, wi, wr + wi))
                            return tuple(p + v * t for p, v, t in terms)

                        put(a, lax.fori_loop(0, a + 1, pair, (zero, zero, zero)))
                        return carry

                    lax.fori_loop(0, nb, out_block, 0)
        return carry

    lax.fori_loop(0, chans // 8, tile, 0)
    loads[2].wait()
    loads[3].wait()
    skip = skip_ref[...]
    stores = []
    for part in range(2):
        spec = z_ref[:, part].reshape(tm * chans, 2 * block)
        high = spec.astype(bf16)
        low = (spec - high.astype(f32)).astype(bf16)
        conv = dot(high, gh_ref[...]) + dot(low, gh_ref[...]) + dot(high, gl_ref[...])
        inputs = both_ref[:, 0, :, part * block : (part + 1) * block].astype(f32)
        out_ref[:, part] = (conv.reshape(tm, chans, block) + skip[None] * inputs).astype(bf16)
        store = pltpu.make_async_copy(
            out_ref.at[:, part], out_hbm.at[:, part], out_sems.at[part]
        )
        store.start()
        stores.append(store)
    for store in stores:
        store.wait()


def mix(conv_refs, gate_refs, chip, core, mixed_ref, ready_ref, gain_ref, square):
    rows, width = gate_refs[0].shape
    for j, (conv_ref, gate_ref) in enumerate(zip(conv_refs, gate_refs)):
        at = core ^ j
        conv = conv_ref[:, core].reshape(width, rows).T.astype(f32)
        mixed = (gate_ref[...].astype(f32) * conv).astype(bf16)
        if mixed_ref is not None:
            mixed_ref[j] = mixed
        wide = mixed.astype(f32)
        square = square + jnp.sum(wide * wide, axis=-1, keepdims=True)
        lanes = pl.ds(pl.multiple_of(at * width, width), width)
        ready_ref[:, lanes] = (wide * gain_ref[2 * chip + at]).astype(bf16)
    return square


def feed_first_kernel(
    chip_ref,
    core_ref,
    conv0_ref,
    conv1_ref,
    gate0_ref,
    gate1_ref,
    gain_hbm,
    wg0_hbm,
    wu0_hbm,
    wg1_hbm,
    wu1_hbm,
    wd0_hbm,
    wd1_hbm,
    mixed_ref,
    square_ref,
    gain_ref,
    sums_ref,
    rest_ref,
    down_ref,
    ready_ref,
    now_ref,
    sems,
):
    chip, core = chip_ref[0], core_ref[0]
    depth = now_ref.shape[1]
    hidden = wd0_hbm.shape[0]
    here = pl.ds(pl.multiple_of(chip * depth, depth), depth)
    there = pl.ds(pl.multiple_of((1 - chip) * depth, depth), depth)
    weights = (wg0_hbm, wu0_hbm, wg1_hbm, wu1_hbm)
    loads = start_loads(
        [(gain_hbm, gain_ref)]
        + [(weight.at[here], now_ref.at[at]) for at, weight in enumerate(weights)]
        + [(weight.at[there], rest_ref.at[at]) for at, weight in enumerate(weights)]
        + [
            (weight, down_ref.at[pl.ds(at * hidden, hidden)])
            for at, weight in enumerate((wd0_hbm, wd1_hbm))
        ],
        sems,
    )
    rows = gate0_ref.shape[0]
    loads[0].wait()
    square_ref[...] = mix(
        (conv0_ref, conv1_ref),
        (gate0_ref, gate1_ref),
        chip,
        core,
        mixed_ref,
        ready_ref,
        gain_ref,
        jnp.zeros((rows, 1), f32),
    )
    ready = ready_ref[...]
    for at in range(4):
        loads[1 + at].wait()
        sums_ref[at] = dot(ready, now_ref[at])
    for load in loads[5:]:
        load.wait()


def feed_second_kernel(
    chip_ref,
    core_ref,
    conv2_ref,
    conv3_ref,
    gate2_ref,
    gate3_ref,
    mixed_ref,
    square_ref,
    gain_ref,
    sums_ref,
    rest_ref,
    down_ref,
    out0_ref,
    out1_ref,
    out2_ref,
    out3_ref,
    ready_ref,
):
    chip, core = chip_ref[0], core_ref[0]
    rows, width = gate2_ref.shape
    square = mix(
        (conv2_ref, conv3_ref),
        (gate2_ref, gate3_ref),
        1 - chip,
        core,
        None,
        ready_ref,
        gain_ref,
        square_ref[...],
    )
    scale = lax.rsqrt(square / (gain_ref.shape[0] * width) + 1e-06)
    ready = ready_ref[...]
    parts = []
    for at in range(2):
        gate = scale * (sums_ref[2 * at] + dot(ready, rest_ref[2 * at]))
        up = scale * (sums_ref[2 * at + 1] + dot(ready, rest_ref[2 * at + 1]))
        parts.append((gate / (1.0 + jnp.exp(-gate)) * up).astype(bf16))
    hidden = jnp.concatenate(parts, axis=1)
    for j, out_ref in ((2, out2_ref), (3, out3_ref), (1, out1_ref), (0, out0_ref)):
        at = (2 * chip + core) ^ j
        part = dot(hidden, down_ref[:, pl.ds(pl.multiple_of(at * width, width), width)])
        if j < 2:
            part = part + mixed_ref[j].astype(f32)
        out_ref[...] = part.astype(bf16)


def finish_kernel(core_ref, own_ref, side_ref, core1_ref, side1_ref, out_ref):
    block = own_ref.shape[0]
    same = pl.ds(pl.multiple_of(core_ref[0] * block, block), block)
    other = pl.ds(pl.multiple_of((1 - core_ref[0]) * block, block), block)
    out_ref[same, :] = (own_ref[...].astype(f32) + side_ref[...].astype(f32)).astype(bf16)
    out_ref[other, :] = (core1_ref[...].astype(f32) + side1_ref[...].astype(f32)).astype(bf16)


VMEM = pltpu.MemorySpace.VMEM
SMEM = pltpu.MemorySpace.SMEM
HBM = pltpu.MemorySpace.HBM


def whole(space=VMEM):
    return pl.BlockSpec(memory_space=space)


def stay(array):
    return pltpu.with_memory_space_constraint(array, HBM)


def params(mib):
    return pltpu.CompilerParams(vmem_limit_bytes=mib << 20)


def shards(
    series_value,
    series_gate,
    long_filter,
    step_table,
    diffusion_step,
    mask_embed,
    block_flags,
    skip_gain,
    norm_gain,
    w_gate,
    w_up,
    w_down,
):
    tm = lax.axis_size("tm")
    chip, core = lax.axis_index("x"), lax.axis_index("core")
    place = chip.reshape(1).astype(jnp.int32), core.reshape(1).astype(jnp.int32)
    rows, width = series_value.shape
    own = width // tm
    block = rows // 2
    depth = 2 * width

    def swap(values, bits):
        return lax.ppermute(values, ("x", "core"), [(at, at ^ bits) for at in range(4)])

    direct = own % 16 == 0
    shape = (tm, 2, own, rows) if direct else (1, 2, width, rows)
    made = pl.pallas_call(
        prepare_kernel,
        out_shape=jax.ShapeDtypeStruct(shape, bf16),
        in_specs=[whole(SMEM)] + [whole(HBM)] * 5,
        out_specs=whole(HBM),
        scratch_shapes=[
            pltpu.SMEM(block_flags.shape, jnp.int32),
            pltpu.VMEM(series_value.shape, bf16),
            pltpu.VMEM(long_filter.shape, bf16),
            pltpu.VMEM(step_table.shape, f32),
            pltpu.VMEM((1, width), f32),
            pltpu.VMEM(shape, bf16),
            pltpu.SemaphoreType.DMA((5,)),
            pltpu.SemaphoreType.DMA((2 * max(1, width // 128),)),
        ],
        compiler_params=params(32),
        name="prepare",
    )(
        diffusion_step,
        *map(stay, (block_flags, series_value, long_filter, step_table)),
        stay(mask_embed.reshape(1, width)),
    )
    if not direct:
        made = made.reshape(2, tm, own, rows).transpose(1, 0, 2, 3)
    both = lax.all_to_all(made, "tm", split_axis=0, concat_axis=0, tiled=True)

    gate_own = lax.dynamic_slice_in_dim(series_gate, core * block, block, 0)
    gate_other = lax.dynamic_slice_in_dim(series_gate, (1 - core) * block, block, 0)
    gates = (gate_own, swap(gate_other, 1), swap(gate_own, 2), swap(gate_other, 3))
    wg1, wu1, wd1 = swap(w_gate, 1), swap(w_up, 1), swap(w_down, 1)

    skip = lax.dynamic_slice_in_dim(skip_gain, lax.axis_index("tm") * own, own, 0)
    skip = skip.reshape(own, 1)
    held = own
    if not direct:
        held = -(-own // 16) * 16
        both = jnp.pad(both, ((0, 0), (0, 0), (0, held - own), (0, 0)))
        skip = jnp.pad(skip, ((0, held - own), (0, 0)))
    both, gates = lax.optimization_barrier((both, gates))
    tables = [stay(jnp.asarray(table)) for table in block_tables(block)]
    conv = pl.pallas_call(
        convolve_kernel,
        out_shape=jax.ShapeDtypeStruct((tm, 2, held, block), bf16),
        in_specs=[whole()] + [whole(HBM)] * 4 + [whole()],
        out_specs=whole(HBM),
        scratch_shapes=[pltpu.VMEM((tm, 2, held, 2 * block), f32)] * 3
        + [pltpu.VMEM(table.shape, bf16) for table in tables]
        + [pltpu.VMEM((tm, 2, held, block), bf16)]
        + [pltpu.SemaphoreType.DMA((4,)), pltpu.SemaphoreType.DMA((2,))],
        compiler_params=params(24),
        name="convolve",
    )(both, *tables, skip)
    if not direct:
        conv = conv[:, :, :own]

    conv = lax.all_to_all(conv, "tm", split_axis=0, concat_axis=0, tiled=True)
    aside = swap(conv, 2)
    beside = swap(conv, 1)

    def view(values):
        if not direct:
            values = values.transpose(1, 0, 2, 3).reshape(1, 2, width, block)
        return values

    gain = norm_gain.reshape(4, 1, width)
    held = [
        ((2, block, width), bf16),
        ((block, 1), f32),
        ((4, 1, width), f32),
        ((4, block, w_gate.shape[1]), f32),
        ((4, depth, w_gate.shape[1]), bf16),
        ((2 * w_down.shape[0], w_down.shape[1]), bf16),
    ]
    kept = pl.pallas_call(
        feed_first_kernel,
        out_shape=[jax.ShapeDtypeStruct(*spec) for spec in held],
        in_specs=[whole(SMEM)] * 2 + [whole()] * 4 + [whole(HBM)] * 7,
        out_specs=[whole()] * 6,
        scratch_shapes=[
            pltpu.VMEM((block, depth), bf16),
            pltpu.VMEM((4, depth, w_gate.shape[1]), bf16),
            pltpu.SemaphoreType.DMA((11,)),
        ],
        compiler_params=params(24),
        name="feed_first",
    )(
        *place,
        view(conv),
        view(beside),
        *gates[:2],
        *map(stay, (gain, w_gate, w_up, wg1, wu1, w_down, wd1)),
    )
    aside, kept = lax.optimization_barrier((aside, kept))
    outs = pl.pallas_call(
        feed_second_kernel,
        out_shape=[jax.ShapeDtypeStruct((block, width), bf16)] * 4,
        in_specs=[whole(SMEM)] * 2 + [whole()] * 10,
        out_specs=[whole()] * 4,
        scratch_shapes=[pltpu.VMEM((block, depth), bf16)],
        compiler_params=params(24),
        name="feed_second",
    )(*place, view(aside), view(swap(aside, 1)), *gates[2:], *kept)
    return pl.pallas_call(
        finish_kernel,
        out_shape=jax.ShapeDtypeStruct((rows, width), bf16),
        in_specs=[whole(SMEM)] + [whole()] * 4,
        out_specs=whole(),
        compiler_params=params(8),
        name="finish",
    )(place[1], outs[0], swap(outs[2], 2), swap(outs[1], 1), swap(outs[3], 3))


def solution(mesh):
    axes = mesh.devices.reshape(mesh.shape["tm"], mesh.shape["chan"] // 2, 2)
    mesh = jax.sharding.Mesh(axes, ("tm", "x", "core"))
    chan = ("x", "core")
    placed = (
        P("tm", chan),
        P("tm", chan),
        P("tm", chan),
        P(None, chan),
        P(),
        P(chan),
        P("tm"),
        P(chan),
        P(),
        P(None, chan),
        P(None, chan),
        P(chan, None),
    )
    return jax.shard_map(
        shards, mesh=mesh, in_specs=placed, out_specs=P("tm", chan), check_vma=False
    )
```

```python
import functools

import jax
import jax.numpy as jnp
import numpy as np
from jax import lax
from jax.experimental import pallas as pl
from jax.experimental.pallas import tpu as pltpu
from jax.sharding import PartitionSpec as P

FLAGBLK = 64
bf16 = jnp.bfloat16
f32 = jnp.float32


def split_table(table):
    high = table.astype(bf16)
    low = (table - high.astype(np.float64)).astype(bf16)
    return high, low


def block_tables(block):
    freq = np.concatenate([np.arange(0, block, 2), np.arange(1, block, 2)])
    time = np.arange(block)
    turn = np.pi * ((2 * freq[None, :] + 1) * time[:, None] % (4 * block)) / (2 * block)
    forward = np.concatenate([np.cos(turn), -np.sin(turn)], axis=1)
    turn = np.pi * ((2 * freq[:, None] + 1) * (block + time[None, :]) % (4 * block)) / (2 * block)
    inverse = np.concatenate([np.cos(turn), -np.sin(turn)], axis=0) / block
    return split_table(forward) + split_table(inverse)


def dot(left, right):
    return jnp.dot(left, right, preferred_element_type=f32)


def start_loads(pairs, sems):
    loads = [
        pltpu.make_async_copy(src, dst, sems.at[at]) for at, (src, dst) in enumerate(pairs)
    ]
    for load in loads:
        load.start()
    return loads


def prepare_kernel(
    step_ref,
    flags_hbm,
    value_hbm,
    filter_hbm,
    table_hbm,
    mask_hbm,
    out_hbm,
    flags_ref,
    value_ref,
    filter_ref,
    table_ref,
    mask_ref,
    out_ref,
    sems,
    out_sems,
):
    loads = start_loads(
        (
            (filter_hbm, filter_ref),
            (value_hbm, value_ref),
            (flags_hbm, flags_ref),
            (table_hbm, table_ref),
            (mask_hbm, mask_ref),
        ),
        sems,
    )
    rows, width = value_ref.shape
    groups = out_ref.shape[0]
    lanes = 128
    stores = []

    def store(which, low, values):
        share = groups * lanes // width
        first = groups * low // width
        part = out_ref.at[pl.ds(first, share), which]
        part[...] = values.T.reshape(part.shape)
        copy = pltpu.make_async_copy(
            part, out_hbm.at[pl.ds(first, share), which], out_sems.at[len(stores)]
        )
        copy.start()
        stores.append(copy)

    steps = width // lanes if groups * lanes % width == 0 else 1
    lanes = width // steps
    loads[0].wait()
    for low in range(0, width, lanes):
        store(1, low, filter_ref[:, low : low + lanes])
    for load in loads[1:]:
        load.wait()
    embed = table_ref[pl.ds(step_ref[0], 1), :]
    mask = mask_ref[...]
    for low in range(0, width, lanes):
        here = slice(low, low + lanes)
        parts = []
        for at in range(rows // FLAGBLK):
            values = value_ref[at * FLAGBLK : (at + 1) * FLAGBLK, here].astype(f32)
            flag = flags_ref[at].astype(f32)
            parts.append((values + embed[:, here] + flag * mask[:, here]).astype(bf16))
        store(0, low, jnp.concatenate(parts, axis=0))
    for copy in stores:
        copy.wait()


def convolve_kernel(
    core_ref,
    both_ref,
    fh_ref,
    fl_ref,
    gh_hbm,
    gl_hbm,
    skip_ref,
    out_hbm,
    x_ref,
    h_ref,
    z_ref,
    gh_ref,
    gl_ref,
    out_ref,
    sems,
    out_sems,
):
    loads = start_loads(((gh_hbm, gh_ref), (gl_hbm, gl_ref)), sems)
    tm, _, chans, rows = both_ref.shape
    block = rows // 2
    half = block // 2
    nb = 2 * tm
    for which, dst in ((0, x_ref), (1, h_ref)):
        for part in range(2):
            data = both_ref[:, which, :, part * block : (part + 1) * block]
            data = data.reshape(tm * chans, block)
            spec = dot(data, fh_ref[...]) + dot(data, fl_ref[...])
            dst[:, part] = spec.reshape(tm, chans, 2 * block)

    def read(ref, at, sub, lanes):
        return ref[at // 2, at % 2, sub, lanes]

    def window(prev_re, prev_im, cur_re, cur_im, odd):
        if odd:
            return prev_re - cur_im, prev_im + cur_re
        return prev_re + cur_im, prev_im - cur_re

    def tile(step, carry):
        sub = pl.ds(pl.multiple_of(step * 8, 8), 8)
        width = min(128, half)
        for odd in range(2):
            for low in range(odd * half, (odd + 1) * half, width):
                re = slice(low, low + width)
                im = slice(block + low, block + low + width)
                zero = jnp.zeros((8, width), f32)

                def put(a, acc):
                    z_ref[a // 2, a % 2, sub, re] = acc[0] - acc[1]
                    z_ref[a // 2, a % 2, sub, im] = acc[2] - acc[0] - acc[1]

                def load(at):
                    xr, xi = read(x_ref, at, sub, re), read(x_ref, at, sub, im)
                    return xr, xi, xr + xi

                if nb <= 16:
                    taps = []
                    prev = (zero, zero)
                    for d in range(nb):
                        cur = read(h_ref, d, sub, re), read(h_ref, d, sub, im)
                        wr, wi = window(*prev, *cur, odd)
                        taps.append((wr, wi, wr + wi))
                        prev = cur
                    values = [load(at) for at in range(nb)]
                    for a in range(nb):
                        acc = None
                        for d in range(a + 1):
                            terms = [v * t for v, t in zip(values[a - d], taps[d])]
                            acc = terms if acc is None else [p + q for p, q in zip(acc, terms)]
                        put(a, acc)
                else:

                    def out_block(a, carry):
                        def pair(d, acc):
                            before = jnp.maximum(d - 1, 0)
                            keep = (d > 0).astype(f32)
                            wr, wi = window(
                                keep * read(h_ref, before, sub, re),
                                keep * read(h_ref, before, sub, im),
                                read(h_ref, d, sub, re),
                                read(h_ref, d, sub, im),
                                odd,
                            )
                            terms = zip(acc, load(a - d), (wr, wi, wr + wi))
                            return tuple(p + v * t for p, v, t in terms)

                        put(a, lax.fori_loop(0, a + 1, pair, (zero, zero, zero)))
                        return carry

                    lax.fori_loop(0, nb, out_block, 0)
        return carry

    lax.fori_loop(0, chans // 8, tile, 0)
    for load in loads:
        load.wait()
    skip = skip_ref[...]
    stores = []
    for part in range(2):
        spec = z_ref[:, part].reshape(tm * chans, 2 * block)
        high = spec.astype(bf16)
        low = (spec - high.astype(f32)).astype(bf16)
        conv = dot(high, gh_ref[...]) + dot(low, gh_ref[...]) + dot(high, gl_ref[...])
        inputs = both_ref[:, 0, :, part * block : (part + 1) * block].astype(f32)
        out_ref[:, part] = (conv.reshape(tm, chans, block) + skip[None] * inputs).astype(bf16)
        store = pltpu.make_async_copy(
            out_ref.at[:, part], out_hbm.at[:, part ^ core_ref[0]], out_sems.at[part]
        )
        store.start()
        stores.append(store)
    for store in stores:
        store.wait()


def mix(conv_refs, gate_refs, chip, core, mixed_ref, ready_ref, gain_ref, square):
    rows, width = gate_refs[0].shape
    for j, (conv_ref, gate_ref) in enumerate(zip(conv_refs, gate_refs)):
        at = core ^ j
        conv = conv_ref[...].reshape(width, rows).T.astype(f32)
        mixed = (gate_ref[...].astype(f32) * conv).astype(bf16)
        if mixed_ref is not None:
            mixed_ref[j] = mixed
        wide = mixed.astype(f32)
        square = square + jnp.sum(wide * wide, axis=-1, keepdims=True)
        lanes = pl.ds(pl.multiple_of(at * width, width), width)
        ready_ref[:, lanes] = (wide * gain_ref[2 * chip + at]).astype(bf16)
    return square


def feed_first_kernel(
    chip_ref,
    core_ref,
    conv0_ref,
    conv1_ref,
    gate0_ref,
    gate1_ref,
    gain_hbm,
    wg0_hbm,
    wu0_hbm,
    wg1_hbm,
    wu1_hbm,
    wd0_hbm,
    wd1_hbm,
    mixed_ref,
    square_ref,
    gain_ref,
    sums_ref,
    rest_ref,
    down_ref,
    ready_ref,
    now_ref,
    sems,
):
    chip, core = chip_ref[0], core_ref[0]
    depth = now_ref.shape[1]
    hidden = wd0_hbm.shape[0]
    here = pl.ds(pl.multiple_of(chip * depth, depth), depth)
    there = pl.ds(pl.multiple_of((1 - chip) * depth, depth), depth)
    weights = (wg0_hbm, wu0_hbm, wg1_hbm, wu1_hbm)
    loads = start_loads(
        [(gain_hbm, gain_ref)]
        + [(weight.at[here], now_ref.at[at]) for at, weight in enumerate(weights)]
        + [(weight.at[there], rest_ref.at[at]) for at, weight in enumerate(weights)]
        + [
            (weight, down_ref.at[pl.ds(at * hidden, hidden)])
            for at, weight in enumerate((wd0_hbm, wd1_hbm))
        ],
        sems,
    )
    rows = gate0_ref.shape[0]
    loads[0].wait()
    square_ref[...] = mix(
        (conv0_ref, conv1_ref),
        (gate0_ref, gate1_ref),
        chip,
        core,
        mixed_ref,
        ready_ref,
        gain_ref,
        jnp.zeros((rows, 1), f32),
    )
    ready = ready_ref[...]
    for at in range(4):
        loads[1 + at].wait()
        sums_ref[at] = dot(ready, now_ref[at])
    for load in loads[5:]:
        load.wait()


def feed_second_kernel(
    chip_ref,
    core_ref,
    conv2_ref,
    conv3_ref,
    gate2_ref,
    gate3_ref,
    mixed_ref,
    square_ref,
    gain_ref,
    sums_ref,
    rest_ref,
    down_ref,
    out0_ref,
    out1_ref,
    out2_ref,
    out3_ref,
    ready_ref,
):
    chip, core = chip_ref[0], core_ref[0]
    rows, width = gate2_ref.shape
    square = mix(
        (conv2_ref, conv3_ref),
        (gate2_ref, gate3_ref),
        1 - chip,
        core,
        None,
        ready_ref,
        gain_ref,
        square_ref[...],
    )
    scale = lax.rsqrt(square / (gain_ref.shape[0] * width) + 1e-06)
    ready = ready_ref[...]
    parts = []
    for at in range(2):
        gate = scale * (sums_ref[2 * at] + dot(ready, rest_ref[2 * at]))
        up = scale * (sums_ref[2 * at + 1] + dot(ready, rest_ref[2 * at + 1]))
        parts.append((gate / (1.0 + jnp.exp(-gate)) * up).astype(bf16))
    hidden = jnp.concatenate(parts, axis=1)
    for j, out_ref in ((2, out2_ref), (3, out3_ref), (1, out1_ref), (0, out0_ref)):
        at = (2 * chip + core) ^ j
        part = dot(hidden, down_ref[:, pl.ds(pl.multiple_of(at * width, width), width)])
        if j < 2:
            part = part + mixed_ref[j].astype(f32)
        out_ref[...] = part.astype(bf16)


def finish_kernel(core_ref, own_ref, side_ref, core1_ref, side1_ref, out_ref):
    block = own_ref.shape[0]
    same = pl.ds(pl.multiple_of(core_ref[0] * block, block), block)
    other = pl.ds(pl.multiple_of((1 - core_ref[0]) * block, block), block)
    out_ref[same, :] = (own_ref[...].astype(f32) + side_ref[...].astype(f32)).astype(bf16)
    out_ref[other, :] = (core1_ref[...].astype(f32) + side1_ref[...].astype(f32)).astype(bf16)


VMEM = pltpu.MemorySpace.VMEM
SMEM = pltpu.MemorySpace.SMEM
HBM = pltpu.MemorySpace.HBM


def whole(space=VMEM):
    return pl.BlockSpec(memory_space=space)


def stay(array):
    return pltpu.with_memory_space_constraint(array, HBM)


def params(mib):
    return pltpu.CompilerParams(vmem_limit_bytes=mib << 20)


def shards(
    series_value,
    series_gate,
    long_filter,
    step_table,
    diffusion_step,
    mask_embed,
    block_flags,
    skip_gain,
    norm_gain,
    w_gate,
    w_up,
    w_down,
):
    tm = lax.axis_size("tm")
    chip, core = lax.axis_index("x"), lax.axis_index("core")
    place = chip.reshape(1).astype(jnp.int32), core.reshape(1).astype(jnp.int32)
    rows, width = series_value.shape
    own = width // tm
    block = rows // 2
    depth = 2 * width

    def swap(values, bits):
        return lax.ppermute(values, ("x", "core"), [(at, at ^ bits) for at in range(4)])

    direct = own % 16 == 0
    shape = (tm, 2, own, rows) if direct else (1, 2, width, rows)
    made = pl.pallas_call(
        prepare_kernel,
        out_shape=jax.ShapeDtypeStruct(shape, bf16),
        in_specs=[whole(SMEM)] + [whole(HBM)] * 5,
        out_specs=whole(HBM),
        scratch_shapes=[
            pltpu.SMEM(block_flags.shape, jnp.int32),
            pltpu.VMEM(series_value.shape, bf16),
            pltpu.VMEM(long_filter.shape, bf16),
            pltpu.VMEM(step_table.shape, f32),
            pltpu.VMEM((1, width), f32),
            pltpu.VMEM(shape, bf16),
            pltpu.SemaphoreType.DMA((5,)),
            pltpu.SemaphoreType.DMA((2 * max(1, width // 128),)),
        ],
        compiler_params=params(32),
        name="prepare",
    )(
        diffusion_step,
        *map(stay, (block_flags, series_value, long_filter, step_table)),
        stay(mask_embed.reshape(1, width)),
    )
    if not direct:
        made = made.reshape(2, tm, own, rows).transpose(1, 0, 2, 3)
    both = lax.all_to_all(made, "tm", split_axis=0, concat_axis=0, tiled=True)

    gate_own = lax.dynamic_slice_in_dim(series_gate, core * block, block, 0)
    gate_other = lax.dynamic_slice_in_dim(series_gate, (1 - core) * block, block, 0)
    gates = (gate_own, swap(gate_other, 1), swap(gate_own, 2), swap(gate_other, 3))
    wg1, wu1, wd1 = swap(w_gate, 1), swap(w_up, 1), swap(w_down, 1)

    skip = lax.dynamic_slice_in_dim(skip_gain, lax.axis_index("tm") * own, own, 0)
    skip = skip.reshape(own, 1)
    held = own
    if not direct:
        held = -(-own // 16) * 16
        both = jnp.pad(both, ((0, 0), (0, 0), (0, held - own), (0, 0)))
        skip = jnp.pad(skip, ((0, held - own), (0, 0)))
    both, gates = lax.optimization_barrier((both, gates))
    tables = [jnp.asarray(table) for table in block_tables(block)]
    tables = tables[:2] + [stay(table) for table in tables[2:]]
    conv = pl.pallas_call(
        convolve_kernel,
        out_shape=jax.ShapeDtypeStruct((tm, 2, held, block), bf16),
        in_specs=[whole(SMEM)] + [whole()] * 3 + [whole(HBM)] * 2 + [whole()],
        out_specs=whole(HBM),
        scratch_shapes=[pltpu.VMEM((tm, 2, held, 2 * block), f32)] * 3
        + [pltpu.VMEM(table.shape, bf16) for table in tables[2:]]
        + [pltpu.VMEM((tm, 2, held, block), bf16)]
        + [pltpu.SemaphoreType.DMA((2,))] * 2,
        compiler_params=params(24),
        name="convolve",
    )(place[1], both, *tables, skip)
    if not direct:
        conv = conv[:, :, :own]

    conv = lax.all_to_all(conv, "tm", split_axis=0, concat_axis=0, tiled=True)
    mine, theirs = conv[:, 0], conv[:, 1]
    aside, across, beside = swap(mine, 2), swap(theirs, 3), swap(theirs, 1)

    if not direct:
        mine, beside, aside, across = (
            values.reshape(1, width, block) for values in (mine, beside, aside, across)
        )
    gain = norm_gain.reshape(4, 1, width)
    held = [
        ((2, block, width), bf16),
        ((block, 1), f32),
        ((4, 1, width), f32),
        ((4, block, w_gate.shape[1]), f32),
        ((4, depth, w_gate.shape[1]), bf16),
        ((2 * w_down.shape[0], w_down.shape[1]), bf16),
    ]
    kept = pl.pallas_call(
        feed_first_kernel,
        out_shape=[jax.ShapeDtypeStruct(*spec) for spec in held],
        in_specs=[whole(SMEM)] * 2 + [whole()] * 4 + [whole(HBM)] * 7,
        out_specs=[whole()] * 6,
        scratch_shapes=[
            pltpu.VMEM((block, depth), bf16),
            pltpu.VMEM((4, depth, w_gate.shape[1]), bf16),
            pltpu.SemaphoreType.DMA((11,)),
        ],
        compiler_params=params(24),
        name="feed_first",
    )(
        *place,
        mine,
        beside,
        *gates[:2],
        *map(stay, (gain, w_gate, w_up, wg1, wu1, w_down, wd1)),
    )
    aside, across, kept = lax.optimization_barrier((aside, across, kept))
    outs = pl.pallas_call(
        feed_second_kernel,
        out_shape=[jax.ShapeDtypeStruct((block, width), bf16)] * 4,
        in_specs=[whole(SMEM)] * 2 + [whole()] * 10,
        out_specs=[whole()] * 4,
        scratch_shapes=[pltpu.VMEM((block, depth), bf16)],
        compiler_params=params(24),
        name="feed_second",
    )(*place, aside, across, *gates[2:], *kept)
    return pl.pallas_call(
        finish_kernel,
        out_shape=jax.ShapeDtypeStruct((rows, width), bf16),
        in_specs=[whole(SMEM)] + [whole()] * 4,
        out_specs=whole(),
        compiler_params=params(8),
        name="finish",
    )(place[1], outs[0], swap(outs[2], 2), swap(outs[1], 1), swap(outs[3], 3))


def solution(mesh):
    axes = mesh.devices.reshape(mesh.shape["tm"], mesh.shape["chan"] // 2, 2)
    mesh = jax.sharding.Mesh(axes, ("tm", "x", "core"))
    chan = ("x", "core")
    placed = (
        P("tm", chan),
        P("tm", chan),
        P("tm", chan),
        P(None, chan),
        P(),
        P(chan),
        P("tm"),
        P(chan),
        P(),
        P(None, chan),
        P(None, chan),
        P(chan, None),
    )
    return jax.shard_map(
        shards, mesh=mesh, in_specs=placed, out_specs=P("tm", chan), check_vma=False
    )
```

```python
import functools

import jax
import jax.numpy as jnp
import numpy as np
from jax import lax
from jax.experimental import pallas as pl
from jax.experimental.pallas import tpu as pltpu
from jax.sharding import PartitionSpec as P

FLAGBLK = 64
bf16 = jnp.bfloat16
f32 = jnp.float32


def split_table(table):
    high = table.astype(bf16)
    low = (table - high.astype(np.float64)).astype(bf16)
    return high, low


def block_tables(block):
    freq = np.concatenate([np.arange(0, block, 2), np.arange(1, block, 2)])
    time = np.arange(block)
    turn = np.pi * ((2 * freq[None, :] + 1) * time[:, None] % (4 * block)) / (2 * block)
    forward = np.concatenate([np.cos(turn), -np.sin(turn)], axis=1)
    turn = np.pi * ((2 * freq[:, None] + 1) * (block + time[None, :]) % (4 * block)) / (2 * block)
    inverse = np.concatenate([np.cos(turn), -np.sin(turn)], axis=0) / block
    return split_table(forward) + split_table(inverse)


def dot(left, right):
    return jnp.dot(left, right, preferred_element_type=f32)


def start_loads(pairs, sems):
    loads = [
        pltpu.make_async_copy(src, dst, sems.at[at]) for at, (src, dst) in enumerate(pairs)
    ]
    for load in loads:
        load.start()
    return loads


def prepare_kernel(
    step_ref,
    flags_hbm,
    value_hbm,
    filter_hbm,
    table_hbm,
    mask_hbm,
    out_hbm,
    flags_ref,
    value_ref,
    filter_ref,
    table_ref,
    mask_ref,
    out_ref,
    sems,
    out_sems,
):
    loads = start_loads(
        (
            (filter_hbm, filter_ref),
            (value_hbm, value_ref),
            (flags_hbm, flags_ref),
            (table_hbm, table_ref),
            (mask_hbm, mask_ref),
        ),
        sems,
    )
    rows, width = value_ref.shape
    groups = out_ref.shape[0]
    lanes = 128
    stores = []

    def store(which, low, values):
        share = groups * lanes // width
        first = groups * low // width
        part = out_ref.at[pl.ds(first, share), which]
        part[...] = values.T.reshape(part.shape)
        copy = pltpu.make_async_copy(
            part, out_hbm.at[pl.ds(first, share), which], out_sems.at[len(stores)]
        )
        copy.start()
        stores.append(copy)

    steps = width // lanes if groups * lanes % width == 0 else 1
    lanes = width // steps
    loads[0].wait()
    for low in range(0, width, lanes):
        store(1, low, filter_ref[:, low : low + lanes])
    for load in loads[1:]:
        load.wait()
    embed = table_ref[pl.ds(step_ref[0], 1), :]
    mask = mask_ref[...]
    for low in range(0, width, lanes):
        here = slice(low, low + lanes)
        parts = []
        for at in range(rows // FLAGBLK):
            values = value_ref[at * FLAGBLK : (at + 1) * FLAGBLK, here].astype(f32)
            flag = flags_ref[at].astype(f32)
            parts.append((values + embed[:, here] + flag * mask[:, here]).astype(bf16))
        store(0, low, jnp.concatenate(parts, axis=0))
    for copy in stores:
        copy.wait()


def convolve_kernel(
    core_ref,
    both_ref,
    fh_ref,
    fl_ref,
    gh_hbm,
    gl_hbm,
    skip_ref,
    out_hbm,
    x_ref,
    h_ref,
    z_ref,
    gh_ref,
    gl_ref,
    out_ref,
    sems,
    out_sems,
):
    loads = start_loads(((gh_hbm, gh_ref), (gl_hbm, gl_ref)), sems)
    tm, _, chans, rows = both_ref.shape
    block = rows // 2
    half = block // 2
    nb = 2 * tm
    for which, dst in ((0, x_ref), (1, h_ref)):
        for part in range(2):
            data = both_ref[:, which, :, part * block : (part + 1) * block]
            data = data.reshape(tm * chans, block)
            spec = dot(data, fh_ref[...]) + dot(data, fl_ref[...])
            dst[:, part] = spec.reshape(tm, chans, 2 * block)

    def read(ref, at, sub, lanes):
        return ref[at // 2, at % 2, sub, lanes]

    def window(prev_re, prev_im, cur_re, cur_im, odd):
        if odd:
            return prev_re - cur_im, prev_im + cur_re
        return prev_re + cur_im, prev_im - cur_re

    def tile(step, carry):
        sub = pl.ds(pl.multiple_of(step * 8, 8), 8)
        width = min(128, half)
        for odd in range(2):
            for low in range(odd * half, (odd + 1) * half, width):
                re = slice(low, low + width)
                im = slice(block + low, block + low + width)
                zero = jnp.zeros((8, width), f32)

                def put(a, acc):
                    z_ref[a // 2, a % 2, sub, re] = acc[0] - acc[1]
                    z_ref[a // 2, a % 2, sub, im] = acc[2] - acc[0] - acc[1]

                def load(at):
                    xr, xi = read(x_ref, at, sub, re), read(x_ref, at, sub, im)
                    return xr, xi, xr + xi

                if nb <= 16:
                    taps = []
                    prev = (zero, zero)
                    for d in range(nb):
                        cur = read(h_ref, d, sub, re), read(h_ref, d, sub, im)
                        wr, wi = window(*prev, *cur, odd)
                        taps.append((wr, wi, wr + wi))
                        prev = cur
                    values = [load(at) for at in range(nb)]
                    for a in range(nb):
                        acc = None
                        for d in range(a + 1):
                            terms = [v * t for v, t in zip(values[a - d], taps[d])]
                            acc = terms if acc is None else [p + q for p, q in zip(acc, terms)]
                        put(a, acc)
                else:

                    def out_block(a, carry):
                        def pair(d, acc):
                            before = jnp.maximum(d - 1, 0)
                            keep = (d > 0).astype(f32)
                            wr, wi = window(
                                keep * read(h_ref, before, sub, re),
                                keep * read(h_ref, before, sub, im),
                                read(h_ref, d, sub, re),
                                read(h_ref, d, sub, im),
                                odd,
                            )
                            terms = zip(acc, load(a - d), (wr, wi, wr + wi))
                            return tuple(p + v * t for p, v, t in terms)

                        put(a, lax.fori_loop(0, a + 1, pair, (zero, zero, zero)))
                        return carry

                    lax.fori_loop(0, nb, out_block, 0)
        return carry

    lax.fori_loop(0, chans // 8, tile, 0)
    for load in loads:
        load.wait()
    skip = skip_ref[...]
    stores = []
    for part in range(2):
        spec = z_ref[:, part].reshape(tm * chans, 2 * block)
        high = spec.astype(bf16)
        low = (spec - high.astype(f32)).astype(bf16)
        conv = dot(high, gh_ref[...]) + dot(low, gh_ref[...]) + dot(high, gl_ref[...])
        inputs = both_ref[:, 0, :, part * block : (part + 1) * block].astype(f32)
        out_ref[:, part] = (conv.reshape(tm, chans, block) + skip[None] * inputs).astype(bf16)
        store = pltpu.make_async_copy(
            out_ref.at[:, part], out_hbm.at[:, part ^ core_ref[0]], out_sems.at[part]
        )
        store.start()
        stores.append(store)
    for store in stores:
        store.wait()


def mix(conv_refs, gate_refs, chip, core, mixed_ref, ready_ref, gain_ref, square):
    rows, width = gate_refs[0].shape
    for j, (conv_ref, gate_ref) in enumerate(zip(conv_refs, gate_refs)):
        at = core ^ j
        conv = conv_ref[...].reshape(width, rows).T.astype(f32)
        mixed = (gate_ref[...].astype(f32) * conv).astype(bf16)
        if mixed_ref is not None:
            mixed_ref[j] = mixed
        wide = mixed.astype(f32)
        square = square + jnp.sum(wide * wide, axis=-1, keepdims=True)
        lanes = pl.ds(pl.multiple_of(at * width, width), width)
        ready_ref[:, lanes] = (wide * gain_ref[2 * chip + at]).astype(bf16)
    return square


def feed_first_kernel(
    chip_ref,
    core_ref,
    conv0_ref,
    conv1_ref,
    gate0_ref,
    gate1_ref,
    gain_hbm,
    wg0_hbm,
    wu0_hbm,
    wg1_hbm,
    wu1_hbm,
    wd0_hbm,
    wd1_hbm,
    mixed_ref,
    square_ref,
    gain_ref,
    sums_ref,
    rest_ref,
    down_ref,
    ready_ref,
    now_ref,
    sems,
):
    chip, core = chip_ref[0], core_ref[0]
    depth = now_ref.shape[1]
    hidden = wd0_hbm.shape[0]
    here = pl.ds(pl.multiple_of(chip * depth, depth), depth)
    there = pl.ds(pl.multiple_of((1 - chip) * depth, depth), depth)
    weights = (wg0_hbm, wu0_hbm, wg1_hbm, wu1_hbm)
    loads = start_loads(
        [(gain_hbm, gain_ref)]
        + [(weight.at[here], now_ref.at[at]) for at, weight in enumerate(weights)]
        + [(weight.at[there], rest_ref.at[at]) for at, weight in enumerate(weights)]
        + [
            (weight, down_ref.at[pl.ds(at * hidden, hidden)])
            for at, weight in enumerate((wd0_hbm, wd1_hbm))
        ],
        sems,
    )
    rows = gate0_ref.shape[0]
    loads[0].wait()
    square_ref[...] = mix(
        (conv0_ref, conv1_ref),
        (gate0_ref, gate1_ref),
        chip,
        core,
        mixed_ref,
        ready_ref,
        gain_ref,
        jnp.zeros((rows, 1), f32),
    )
    ready = ready_ref[...]
    for at in range(4):
        loads[1 + at].wait()
        sums_ref[at] = dot(ready, now_ref[at])
    for load in loads[5:]:
        load.wait()


def feed_second_kernel(
    chip_ref,
    core_ref,
    conv2_ref,
    conv3_ref,
    gate2_ref,
    gate3_ref,
    square_ref,
    gain_ref,
    sums_ref,
    rest_ref,
    down_ref,
    hidden_ref,
    out2_ref,
    out3_ref,
    ready_ref,
):
    chip, core = chip_ref[0], core_ref[0]
    rows, width = gate2_ref.shape
    square = mix(
        (conv2_ref, conv3_ref),
        (gate2_ref, gate3_ref),
        1 - chip,
        core,
        None,
        ready_ref,
        gain_ref,
        square_ref[...],
    )
    scale = lax.rsqrt(square / (gain_ref.shape[0] * width) + 1e-06)
    ready = ready_ref[...]
    parts = []
    for at in range(2):
        gate = scale * (sums_ref[2 * at] + dot(ready, rest_ref[2 * at]))
        up = scale * (sums_ref[2 * at + 1] + dot(ready, rest_ref[2 * at + 1]))
        parts.append((gate / (1.0 + jnp.exp(-gate)) * up).astype(bf16))
    hidden = jnp.concatenate(parts, axis=1)
    hidden_ref[...] = hidden
    for j, out_ref in ((2, out2_ref), (3, out3_ref)):
        out_ref[...] = piece(hidden, down_ref, (2 * chip + core) ^ j, width).astype(bf16)


def piece(hidden, down_ref, at, width):
    return dot(hidden, down_ref[:, pl.ds(pl.multiple_of(at * width, width), width)])


def feed_third_kernel(chip_ref, core_ref, hidden_ref, down_ref, mixed_ref, out0_ref, out1_ref):
    here = 2 * chip_ref[0] + core_ref[0]
    width = out0_ref.shape[1]
    hidden = hidden_ref[...]
    for j, out_ref in ((1, out1_ref), (0, out0_ref)):
        part = piece(hidden, down_ref, here ^ j, width) + mixed_ref[j].astype(f32)
        out_ref[...] = part.astype(out_ref.dtype)


def finish_kernel(core_ref, own_ref, side_ref, core1_ref, side1_ref, out_ref):
    block = own_ref.shape[0]
    same = pl.ds(pl.multiple_of(core_ref[0] * block, block), block)
    other = pl.ds(pl.multiple_of((1 - core_ref[0]) * block, block), block)
    out_ref[same, :] = (own_ref[...] + side_ref[...].astype(f32)).astype(bf16)
    out_ref[other, :] = (core1_ref[...].astype(f32) + side1_ref[...].astype(f32)).astype(bf16)


VMEM = pltpu.MemorySpace.VMEM
SMEM = pltpu.MemorySpace.SMEM
HBM = pltpu.MemorySpace.HBM


def whole(space=VMEM):
    return pl.BlockSpec(memory_space=space)


def stay(array):
    return pltpu.with_memory_space_constraint(array, HBM)


def params(mib):
    return pltpu.CompilerParams(vmem_limit_bytes=mib << 20)


def shards(
    series_value,
    series_gate,
    long_filter,
    step_table,
    diffusion_step,
    mask_embed,
    block_flags,
    skip_gain,
    norm_gain,
    w_gate,
    w_up,
    w_down,
):
    tm = lax.axis_size("tm")
    chip, core = lax.axis_index("x"), lax.axis_index("core")
    place = chip.reshape(1).astype(jnp.int32), core.reshape(1).astype(jnp.int32)
    rows, width = series_value.shape
    own = width // tm
    block = rows // 2
    depth = 2 * width

    def swap(values, bits):
        return lax.ppermute(values, ("x", "core"), [(at, at ^ bits) for at in range(4)])

    direct = own % 16 == 0
    shape = (tm, 2, own, rows) if direct else (1, 2, width, rows)
    made = pl.pallas_call(
        prepare_kernel,
        out_shape=jax.ShapeDtypeStruct(shape, bf16),
        in_specs=[whole(SMEM)] + [whole(HBM)] * 5,
        out_specs=whole(HBM),
        scratch_shapes=[
            pltpu.SMEM(block_flags.shape, jnp.int32),
            pltpu.VMEM(series_value.shape, bf16),
            pltpu.VMEM(long_filter.shape, bf16),
            pltpu.VMEM(step_table.shape, f32),
            pltpu.VMEM((1, width), f32),
            pltpu.VMEM(shape, bf16),
            pltpu.SemaphoreType.DMA((5,)),
            pltpu.SemaphoreType.DMA((2 * max(1, width // 128),)),
        ],
        compiler_params=params(32),
        name="prepare",
    )(
        diffusion_step,
        *map(stay, (block_flags, series_value, long_filter, step_table)),
        stay(mask_embed.reshape(1, width)),
    )
    if not direct:
        made = made.reshape(2, tm, own, rows).transpose(1, 0, 2, 3)
    both = lax.all_to_all(made, "tm", split_axis=0, concat_axis=0, tiled=True)

    gate_own = lax.dynamic_slice_in_dim(series_gate, core * block, block, 0)
    gate_other = lax.dynamic_slice_in_dim(series_gate, (1 - core) * block, block, 0)
    gates = (gate_own, swap(gate_other, 1), swap(gate_own, 2), swap(gate_other, 3))
    wg1, wu1, wd1 = swap(w_gate, 1), swap(w_up, 1), swap(w_down, 1)

    skip = lax.dynamic_slice_in_dim(skip_gain, lax.axis_index("tm") * own, own, 0)
    skip = skip.reshape(own, 1)
    held = own
    if not direct:
        held = -(-own // 16) * 16
        both = jnp.pad(both, ((0, 0), (0, 0), (0, held - own), (0, 0)))
        skip = jnp.pad(skip, ((0, held - own), (0, 0)))
    both, gates = lax.optimization_barrier((both, gates))
    tables = [jnp.asarray(table) for table in block_tables(block)]
    tables = tables[:2] + [stay(table) for table in tables[2:]]
    conv = pl.pallas_call(
        convolve_kernel,
        out_shape=jax.ShapeDtypeStruct((tm, 2, held, block), bf16),
        in_specs=[whole(SMEM)] + [whole()] * 3 + [whole(HBM)] * 2 + [whole()],
        out_specs=whole(HBM),
        scratch_shapes=[pltpu.VMEM((tm, 2, held, 2 * block), f32)] * 3
        + [pltpu.VMEM(table.shape, bf16) for table in tables[2:]]
        + [pltpu.VMEM((tm, 2, held, block), bf16)]
        + [pltpu.SemaphoreType.DMA((2,))] * 2,
        compiler_params=params(24),
        name="convolve",
    )(place[1], both, *tables, skip)
    if not direct:
        conv = conv[:, :, :own]

    conv = lax.all_to_all(conv, "tm", split_axis=0, concat_axis=0, tiled=True)
    mine, theirs = conv[:, 0], conv[:, 1]
    aside, across, beside = swap(mine, 2), swap(theirs, 3), swap(theirs, 1)

    if not direct:
        mine, beside, aside, across = (
            values.reshape(1, width, block) for values in (mine, beside, aside, across)
        )
    gain = norm_gain.reshape(4, 1, width)
    held = [
        ((2, block, width), bf16),
        ((block, 1), f32),
        ((4, 1, width), f32),
        ((4, block, w_gate.shape[1]), f32),
        ((4, depth, w_gate.shape[1]), bf16),
        ((2 * w_down.shape[0], w_down.shape[1]), bf16),
    ]
    kept = pl.pallas_call(
        feed_first_kernel,
        out_shape=[jax.ShapeDtypeStruct(*spec) for spec in held],
        in_specs=[whole(SMEM)] * 2 + [whole()] * 4 + [whole(HBM)] * 7,
        out_specs=[whole()] * 6,
        scratch_shapes=[
            pltpu.VMEM((block, depth), bf16),
            pltpu.VMEM((4, depth, w_gate.shape[1]), bf16),
            pltpu.SemaphoreType.DMA((11,)),
        ],
        compiler_params=params(24),
        name="feed_first",
    )(
        *place,
        mine,
        beside,
        *gates[:2],
        *map(stay, (gain, w_gate, w_up, wg1, wu1, w_down, wd1)),
    )
    aside, across, kept = lax.optimization_barrier((aside, across, kept))
    mixed, *kept = kept
    shape = jax.ShapeDtypeStruct((block, width), bf16)
    hidden, *remote = pl.pallas_call(
        feed_second_kernel,
        out_shape=[jax.ShapeDtypeStruct((block, 2 * w_gate.shape[1]), bf16), shape, shape],
        in_specs=[whole(SMEM)] * 2 + [whole()] * 9,
        out_specs=[whole()] * 3,
        scratch_shapes=[pltpu.VMEM((block, depth), bf16)],
        compiler_params=params(24),
        name="feed_second",
    )(*place, aside, across, *gates[2:], *kept)
    side, side1 = swap(remote[0], 2), swap(remote[1], 3)
    local = pl.pallas_call(
        feed_third_kernel,
        out_shape=[jax.ShapeDtypeStruct((block, width), f32), shape],
        in_specs=[whole(SMEM)] * 2 + [whole()] * 3,
        out_specs=[whole()] * 2,
        compiler_params=params(16),
        name="feed_third",
    )(*place, hidden, kept[-1], mixed)
    owned, lent = local
    lent, side = lax.optimization_barrier((lent, side))
    return pl.pallas_call(
        finish_kernel,
        out_shape=jax.ShapeDtypeStruct((rows, width), bf16),
        in_specs=[whole(SMEM)] + [whole()] * 4,
        out_specs=whole(),
        compiler_params=params(8),
        name="finish",
    )(place[1], owned, side, swap(lent, 1), side1)


def solution(mesh):
    axes = mesh.devices.reshape(mesh.shape["tm"], mesh.shape["chan"] // 2, 2)
    mesh = jax.sharding.Mesh(axes, ("tm", "x", "core"))
    chan = ("x", "core")
    placed = (
        P("tm", chan),
        P("tm", chan),
        P("tm", chan),
        P(None, chan),
        P(),
        P(chan),
        P("tm"),
        P(chan),
        P(),
        P(None, chan),
        P(None, chan),
        P(chan, None),
    )
    return jax.shard_map(
        shards, mesh=mesh, in_specs=placed, out_specs=P("tm", chan), check_vma=False
    )
```

```python
import functools

import jax
import jax.numpy as jnp
import numpy as np
from jax import lax
from jax.experimental import pallas as pl
from jax.experimental.pallas import tpu as pltpu
from jax.sharding import PartitionSpec as P

FLAGBLK = 64
bf16 = jnp.bfloat16
f32 = jnp.float32


def split_table(table):
    high = table.astype(bf16)
    low = (table - high.astype(np.float64)).astype(bf16)
    return high, low


def block_tables(block):
    freq = np.concatenate([np.arange(0, block, 2), np.arange(1, block, 2)])
    time = np.arange(block)
    turn = np.pi * ((2 * freq[None, :] + 1) * time[:, None] % (4 * block)) / (2 * block)
    forward = np.concatenate([np.cos(turn), -np.sin(turn)], axis=1)
    turn = np.pi * ((2 * freq[:, None] + 1) * (block + time[None, :]) % (4 * block)) / (2 * block)
    inverse = np.concatenate([np.cos(turn), -np.sin(turn)], axis=0) / block
    return split_table(forward) + split_table(inverse)


def dot(left, right):
    return jnp.dot(left, right, preferred_element_type=f32)


def start_loads(pairs, sems):
    loads = [
        pltpu.make_async_copy(src, dst, sems.at[at]) for at, (src, dst) in enumerate(pairs)
    ]
    for load in loads:
        load.start()
    return loads


def prepare_kernel(
    step_ref,
    flags_hbm,
    value_hbm,
    filter_hbm,
    table_hbm,
    mask_hbm,
    out_hbm,
    flags_ref,
    value_ref,
    filter_ref,
    table_ref,
    mask_ref,
    out_ref,
    sems,
    out_sems,
):
    loads = start_loads(
        (
            (filter_hbm, filter_ref),
            (value_hbm, value_ref),
            (flags_hbm, flags_ref),
            (table_hbm, table_ref),
            (mask_hbm, mask_ref),
        ),
        sems,
    )
    rows, width = value_ref.shape
    groups = out_ref.shape[0]
    lanes = 128
    stores = []

    def store(which, low, values):
        share = groups * lanes // width
        first = groups * low // width
        part = out_ref.at[pl.ds(first, share), which]
        part[...] = values.T.reshape(part.shape)
        copy = pltpu.make_async_copy(
            part, out_hbm.at[pl.ds(first, share), which], out_sems.at[len(stores)]
        )
        copy.start()
        stores.append(copy)

    steps = width // lanes if groups * lanes % width == 0 else 1
    lanes = width // steps
    loads[0].wait()
    for low in range(0, width, lanes):
        store(1, low, filter_ref[:, low : low + lanes])
    for load in loads[1:]:
        load.wait()
    embed = table_ref[pl.ds(step_ref[0], 1), :]
    mask = mask_ref[...]
    for low in range(0, width, lanes):
        here = slice(low, low + lanes)
        parts = []
        for at in range(rows // FLAGBLK):
            values = value_ref[at * FLAGBLK : (at + 1) * FLAGBLK, here].astype(f32)
            flag = flags_ref[at].astype(f32)
            parts.append((values + embed[:, here] + flag * mask[:, here]).astype(bf16))
        store(0, low, jnp.concatenate(parts, axis=0))
    for copy in stores:
        copy.wait()


def convolve_kernel(
    core_ref,
    both_ref,
    fh_ref,
    fl_ref,
    gh_hbm,
    gl_hbm,
    skip_ref,
    out_hbm,
    x_ref,
    h_ref,
    z_ref,
    gh_ref,
    gl_ref,
    out_ref,
    sems,
    out_sems,
):
    loads = start_loads(((gh_hbm, gh_ref), (gl_hbm, gl_ref)), sems)
    tm, _, chans, rows = both_ref.shape
    block = rows // 2
    half = block // 2
    nb = 2 * tm
    for which, dst in ((0, x_ref), (1, h_ref)):
        for part in range(2):
            data = both_ref[:, which, :, part * block : (part + 1) * block]
            data = data.reshape(tm * chans, block)
            spec = dot(data, fh_ref[...]) + dot(data, fl_ref[...])
            dst[:, part] = spec.reshape(tm, chans, 2 * block)

    def read(ref, at, sub, lanes):
        return ref[at // 2, at % 2, sub, lanes]

    def window(prev_re, prev_im, cur_re, cur_im, odd):
        if odd:
            return prev_re - cur_im, prev_im + cur_re
        return prev_re + cur_im, prev_im - cur_re

    def tile(step, carry):
        sub = pl.ds(pl.multiple_of(step * 8, 8), 8)
        width = min(128, half)
        for odd in range(2):
            for low in range(odd * half, (odd + 1) * half, width):
                re = slice(low, low + width)
                im = slice(block + low, block + low + width)
                zero = jnp.zeros((8, width), f32)

                def put(a, acc):
                    z_ref[a // 2, a % 2, sub, re] = acc[0] - acc[1]
                    z_ref[a // 2, a % 2, sub, im] = acc[2] - acc[0] - acc[1]

                def load(at):
                    xr, xi = read(x_ref, at, sub, re), read(x_ref, at, sub, im)
                    return xr, xi, xr + xi

                if nb <= 16:
                    taps = []
                    prev = (zero, zero)
                    for d in range(nb):
                        cur = read(h_ref, d, sub, re), read(h_ref, d, sub, im)
                        wr, wi = window(*prev, *cur, odd)
                        taps.append((wr, wi, wr + wi))
                        prev = cur
                    values = [load(at) for at in range(nb)]
                    for a in range(nb):
                        acc = None
                        for d in range(a + 1):
                            terms = [v * t for v, t in zip(values[a - d], taps[d])]
                            acc = terms if acc is None else [p + q for p, q in zip(acc, terms)]
                        put(a, acc)
                else:

                    def out_block(a, carry):
                        def pair(d, acc):
                            before = jnp.maximum(d - 1, 0)
                            keep = (d > 0).astype(f32)
                            wr, wi = window(
                                keep * read(h_ref, before, sub, re),
                                keep * read(h_ref, before, sub, im),
                                read(h_ref, d, sub, re),
                                read(h_ref, d, sub, im),
                                odd,
                            )
                            terms = zip(acc, load(a - d), (wr, wi, wr + wi))
                            return tuple(p + v * t for p, v, t in terms)

                        put(a, lax.fori_loop(0, a + 1, pair, (zero, zero, zero)))
                        return carry

                    lax.fori_loop(0, nb, out_block, 0)
        return carry

    lax.fori_loop(0, chans // 8, tile, 0)
    for load in loads:
        load.wait()
    skip = skip_ref[...]
    stores = []
    for part in range(2):
        spec = z_ref[:, part].reshape(tm * chans, 2 * block)
        high = spec.astype(bf16)
        low = (spec - high.astype(f32)).astype(bf16)
        conv = dot(high, gh_ref[...]) + dot(low, gh_ref[...]) + dot(high, gl_ref[...])
        inputs = both_ref[:, 0, :, part * block : (part + 1) * block].astype(f32)
        out_ref[:, part] = (conv.reshape(tm, chans, block) + skip[None] * inputs).astype(bf16)
        store = pltpu.make_async_copy(
            out_ref.at[:, part], out_hbm.at[:, part ^ core_ref[0]], out_sems.at[part]
        )
        store.start()
        stores.append(store)
    for store in stores:
        store.wait()


def mix(conv_refs, gate_refs, ats, mixed_ref, ready_ref, gain_ref, square):
    rows, width = gate_refs[0].shape
    for j, (conv_ref, gate_ref, at) in enumerate(zip(conv_refs, gate_refs, ats)):
        conv = conv_ref[...].reshape(width, rows).T.astype(f32)
        mixed = (gate_ref[...].astype(f32) * conv).astype(bf16)
        if j == 0:
            mixed_ref[...] = mixed
        wide = mixed.astype(f32)
        square = square + jnp.sum(wide * wide, axis=-1, keepdims=True)
        ready_ref[:, j * width : (j + 1) * width] = (wide * gain_ref[at]).astype(bf16)
    return square


def feed_first_kernel(
    chip_ref,
    core_ref,
    conv0_ref,
    gate0_ref,
    gain_hbm,
    wg0_hbm,
    wu0_hbm,
    wg1_hbm,
    wu1_hbm,
    wd0_hbm,
    wd1_hbm,
    mixed_ref,
    square_ref,
    gain_ref,
    sums_ref,
    rest_ref,
    down_ref,
    ready_ref,
    now_ref,
    sems,
):
    here = 2 * chip_ref[0] + core_ref[0]
    rows, width = gate0_ref.shape
    hidden = wd0_hbm.shape[0]
    weights = (wg0_hbm, wu0_hbm, wg1_hbm, wu1_hbm)

    def source(weight, j):
        return weight.at[pl.ds(pl.multiple_of((here ^ j) * width, width), width)]

    loads = start_loads(
        [(gain_hbm, gain_ref)]
        + [(source(weight, 0), now_ref.at[at]) for at, weight in enumerate(weights)]
        + [
            (source(weight, j), rest_ref.at[at, pl.ds((j - 1) * width, width)])
            for j in (1, 2, 3)
            for at, weight in enumerate(weights)
        ]
        + [
            (weight, down_ref.at[pl.ds(at * hidden, hidden)])
            for at, weight in enumerate((wd0_hbm, wd1_hbm))
        ],
        sems,
    )
    loads[0].wait()
    square_ref[...] = mix(
        (conv0_ref,),
        (gate0_ref,),
        (here,),
        mixed_ref,
        ready_ref,
        gain_ref,
        jnp.zeros((rows, 1), f32),
    )
    ready = ready_ref[...]
    for at in range(4):
        loads[1 + at].wait()
        sums_ref[at] = dot(ready, now_ref[at])
    for load in loads[5:]:
        load.wait()


def feed_second_kernel(
    chip_ref,
    core_ref,
    conv1_ref,
    conv2_ref,
    conv3_ref,
    gate1_ref,
    gate2_ref,
    gate3_ref,
    square_ref,
    gain_ref,
    sums_ref,
    rest_ref,
    down_ref,
    mixed_ref,
    hidden_ref,
    out2_ref,
    out3_ref,
    ready_ref,
):
    here = 2 * chip_ref[0] + core_ref[0]
    width = gate1_ref.shape[1]
    square = mix(
        (conv1_ref, conv2_ref, conv3_ref),
        (gate1_ref, gate2_ref, gate3_ref),
        (here ^ 1, here ^ 2, here ^ 3),
        mixed_ref,
        ready_ref,
        gain_ref,
        square_ref[...],
    )
    scale = lax.rsqrt(square / (gain_ref.shape[0] * width) + 1e-06)
    ready = ready_ref[...]
    parts = []
    for at in range(2):
        gate = scale * (sums_ref[2 * at] + dot(ready, rest_ref[2 * at]))
        up = scale * (sums_ref[2 * at + 1] + dot(ready, rest_ref[2 * at + 1]))
        parts.append((gate / (1.0 + jnp.exp(-gate)) * up).astype(bf16))
    hidden = jnp.concatenate(parts, axis=1)
    hidden_ref[...] = hidden
    for j, out_ref in ((2, out2_ref), (3, out3_ref)):
        out_ref[...] = piece(hidden, down_ref, here ^ j, width).astype(bf16)


def piece(hidden, down_ref, at, width):
    return dot(hidden, down_ref[:, pl.ds(pl.multiple_of(at * width, width), width)])


def feed_third_kernel(
    chip_ref, core_ref, hidden_ref, down_ref, mixed0_ref, mixed1_ref, out0_ref, out1_ref
):
    here = 2 * chip_ref[0] + core_ref[0]
    width = out0_ref.shape[1]
    hidden = hidden_ref[...]
    for j, mixed_ref, out_ref in ((1, mixed1_ref, out1_ref), (0, mixed0_ref, out0_ref)):
        part = piece(hidden, down_ref, here ^ j, width) + mixed_ref[...].astype(f32)
        out_ref[...] = part.astype(out_ref.dtype)


def finish_kernel(core_ref, own_ref, side_ref, core1_ref, side1_ref, out_ref):
    block = own_ref.shape[0]
    same = pl.ds(pl.multiple_of(core_ref[0] * block, block), block)
    other = pl.ds(pl.multiple_of((1 - core_ref[0]) * block, block), block)
    out_ref[same, :] = (own_ref[...] + side_ref[...].astype(f32)).astype(bf16)
    out_ref[other, :] = (core1_ref[...].astype(f32) + side1_ref[...].astype(f32)).astype(bf16)


VMEM = pltpu.MemorySpace.VMEM
SMEM = pltpu.MemorySpace.SMEM
HBM = pltpu.MemorySpace.HBM


def whole(space=VMEM):
    return pl.BlockSpec(memory_space=space)


def stay(array):
    return pltpu.with_memory_space_constraint(array, HBM)


def params(mib):
    return pltpu.CompilerParams(vmem_limit_bytes=mib << 20)


def shards(
    series_value,
    series_gate,
    long_filter,
    step_table,
    diffusion_step,
    mask_embed,
    block_flags,
    skip_gain,
    norm_gain,
    w_gate,
    w_up,
    w_down,
):
    tm = lax.axis_size("tm")
    chip, core = lax.axis_index("x"), lax.axis_index("core")
    place = chip.reshape(1).astype(jnp.int32), core.reshape(1).astype(jnp.int32)
    rows, width = series_value.shape
    own = width // tm
    block = rows // 2

    def swap(values, bits):
        return lax.ppermute(values, ("x", "core"), [(at, at ^ bits) for at in range(4)])

    direct = own % 16 == 0
    shape = (tm, 2, own, rows) if direct else (1, 2, width, rows)
    made = pl.pallas_call(
        prepare_kernel,
        out_shape=jax.ShapeDtypeStruct(shape, bf16),
        in_specs=[whole(SMEM)] + [whole(HBM)] * 5,
        out_specs=whole(HBM),
        scratch_shapes=[
            pltpu.SMEM(block_flags.shape, jnp.int32),
            pltpu.VMEM(series_value.shape, bf16),
            pltpu.VMEM(long_filter.shape, bf16),
            pltpu.VMEM(step_table.shape, f32),
            pltpu.VMEM((1, width), f32),
            pltpu.VMEM(shape, bf16),
            pltpu.SemaphoreType.DMA((5,)),
            pltpu.SemaphoreType.DMA((2 * max(1, width // 128),)),
        ],
        compiler_params=params(32),
        name="prepare",
    )(
        diffusion_step,
        *map(stay, (block_flags, series_value, long_filter, step_table)),
        stay(mask_embed.reshape(1, width)),
    )
    if not direct:
        made = made.reshape(2, tm, own, rows).transpose(1, 0, 2, 3)
    both = lax.all_to_all(made, "tm", split_axis=0, concat_axis=0, tiled=True)

    gate_own = lax.dynamic_slice_in_dim(series_gate, core * block, block, 0)
    gate_other = lax.dynamic_slice_in_dim(series_gate, (1 - core) * block, block, 0)
    gates = (gate_own, swap(gate_other, 1), swap(gate_own, 2), swap(gate_other, 3))
    wg1, wu1, wd1 = swap(w_gate, 1), swap(w_up, 1), swap(w_down, 1)

    skip = lax.dynamic_slice_in_dim(skip_gain, lax.axis_index("tm") * own, own, 0)
    skip = skip.reshape(own, 1)
    held = own
    if not direct:
        held = -(-own // 16) * 16
        both = jnp.pad(both, ((0, 0), (0, 0), (0, held - own), (0, 0)))
        skip = jnp.pad(skip, ((0, held - own), (0, 0)))
    both, gates = lax.optimization_barrier((both, gates))
    tables = [jnp.asarray(table) for table in block_tables(block)]
    tables = tables[:2] + [stay(table) for table in tables[2:]]
    conv = pl.pallas_call(
        convolve_kernel,
        out_shape=jax.ShapeDtypeStruct((tm, 2, held, block), bf16),
        in_specs=[whole(SMEM)] + [whole()] * 3 + [whole(HBM)] * 2 + [whole()],
        out_specs=whole(HBM),
        scratch_shapes=[pltpu.VMEM((tm, 2, held, 2 * block), f32)] * 3
        + [pltpu.VMEM(table.shape, bf16) for table in tables[2:]]
        + [pltpu.VMEM((tm, 2, held, block), bf16)]
        + [pltpu.SemaphoreType.DMA((2,))] * 2,
        compiler_params=params(24),
        name="convolve",
    )(place[1], both, *tables, skip)
    if not direct:
        conv = conv[:, :, :own]

    conv = lax.all_to_all(conv, "tm", split_axis=0, concat_axis=0, tiled=True)
    mine, theirs = conv[:, 0], conv[:, 1]
    aside, across = swap(mine, 2), swap(theirs, 3)

    def view(values):
        return values if direct else values.reshape(1, width, block)

    gain = norm_gain.reshape(4, 1, width)
    held = [
        ((block, width), bf16),
        ((block, 1), f32),
        ((4, 1, width), f32),
        ((4, block, w_gate.shape[1]), f32),
        ((4, 3 * width, w_gate.shape[1]), bf16),
        ((2 * w_down.shape[0], w_down.shape[1]), bf16),
    ]
    kept = pl.pallas_call(
        feed_first_kernel,
        out_shape=[jax.ShapeDtypeStruct(*spec) for spec in held],
        in_specs=[whole(SMEM)] * 2 + [whole()] * 2 + [whole(HBM)] * 7,
        out_specs=[whole()] * 6,
        scratch_shapes=[
            pltpu.VMEM((block, width), bf16),
            pltpu.VMEM((4, width, w_gate.shape[1]), bf16),
            pltpu.SemaphoreType.DMA((19,)),
        ],
        compiler_params=params(24),
        name="feed_first",
    )(
        *place,
        view(mine),
        gates[0],
        *map(stay, (gain, w_gate, w_up, wg1, wu1, w_down, wd1)),
    )
    theirs, aside, kept = lax.optimization_barrier((theirs, aside, kept))
    beside = swap(theirs, 1)
    mixed0, *kept = kept
    shape = jax.ShapeDtypeStruct((block, width), bf16)
    mixed1, hidden, *remote = pl.pallas_call(
        feed_second_kernel,
        out_shape=[shape, jax.ShapeDtypeStruct((block, 2 * w_gate.shape[1]), bf16), shape, shape],
        in_specs=[whole(SMEM)] * 2 + [whole()] * 11,
        out_specs=[whole()] * 4,
        scratch_shapes=[pltpu.VMEM((block, 3 * width), bf16)],
        compiler_params=params(24),
        name="feed_second",
    )(*place, *map(view, (beside, aside, across)), *gates[1:], *kept)
    side, side1 = swap(remote[0], 2), swap(remote[1], 3)
    local = pl.pallas_call(
        feed_third_kernel,
        out_shape=[jax.ShapeDtypeStruct((block, width), f32), shape],
        in_specs=[whole(SMEM)] * 2 + [whole()] * 4,
        out_specs=[whole()] * 2,
        compiler_params=params(16),
        name="feed_third",
    )(*place, hidden, kept[-1], mixed0, mixed1)
    owned, lent = local
    lent, side = lax.optimization_barrier((lent, side))
    return pl.pallas_call(
        finish_kernel,
        out_shape=jax.ShapeDtypeStruct((rows, width), bf16),
        in_specs=[whole(SMEM)] + [whole()] * 4,
        out_specs=whole(),
        compiler_params=params(8),
        name="finish",
    )(place[1], owned, side, swap(lent, 1), side1)


def solution(mesh):
    axes = mesh.devices.reshape(mesh.shape["tm"], mesh.shape["chan"] // 2, 2)
    mesh = jax.sharding.Mesh(axes, ("tm", "x", "core"))
    chan = ("x", "core")
    placed = (
        P("tm", chan),
        P("tm", chan),
        P("tm", chan),
        P(None, chan),
        P(),
        P(chan),
        P("tm"),
        P(chan),
        P(),
        P(None, chan),
        P(None, chan),
        P(chan, None),
    )
    return jax.shard_map(
        shards, mesh=mesh, in_specs=placed, out_specs=P("tm", chan), check_vma=False
    )
```

```python
import functools

import jax
import jax.numpy as jnp
import numpy as np
from jax import lax
from jax.experimental import pallas as pl
from jax.experimental.pallas import tpu as pltpu
from jax.sharding import PartitionSpec as P

FLAGBLK = 64
bf16 = jnp.bfloat16
f32 = jnp.float32


def split_table(table):
    high = table.astype(bf16)
    low = (table - high.astype(np.float64)).astype(bf16)
    return high, low


def block_tables(block):
    freq = np.concatenate([np.arange(0, block, 2), np.arange(1, block, 2)])
    time = np.arange(block)
    turn = np.pi * ((2 * freq[None, :] + 1) * time[:, None] % (4 * block)) / (2 * block)
    forward = np.concatenate([np.cos(turn), -np.sin(turn)], axis=1)
    turn = np.pi * ((2 * freq[:, None] + 1) * (block + time[None, :]) % (4 * block)) / (2 * block)
    inverse = np.concatenate([np.cos(turn), -np.sin(turn)], axis=0) / block
    return split_table(forward) + split_table(inverse)


def dot(left, right):
    return jnp.dot(left, right, preferred_element_type=f32)


def start_loads(pairs, sems):
    loads = [
        pltpu.make_async_copy(src, dst, sems.at[at]) for at, (src, dst) in enumerate(pairs)
    ]
    for load in loads:
        load.start()
    return loads


def prepare_kernel(
    step_ref,
    flags_hbm,
    value_hbm,
    filter_hbm,
    table_hbm,
    mask_hbm,
    out_hbm,
    flags_ref,
    value_ref,
    filter_ref,
    table_ref,
    mask_ref,
    out_ref,
    sems,
    out_sems,
):
    loads = start_loads(
        (
            (filter_hbm, filter_ref),
            (value_hbm, value_ref),
            (flags_hbm, flags_ref),
            (table_hbm, table_ref),
            (mask_hbm, mask_ref),
        ),
        sems,
    )
    rows, width = value_ref.shape
    groups = out_ref.shape[0]
    lanes = 128
    stores = []

    def store(which, low, values):
        share = groups * lanes // width
        first = groups * low // width
        part = out_ref.at[pl.ds(first, share), which]
        part[...] = values.T.reshape(part.shape)
        copy = pltpu.make_async_copy(
            part, out_hbm.at[pl.ds(first, share), which], out_sems.at[len(stores)]
        )
        copy.start()
        stores.append(copy)

    steps = width // lanes if groups * lanes % width == 0 else 1
    lanes = width // steps
    loads[0].wait()
    for low in range(0, width, lanes):
        store(1, low, filter_ref[:, low : low + lanes])
    for load in loads[1:]:
        load.wait()
    embed = table_ref[pl.ds(step_ref[0], 1), :]
    mask = mask_ref[...]
    for low in range(0, width, lanes):
        here = slice(low, low + lanes)
        parts = []
        for at in range(rows // FLAGBLK):
            values = value_ref[at * FLAGBLK : (at + 1) * FLAGBLK, here].astype(f32)
            flag = flags_ref[at].astype(f32)
            parts.append((values + embed[:, here] + flag * mask[:, here]).astype(bf16))
        store(0, low, jnp.concatenate(parts, axis=0))
    for copy in stores:
        copy.wait()


def convolve_kernel(
    core_ref,
    both_ref,
    fh_ref,
    fl_ref,
    gh_hbm,
    gl_hbm,
    skip_ref,
    out_ref,
    x_ref,
    h_ref,
    z_ref,
    gh_ref,
    gl_ref,
    sems,
):
    loads = start_loads(((gh_hbm, gh_ref), (gl_hbm, gl_ref)), sems)
    tm, _, chans, rows = both_ref.shape
    block = rows // 2
    half = block // 2
    nb = 2 * tm
    for which, dst in ((0, x_ref), (1, h_ref)):
        for part in range(2):
            data = both_ref[:, which, :, part * block : (part + 1) * block]
            data = data.reshape(tm * chans, block)
            spec = dot(data, fh_ref[...]) + dot(data, fl_ref[...])
            dst[:, part] = spec.reshape(tm, chans, 2 * block)

    def read(ref, at, sub, lanes):
        return ref[at // 2, at % 2, sub, lanes]

    def window(prev_re, prev_im, cur_re, cur_im, odd):
        if odd:
            return prev_re - cur_im, prev_im + cur_re
        return prev_re + cur_im, prev_im - cur_re

    def tile(step, carry):
        sub = pl.ds(pl.multiple_of(step * 8, 8), 8)
        width = min(128, half)
        for odd in range(2):
            for low in range(odd * half, (odd + 1) * half, width):
                re = slice(low, low + width)
                im = slice(block + low, block + low + width)
                zero = jnp.zeros((8, width), f32)

                def put(a, acc):
                    z_ref[a // 2, a % 2, sub, re] = acc[0] - acc[1]
                    z_ref[a // 2, a % 2, sub, im] = acc[2] - acc[0] - acc[1]

                def load(at):
                    xr, xi = read(x_ref, at, sub, re), read(x_ref, at, sub, im)
                    return xr, xi, xr + xi

                if nb <= 16:
                    taps = []
                    prev = (zero, zero)
                    for d in range(nb):
                        cur = read(h_ref, d, sub, re), read(h_ref, d, sub, im)
                        wr, wi = window(*prev, *cur, odd)
                        taps.append((wr, wi, wr + wi))
                        prev = cur
                    values = [load(at) for at in range(nb)]
                    for a in range(nb):
                        acc = None
                        for d in range(a + 1):
                            terms = [v * t for v, t in zip(values[a - d], taps[d])]
                            acc = terms if acc is None else [p + q for p, q in zip(acc, terms)]
                        put(a, acc)
                else:

                    def out_block(a, carry):
                        def pair(d, acc):
                            before = jnp.maximum(d - 1, 0)
                            keep = (d > 0).astype(f32)
                            wr, wi = window(
                                keep * read(h_ref, before, sub, re),
                                keep * read(h_ref, before, sub, im),
                                read(h_ref, d, sub, re),
                                read(h_ref, d, sub, im),
                                odd,
                            )
                            terms = zip(acc, load(a - d), (wr, wi, wr + wi))
                            return tuple(p + v * t for p, v, t in terms)

                        put(a, lax.fori_loop(0, a + 1, pair, (zero, zero, zero)))
                        return carry

                    lax.fori_loop(0, nb, out_block, 0)
        return carry

    lax.fori_loop(0, chans // 8, tile, 0)
    for load in loads:
        load.wait()
    skip = skip_ref[...]
    for part in range(2):
        spec = z_ref[:, part].reshape(tm * chans, 2 * block)
        high = spec.astype(bf16)
        low = (spec - high.astype(f32)).astype(bf16)
        conv = dot(high, gh_ref[...]) + dot(low, gh_ref[...]) + dot(high, gl_ref[...])
        inputs = both_ref[:, 0, :, part * block : (part + 1) * block].astype(f32)
        total = conv.reshape(tm, chans, block) + skip[None] * inputs
        out_ref[:, part ^ core_ref[0]] = total.astype(bf16)


def mix(conv_refs, gate_refs, ats, mixed_ref, ready_ref, gain_ref, square):
    rows, width = gate_refs[0].shape
    for j, (conv_ref, gate_ref, at) in enumerate(zip(conv_refs, gate_refs, ats)):
        conv = conv_ref[...].reshape(width, rows).T.astype(f32)
        mixed = (gate_ref[...].astype(f32) * conv).astype(bf16)
        if j == 0:
            mixed_ref[...] = mixed
        wide = mixed.astype(f32)
        square = square + jnp.sum(wide * wide, axis=-1, keepdims=True)
        ready_ref[:, j * width : (j + 1) * width] = (wide * gain_ref[at]).astype(bf16)
    return square


def feed_first_kernel(
    chip_ref,
    core_ref,
    conv0_ref,
    gate0_ref,
    gain_hbm,
    wg0_hbm,
    wu0_hbm,
    wg1_hbm,
    wu1_hbm,
    wd0_hbm,
    wd1_hbm,
    mixed_ref,
    square_ref,
    gain_ref,
    sums_ref,
    rest_ref,
    down_ref,
    ready_ref,
    now_ref,
    sems,
):
    here = 2 * chip_ref[0] + core_ref[0]
    rows, width = gate0_ref.shape
    hidden = wd0_hbm.shape[0]
    weights = (wg0_hbm, wu0_hbm, wg1_hbm, wu1_hbm)

    def source(weight, j):
        return weight.at[pl.ds(pl.multiple_of((here ^ j) * width, width), width)]

    loads = start_loads(
        [(gain_hbm, gain_ref)]
        + [(source(weight, 0), now_ref.at[at]) for at, weight in enumerate(weights)]
        + [
            (source(weight, j), rest_ref.at[at, pl.ds((j - 1) * width, width)])
            for j in (1, 2, 3)
            for at, weight in enumerate(weights)
        ]
        + [
            (weight, down_ref.at[pl.ds(at * hidden, hidden)])
            for at, weight in enumerate((wd0_hbm, wd1_hbm))
        ],
        sems,
    )
    loads[0].wait()
    square_ref[...] = mix(
        (conv0_ref,),
        (gate0_ref,),
        (here,),
        mixed_ref,
        ready_ref,
        gain_ref,
        jnp.zeros((rows, 1), f32),
    )
    ready = ready_ref[...]
    for at in range(4):
        loads[1 + at].wait()
        sums_ref[at] = dot(ready, now_ref[at])
    for load in loads[5:]:
        load.wait()


def feed_second_kernel(
    chip_ref,
    core_ref,
    conv1_ref,
    conv2_ref,
    conv3_ref,
    gate1_ref,
    gate2_ref,
    gate3_ref,
    square_ref,
    gain_ref,
    sums_ref,
    rest_ref,
    down_ref,
    mixed_ref,
    hidden_ref,
    out2_ref,
    out3_ref,
    ready_ref,
):
    here = 2 * chip_ref[0] + core_ref[0]
    width = gate1_ref.shape[1]
    square = mix(
        (conv1_ref, conv2_ref, conv3_ref),
        (gate1_ref, gate2_ref, gate3_ref),
        (here ^ 1, here ^ 2, here ^ 3),
        mixed_ref,
        ready_ref,
        gain_ref,
        square_ref[...],
    )
    scale = lax.rsqrt(square / (gain_ref.shape[0] * width) + 1e-06)
    ready = ready_ref[...]
    parts = []
    for at in range(2):
        gate = scale * (sums_ref[2 * at] + dot(ready, rest_ref[2 * at]))
        up = scale * (sums_ref[2 * at + 1] + dot(ready, rest_ref[2 * at + 1]))
        parts.append((gate / (1.0 + jnp.exp(-gate)) * up).astype(bf16))
    hidden = jnp.concatenate(parts, axis=1)
    hidden_ref[...] = hidden
    for j, out_ref in ((2, out2_ref), (3, out3_ref)):
        out_ref[...] = piece(hidden, down_ref, here ^ j, width).astype(bf16)


def piece(hidden, down_ref, at, width):
    return dot(hidden, down_ref[:, pl.ds(pl.multiple_of(at * width, width), width)])


def feed_third_kernel(
    chip_ref, core_ref, hidden_ref, down_ref, mixed0_ref, mixed1_ref, out0_ref, out1_ref
):
    here = 2 * chip_ref[0] + core_ref[0]
    width = out0_ref.shape[1]
    hidden = hidden_ref[...]
    for j, mixed_ref, out_ref in ((1, mixed1_ref, out1_ref), (0, mixed0_ref, out0_ref)):
        part = piece(hidden, down_ref, here ^ j, width) + mixed_ref[...].astype(f32)
        out_ref[...] = part.astype(out_ref.dtype)


def finish_kernel(core_ref, own_ref, side_ref, core1_ref, side1_ref, out_ref):
    block = own_ref.shape[0]
    same = pl.ds(pl.multiple_of(core_ref[0] * block, block), block)
    other = pl.ds(pl.multiple_of((1 - core_ref[0]) * block, block), block)
    out_ref[same, :] = (own_ref[...] + side_ref[...].astype(f32)).astype(bf16)
    out_ref[other, :] = (core1_ref[...].astype(f32) + side1_ref[...].astype(f32)).astype(bf16)


VMEM = pltpu.MemorySpace.VMEM
SMEM = pltpu.MemorySpace.SMEM
HBM = pltpu.MemorySpace.HBM


def whole(space=VMEM):
    return pl.BlockSpec(memory_space=space)


def stay(array):
    return pltpu.with_memory_space_constraint(array, HBM)


def params(mib):
    return pltpu.CompilerParams(vmem_limit_bytes=mib << 20)


def shards(
    series_value,
    series_gate,
    long_filter,
    step_table,
    diffusion_step,
    mask_embed,
    block_flags,
    skip_gain,
    norm_gain,
    w_gate,
    w_up,
    w_down,
):
    tm = lax.axis_size("tm")
    chip, core = lax.axis_index("x"), lax.axis_index("core")
    place = chip.reshape(1).astype(jnp.int32), core.reshape(1).astype(jnp.int32)
    rows, width = series_value.shape
    own = width // tm
    block = rows // 2

    def swap(values, bits):
        return lax.ppermute(values, ("x", "core"), [(at, at ^ bits) for at in range(4)])

    direct = own % 16 == 0
    shape = (tm, 2, own, rows) if direct else (1, 2, width, rows)
    made = pl.pallas_call(
        prepare_kernel,
        out_shape=jax.ShapeDtypeStruct(shape, bf16),
        in_specs=[whole(SMEM)] + [whole(HBM)] * 5,
        out_specs=whole(HBM),
        scratch_shapes=[
            pltpu.SMEM(block_flags.shape, jnp.int32),
            pltpu.VMEM(series_value.shape, bf16),
            pltpu.VMEM(long_filter.shape, bf16),
            pltpu.VMEM(step_table.shape, f32),
            pltpu.VMEM((1, width), f32),
            pltpu.VMEM(shape, bf16),
            pltpu.SemaphoreType.DMA((5,)),
            pltpu.SemaphoreType.DMA((2 * max(1, width // 128),)),
        ],
        compiler_params=params(32),
        name="prepare",
    )(
        diffusion_step,
        *map(stay, (block_flags, series_value, long_filter, step_table)),
        stay(mask_embed.reshape(1, width)),
    )
    if not direct:
        made = made.reshape(2, tm, own, rows).transpose(1, 0, 2, 3)
    both = lax.all_to_all(made, "tm", split_axis=0, concat_axis=0, tiled=True)

    gate_own = lax.dynamic_slice_in_dim(series_gate, core * block, block, 0)
    gate_other = lax.dynamic_slice_in_dim(series_gate, (1 - core) * block, block, 0)
    gates = (gate_own, swap(gate_other, 1), swap(gate_own, 2), swap(gate_other, 3))
    wg1, wu1, wd1 = swap(w_gate, 1), swap(w_up, 1), swap(w_down, 1)

    skip = lax.dynamic_slice_in_dim(skip_gain, lax.axis_index("tm") * own, own, 0)
    skip = skip.reshape(own, 1)
    held = own
    if not direct:
        held = -(-own // 16) * 16
        both = jnp.pad(both, ((0, 0), (0, 0), (0, held - own), (0, 0)))
        skip = jnp.pad(skip, ((0, held - own), (0, 0)))
    both, gates = lax.optimization_barrier((both, gates))
    tables = [jnp.asarray(table) for table in block_tables(block)]
    tables = tables[:2] + [stay(table) for table in tables[2:]]
    conv = pl.pallas_call(
        convolve_kernel,
        out_shape=jax.ShapeDtypeStruct((tm, 2, held, block), bf16),
        in_specs=[whole(SMEM)] + [whole()] * 3 + [whole(HBM)] * 2 + [whole()],
        out_specs=whole(),
        scratch_shapes=[pltpu.VMEM((tm, 2, held, 2 * block), f32)] * 3
        + [pltpu.VMEM(table.shape, bf16) for table in tables[2:]]
        + [pltpu.SemaphoreType.DMA((2,))],
        compiler_params=params(24),
        name="convolve",
    )(place[1], both, *tables, skip)
    if not direct:
        conv = conv[:, :, :own]

    conv = lax.all_to_all(conv, "tm", split_axis=0, concat_axis=0, tiled=True)
    mine, theirs = conv[:, 0], conv[:, 1]
    aside, across = swap(mine, 2), swap(theirs, 3)

    def view(values):
        return values if direct else values.reshape(1, width, block)

    gain = norm_gain.reshape(4, 1, width)
    held = [
        ((block, width), bf16),
        ((block, 1), f32),
        ((4, 1, width), f32),
        ((4, block, w_gate.shape[1]), f32),
        ((4, 3 * width, w_gate.shape[1]), bf16),
        ((2 * w_down.shape[0], w_down.shape[1]), bf16),
    ]
    kept = pl.pallas_call(
        feed_first_kernel,
        out_shape=[jax.ShapeDtypeStruct(*spec) for spec in held],
        in_specs=[whole(SMEM)] * 2 + [whole()] * 2 + [whole(HBM)] * 7,
        out_specs=[whole()] * 6,
        scratch_shapes=[
            pltpu.VMEM((block, width), bf16),
            pltpu.VMEM((4, width, w_gate.shape[1]), bf16),
            pltpu.SemaphoreType.DMA((19,)),
        ],
        compiler_params=params(24),
        name="feed_first",
    )(
        *place,
        view(mine),
        gates[0],
        *map(stay, (gain, w_gate, w_up, wg1, wu1, w_down, wd1)),
    )
    theirs, aside, kept = lax.optimization_barrier((theirs, aside, kept))
    beside = swap(theirs, 1)
    mixed0, *kept = kept
    shape = jax.ShapeDtypeStruct((block, width), bf16)
    mixed1, hidden, *remote = pl.pallas_call(
        feed_second_kernel,
        out_shape=[shape, jax.ShapeDtypeStruct((block, 2 * w_gate.shape[1]), bf16), shape, shape],
        in_specs=[whole(SMEM)] * 2 + [whole()] * 11,
        out_specs=[whole()] * 4,
        scratch_shapes=[pltpu.VMEM((block, 3 * width), bf16)],
        compiler_params=params(24),
        name="feed_second",
    )(*place, *map(view, (beside, aside, across)), *gates[1:], *kept)
    side, side1 = swap(remote[0], 2), swap(remote[1], 3)
    local = pl.pallas_call(
        feed_third_kernel,
        out_shape=[jax.ShapeDtypeStruct((block, width), f32), shape],
        in_specs=[whole(SMEM)] * 2 + [whole()] * 4,
        out_specs=[whole()] * 2,
        compiler_params=params(16),
        name="feed_third",
    )(*place, hidden, kept[-1], mixed0, mixed1)
    owned, lent = local
    lent, side = lax.optimization_barrier((lent, side))
    return pl.pallas_call(
        finish_kernel,
        out_shape=jax.ShapeDtypeStruct((rows, width), bf16),
        in_specs=[whole(SMEM)] + [whole()] * 4,
        out_specs=whole(),
        compiler_params=params(8),
        name="finish",
    )(place[1], owned, side, swap(lent, 1), side1)


def solution(mesh):
    axes = mesh.devices.reshape(mesh.shape["tm"], mesh.shape["chan"] // 2, 2)
    mesh = jax.sharding.Mesh(axes, ("tm", "x", "core"))
    chan = ("x", "core")
    placed = (
        P("tm", chan),
        P("tm", chan),
        P("tm", chan),
        P(None, chan),
        P(),
        P(chan),
        P("tm"),
        P(chan),
        P(),
        P(None, chan),
        P(None, chan),
        P(chan, None),
    )
    return jax.shard_map(
        shards, mesh=mesh, in_specs=placed, out_specs=P("tm", chan), check_vma=False
    )
```

```python
import functools

import jax
import jax.numpy as jnp
import numpy as np
from jax import lax
from jax.experimental import pallas as pl
from jax.experimental.pallas import tpu as pltpu
from jax.sharding import PartitionSpec as P

FLAGBLK = 64
bf16 = jnp.bfloat16
f32 = jnp.float32


def split_table(table):
    high = table.astype(bf16)
    low = (table - high.astype(np.float64)).astype(bf16)
    return high, low


def block_tables(block):
    freq = np.concatenate([np.arange(0, block, 2), np.arange(1, block, 2)])
    time = np.arange(block)
    turn = np.pi * ((2 * freq[None, :] + 1) * time[:, None] % (4 * block)) / (2 * block)
    forward = np.concatenate([np.cos(turn), -np.sin(turn)], axis=1)
    turn = np.pi * ((2 * freq[:, None] + 1) * (block + time[None, :]) % (4 * block)) / (2 * block)
    inverse = np.concatenate([np.cos(turn), -np.sin(turn)], axis=0) / block
    return split_table(forward) + split_table(inverse)


def dot(left, right):
    return jnp.dot(left, right, preferred_element_type=f32)


def start_loads(pairs, sems):
    loads = [
        pltpu.make_async_copy(src, dst, sems.at[at]) for at, (src, dst) in enumerate(pairs)
    ]
    for load in loads:
        load.start()
    return loads


def prepare_kernel(
    step_ref,
    flags_hbm,
    value_hbm,
    filter_hbm,
    table_hbm,
    mask_hbm,
    out_hbm,
    flags_ref,
    value_ref,
    filter_ref,
    table_ref,
    mask_ref,
    out_ref,
    sems,
    out_sems,
):
    loads = start_loads(
        (
            (filter_hbm, filter_ref),
            (value_hbm, value_ref),
            (flags_hbm, flags_ref),
            (table_hbm, table_ref),
            (mask_hbm, mask_ref),
        ),
        sems,
    )
    rows, width = value_ref.shape
    groups = out_ref.shape[0]
    lanes = 128
    stores = []

    def store(which, low, values):
        share = groups * lanes // width
        first = groups * low // width
        part = out_ref.at[pl.ds(first, share), which]
        part[...] = values.T.reshape(part.shape)
        copy = pltpu.make_async_copy(
            part, out_hbm.at[pl.ds(first, share), which], out_sems.at[len(stores)]
        )
        copy.start()
        stores.append(copy)

    steps = width // lanes if groups * lanes % width == 0 else 1
    lanes = width // steps
    loads[0].wait()
    for low in range(0, width, lanes):
        store(1, low, filter_ref[:, low : low + lanes])
    for load in loads[1:]:
        load.wait()
    embed = table_ref[pl.ds(step_ref[0], 1), :]
    mask = mask_ref[...]
    for low in range(0, width, lanes):
        here = slice(low, low + lanes)
        parts = []
        for at in range(rows // FLAGBLK):
            values = value_ref[at * FLAGBLK : (at + 1) * FLAGBLK, here].astype(f32)
            flag = flags_ref[at].astype(f32)
            parts.append((values + embed[:, here] + flag * mask[:, here]).astype(bf16))
        store(0, low, jnp.concatenate(parts, axis=0))
    for copy in stores:
        copy.wait()


def convolve_kernel(
    core_ref,
    both_ref,
    fh_ref,
    fl_ref,
    gh_hbm,
    gl_hbm,
    skip_ref,
    out_ref,
    x_ref,
    h_ref,
    z_ref,
    gh_ref,
    gl_ref,
    sems,
):
    loads = start_loads(((gh_hbm, gh_ref), (gl_hbm, gl_ref)), sems)
    tm, _, chans, rows = both_ref.shape
    block = rows // 2
    half = block // 2
    nb = 2 * tm
    for which, dst in ((0, x_ref), (1, h_ref)):
        for part in range(2):
            data = both_ref[:, which, :, part * block : (part + 1) * block]
            data = data.reshape(tm * chans, block)
            spec = dot(data, fh_ref[...]) + dot(data, fl_ref[...])
            dst[:, part] = spec.reshape(tm, chans, 2 * block)

    def read(ref, at, sub, lanes):
        return ref[at // 2, at % 2, sub, lanes]

    def window(prev_re, prev_im, cur_re, cur_im, odd):
        if odd:
            return prev_re - cur_im, prev_im + cur_re
        return prev_re + cur_im, prev_im - cur_re

    def tile(step, carry):
        sub = pl.ds(pl.multiple_of(step * 8, 8), 8)
        width = min(128, half)
        for odd in range(2):
            for low in range(odd * half, (odd + 1) * half, width):
                re = slice(low, low + width)
                im = slice(block + low, block + low + width)
                zero = jnp.zeros((8, width), f32)

                def put(a, acc):
                    z_ref[a // 2, a % 2, sub, re] = acc[0] - acc[1]
                    z_ref[a // 2, a % 2, sub, im] = acc[2] - acc[0] - acc[1]

                def load(at):
                    xr, xi = read(x_ref, at, sub, re), read(x_ref, at, sub, im)
                    return xr, xi, xr + xi

                if nb <= 16:
                    taps = []
                    prev = (zero, zero)
                    for d in range(nb):
                        cur = read(h_ref, d, sub, re), read(h_ref, d, sub, im)
                        wr, wi = window(*prev, *cur, odd)
                        taps.append((wr, wi, wr + wi))
                        prev = cur
                    values = [load(at) for at in range(nb)]
                    for a in range(nb):
                        acc = None
                        for d in range(a + 1):
                            terms = [v * t for v, t in zip(values[a - d], taps[d])]
                            acc = terms if acc is None else [p + q for p, q in zip(acc, terms)]
                        put(a, acc)
                else:

                    def out_block(a, carry):
                        def pair(d, acc):
                            before = jnp.maximum(d - 1, 0)
                            keep = (d > 0).astype(f32)
                            wr, wi = window(
                                keep * read(h_ref, before, sub, re),
                                keep * read(h_ref, before, sub, im),
                                read(h_ref, d, sub, re),
                                read(h_ref, d, sub, im),
                                odd,
                            )
                            terms = zip(acc, load(a - d), (wr, wi, wr + wi))
                            return tuple(p + v * t for p, v, t in terms)

                        put(a, lax.fori_loop(0, a + 1, pair, (zero, zero, zero)))
                        return carry

                    lax.fori_loop(0, nb, out_block, 0)
        return carry

    lax.fori_loop(0, chans // 8, tile, 0)
    for load in loads:
        load.wait()
    skip = skip_ref[...]
    for part in range(2):
        spec = z_ref[:, part].reshape(tm * chans, 2 * block)
        high = spec.astype(bf16)
        low = (spec - high.astype(f32)).astype(bf16)
        conv = dot(high, gh_ref[...]) + dot(low, gh_ref[...]) + dot(high, gl_ref[...])
        inputs = both_ref[:, 0, :, part * block : (part + 1) * block].astype(f32)
        total = conv.reshape(tm, chans, block) + skip[None] * inputs
        out_ref[:, part ^ core_ref[0]] = total.astype(bf16)


def mix(conv_refs, gate_refs, ats, mixed_ref, ready_ref, gain_ref, square):
    rows, width = gate_refs[0].shape
    for j, (conv_ref, gate_ref, at) in enumerate(zip(conv_refs, gate_refs, ats)):
        conv = conv_ref[...].reshape(width, rows).T.astype(f32)
        mixed = (gate_ref[...].astype(f32) * conv).astype(bf16)
        if j == 0 and mixed_ref is not None:
            mixed_ref[...] = mixed
        wide = mixed.astype(f32)
        square = square + jnp.sum(wide * wide, axis=-1, keepdims=True)
        ready_ref[:, j * width : (j + 1) * width] = (wide * gain_ref[at]).astype(bf16)
    return square


def feed_first_kernel(
    chip_ref,
    core_ref,
    conv0_ref,
    gate0_ref,
    gain_hbm,
    wg0_hbm,
    wu0_hbm,
    wg1_hbm,
    wu1_hbm,
    wd0_hbm,
    wd1_hbm,
    mixed_ref,
    square_ref,
    gain_ref,
    sums_ref,
    straight_ref,
    rest_ref,
    down_ref,
    ready_ref,
    now_ref,
    sems,
):
    here = 2 * chip_ref[0] + core_ref[0]
    rows, width = gate0_ref.shape
    hidden = wd0_hbm.shape[0]
    weights = (wg0_hbm, wu0_hbm, wg1_hbm, wu1_hbm)

    def source(weight, j):
        return weight.at[pl.ds(pl.multiple_of((here ^ j) * width, width), width)]

    loads = start_loads(
        [(gain_hbm, gain_ref)]
        + [(source(weight, 0), now_ref.at[at]) for at, weight in enumerate(weights)]
        + [(source(weight, 2), straight_ref.at[at]) for at, weight in enumerate(weights)]
        + [
            (source(weight, j), rest_ref.at[at, pl.ds(first, width)])
            for j, first in ((1, 0), (3, width))
            for at, weight in enumerate(weights)
        ]
        + [
            (weight, down_ref.at[pl.ds(at * hidden, hidden)])
            for at, weight in enumerate((wd0_hbm, wd1_hbm))
        ],
        sems,
    )
    loads[0].wait()
    square_ref[...] = mix(
        (conv0_ref,),
        (gate0_ref,),
        (here,),
        mixed_ref,
        ready_ref,
        gain_ref,
        jnp.zeros((rows, 1), f32),
    )
    ready = ready_ref[...]
    for at in range(4):
        loads[1 + at].wait()
        sums_ref[at] = dot(ready, now_ref[at])
    for load in loads[5:]:
        load.wait()


def feed_middle_kernel(
    chip_ref,
    core_ref,
    conv2_ref,
    gate2_ref,
    square_ref,
    gain_ref,
    sums_ref,
    straight_ref,
    square_out_ref,
    sums_out_ref,
    ready_ref,
):
    here = 2 * chip_ref[0] + core_ref[0]
    square_out_ref[...] = mix(
        (conv2_ref,), (gate2_ref,), (here ^ 2,), None, ready_ref, gain_ref, square_ref[...]
    )
    ready = ready_ref[...]
    for at in range(4):
        sums_out_ref[at] = sums_ref[at] + dot(ready, straight_ref[at])


def feed_second_kernel(
    chip_ref,
    core_ref,
    conv1_ref,
    conv3_ref,
    gate1_ref,
    gate3_ref,
    square_ref,
    gain_ref,
    sums_ref,
    rest_ref,
    down_ref,
    mixed_ref,
    hidden_ref,
    out2_ref,
    out3_ref,
    ready_ref,
):
    here = 2 * chip_ref[0] + core_ref[0]
    width = gate1_ref.shape[1]
    square = mix(
        (conv1_ref, conv3_ref),
        (gate1_ref, gate3_ref),
        (here ^ 1, here ^ 3),
        mixed_ref,
        ready_ref,
        gain_ref,
        square_ref[...],
    )
    scale = lax.rsqrt(square / (gain_ref.shape[0] * width) + 1e-06)
    ready = ready_ref[...]
    parts = []
    for at in range(2):
        gate = scale * (sums_ref[2 * at] + dot(ready, rest_ref[2 * at]))
        up = scale * (sums_ref[2 * at + 1] + dot(ready, rest_ref[2 * at + 1]))
        parts.append((gate / (1.0 + jnp.exp(-gate)) * up).astype(bf16))
    hidden = jnp.concatenate(parts, axis=1)
    hidden_ref[...] = hidden
    for j, out_ref in ((2, out2_ref), (3, out3_ref)):
        out_ref[...] = piece(hidden, down_ref, here ^ j, width).astype(bf16)


def piece(hidden, down_ref, at, width):
    return dot(hidden, down_ref[:, pl.ds(pl.multiple_of(at * width, width), width)])


def feed_third_kernel(
    chip_ref, core_ref, hidden_ref, down_ref, mixed0_ref, mixed1_ref, out0_ref, out1_ref
):
    here = 2 * chip_ref[0] + core_ref[0]
    width = out0_ref.shape[1]
    hidden = hidden_ref[...]
    for j, mixed_ref, out_ref in ((1, mixed1_ref, out1_ref), (0, mixed0_ref, out0_ref)):
        part = piece(hidden, down_ref, here ^ j, width) + mixed_ref[...].astype(f32)
        out_ref[...] = part.astype(out_ref.dtype)


def finish_kernel(core_ref, own_ref, side_ref, core1_ref, side1_ref, out_ref):
    block = own_ref.shape[0]
    same = pl.ds(pl.multiple_of(core_ref[0] * block, block), block)
    other = pl.ds(pl.multiple_of((1 - core_ref[0]) * block, block), block)
    out_ref[same, :] = (own_ref[...] + side_ref[...].astype(f32)).astype(bf16)
    out_ref[other, :] = (core1_ref[...].astype(f32) + side1_ref[...].astype(f32)).astype(bf16)


VMEM = pltpu.MemorySpace.VMEM
SMEM = pltpu.MemorySpace.SMEM
HBM = pltpu.MemorySpace.HBM


def whole(space=VMEM):
    return pl.BlockSpec(memory_space=space)


def stay(array):
    return pltpu.with_memory_space_constraint(array, HBM)


def params(mib):
    return pltpu.CompilerParams(vmem_limit_bytes=mib << 20)


def shards(
    series_value,
    series_gate,
    long_filter,
    step_table,
    diffusion_step,
    mask_embed,
    block_flags,
    skip_gain,
    norm_gain,
    w_gate,
    w_up,
    w_down,
):
    tm = lax.axis_size("tm")
    chip, core = lax.axis_index("x"), lax.axis_index("core")
    place = chip.reshape(1).astype(jnp.int32), core.reshape(1).astype(jnp.int32)
    rows, width = series_value.shape
    own = width // tm
    block = rows // 2

    def swap(values, bits):
        return lax.ppermute(values, ("x", "core"), [(at, at ^ bits) for at in range(4)])

    direct = own % 16 == 0
    shape = (tm, 2, own, rows) if direct else (1, 2, width, rows)
    made = pl.pallas_call(
        prepare_kernel,
        out_shape=jax.ShapeDtypeStruct(shape, bf16),
        in_specs=[whole(SMEM)] + [whole(HBM)] * 5,
        out_specs=whole(HBM),
        scratch_shapes=[
            pltpu.SMEM(block_flags.shape, jnp.int32),
            pltpu.VMEM(series_value.shape, bf16),
            pltpu.VMEM(long_filter.shape, bf16),
            pltpu.VMEM(step_table.shape, f32),
            pltpu.VMEM((1, width), f32),
            pltpu.VMEM(shape, bf16),
            pltpu.SemaphoreType.DMA((5,)),
            pltpu.SemaphoreType.DMA((2 * max(1, width // 128),)),
        ],
        compiler_params=params(32),
        name="prepare",
    )(
        diffusion_step,
        *map(stay, (block_flags, series_value, long_filter, step_table)),
        stay(mask_embed.reshape(1, width)),
    )
    if not direct:
        made = made.reshape(2, tm, own, rows).transpose(1, 0, 2, 3)
    both = lax.all_to_all(made, "tm", split_axis=0, concat_axis=0, tiled=True)

    gate_own = lax.dynamic_slice_in_dim(series_gate, core * block, block, 0)
    gate_other = lax.dynamic_slice_in_dim(series_gate, (1 - core) * block, block, 0)
    gates = (gate_own, swap(gate_other, 1), swap(gate_own, 2), swap(gate_other, 3))
    wg1, wu1, wd1 = swap(w_gate, 1), swap(w_up, 1), swap(w_down, 1)

    skip = lax.dynamic_slice_in_dim(skip_gain, lax.axis_index("tm") * own, own, 0)
    skip = skip.reshape(own, 1)
    held = own
    if not direct:
        held = -(-own // 16) * 16
        both = jnp.pad(both, ((0, 0), (0, 0), (0, held - own), (0, 0)))
        skip = jnp.pad(skip, ((0, held - own), (0, 0)))
    both, gates = lax.optimization_barrier((both, gates))
    tables = [jnp.asarray(table) for table in block_tables(block)]
    tables = tables[:2] + [stay(table) for table in tables[2:]]
    conv = pl.pallas_call(
        convolve_kernel,
        out_shape=jax.ShapeDtypeStruct((tm, 2, held, block), bf16),
        in_specs=[whole(SMEM)] + [whole()] * 3 + [whole(HBM)] * 2 + [whole()],
        out_specs=whole(),
        scratch_shapes=[pltpu.VMEM((tm, 2, held, 2 * block), f32)] * 3
        + [pltpu.VMEM(table.shape, bf16) for table in tables[2:]]
        + [pltpu.SemaphoreType.DMA((2,))],
        compiler_params=params(24),
        name="convolve",
    )(place[1], both, *tables, skip)
    if not direct:
        conv = conv[:, :, :own]

    conv = lax.all_to_all(conv, "tm", split_axis=0, concat_axis=0, tiled=True)
    mine, theirs = conv[:, 0], conv[:, 1]
    aside, across = swap(mine, 2), swap(theirs, 3)

    def view(values):
        return values if direct else values.reshape(1, width, block)

    gain = norm_gain.reshape(4, 1, width)
    held = [
        ((block, width), bf16),
        ((block, 1), f32),
        ((4, 1, width), f32),
        ((4, block, w_gate.shape[1]), f32),
        ((4, width, w_gate.shape[1]), bf16),
        ((4, 2 * width, w_gate.shape[1]), bf16),
        ((2 * w_down.shape[0], w_down.shape[1]), bf16),
    ]
    kept = pl.pallas_call(
        feed_first_kernel,
        out_shape=[jax.ShapeDtypeStruct(*spec) for spec in held],
        in_specs=[whole(SMEM)] * 2 + [whole()] * 2 + [whole(HBM)] * 7,
        out_specs=[whole()] * 7,
        scratch_shapes=[
            pltpu.VMEM((block, width), bf16),
            pltpu.VMEM((4, width, w_gate.shape[1]), bf16),
            pltpu.SemaphoreType.DMA((19,)),
        ],
        compiler_params=params(24),
        name="feed_first",
    )(
        *place,
        view(mine),
        gates[0],
        *map(stay, (gain, w_gate, w_up, wg1, wu1, w_down, wd1)),
    )
    theirs, aside, kept = lax.optimization_barrier((theirs, aside, kept))
    beside = swap(theirs, 1)
    mixed0, square, gain, sums, straight, rest, down = kept
    square, sums = pl.pallas_call(
        feed_middle_kernel,
        out_shape=[jax.ShapeDtypeStruct(*held[1]), jax.ShapeDtypeStruct(*held[3])],
        in_specs=[whole(SMEM)] * 2 + [whole()] * 6,
        out_specs=[whole()] * 2,
        scratch_shapes=[pltpu.VMEM((block, width), bf16)],
        compiler_params=params(24),
        name="feed_middle",
    )(*place, view(aside), gates[2], square, gain, sums, straight)
    shape = jax.ShapeDtypeStruct((block, width), bf16)
    mixed1, hidden, *remote = pl.pallas_call(
        feed_second_kernel,
        out_shape=[shape, jax.ShapeDtypeStruct((block, 2 * w_gate.shape[1]), bf16), shape, shape],
        in_specs=[whole(SMEM)] * 2 + [whole()] * 9,
        out_specs=[whole()] * 4,
        scratch_shapes=[pltpu.VMEM((block, 2 * width), bf16)],
        compiler_params=params(24),
        name="feed_second",
    )(
        *place,
        view(beside),
        view(across),
        gates[1],
        gates[3],
        square,
        gain,
        sums,
        rest,
        down,
    )
    side, side1 = swap(remote[0], 2), swap(remote[1], 3)
    local = pl.pallas_call(
        feed_third_kernel,
        out_shape=[jax.ShapeDtypeStruct((block, width), f32), shape],
        in_specs=[whole(SMEM)] * 2 + [whole()] * 4,
        out_specs=[whole()] * 2,
        compiler_params=params(16),
        name="feed_third",
    )(*place, hidden, down, mixed0, mixed1)
    owned, lent = local
    lent, side = lax.optimization_barrier((lent, side))
    return pl.pallas_call(
        finish_kernel,
        out_shape=jax.ShapeDtypeStruct((rows, width), bf16),
        in_specs=[whole(SMEM)] + [whole()] * 4,
        out_specs=whole(),
        compiler_params=params(8),
        name="finish",
    )(place[1], owned, side, swap(lent, 1), side1)


def solution(mesh):
    axes = mesh.devices.reshape(mesh.shape["tm"], mesh.shape["chan"] // 2, 2)
    mesh = jax.sharding.Mesh(axes, ("tm", "x", "core"))
    chan = ("x", "core")
    placed = (
        P("tm", chan),
        P("tm", chan),
        P("tm", chan),
        P(None, chan),
        P(),
        P(chan),
        P("tm"),
        P(chan),
        P(),
        P(None, chan),
        P(None, chan),
        P(chan, None),
    )
    return jax.shard_map(
        shards, mesh=mesh, in_specs=placed, out_specs=P("tm", chan), check_vma=False
    )
```

```python
import functools

import jax
import jax.numpy as jnp
import numpy as np
from jax import lax
from jax.experimental import pallas as pl
from jax.experimental.pallas import tpu as pltpu
from jax.sharding import PartitionSpec as P

FLAGBLK = 64
bf16 = jnp.bfloat16
f32 = jnp.float32


def split_table(table):
    high = table.astype(bf16)
    low = (table - high.astype(np.float64)).astype(bf16)
    return high, low


def block_tables(block):
    freq = np.concatenate([np.arange(0, block, 2), np.arange(1, block, 2)])
    time = np.arange(block)
    turn = np.pi * ((2 * freq[None, :] + 1) * time[:, None] % (4 * block)) / (2 * block)
    forward = np.concatenate([np.cos(turn), -np.sin(turn)], axis=1)
    turn = np.pi * ((2 * freq[:, None] + 1) * (block + time[None, :]) % (4 * block)) / (2 * block)
    inverse = np.concatenate([np.cos(turn), -np.sin(turn)], axis=0) / block
    return split_table(forward) + split_table(inverse)


def dot(left, right):
    return jnp.dot(left, right, preferred_element_type=f32)


def start_loads(pairs, sems):
    loads = [
        pltpu.make_async_copy(src, dst, sems.at[at]) for at, (src, dst) in enumerate(pairs)
    ]
    for load in loads:
        load.start()
    return loads


def prepare_kernel(
    step_ref,
    flags_hbm,
    value_hbm,
    filter_hbm,
    table_hbm,
    mask_hbm,
    out_hbm,
    flags_ref,
    value_ref,
    filter_ref,
    table_ref,
    mask_ref,
    out_ref,
    sems,
    out_sems,
):
    loads = start_loads(
        (
            (filter_hbm, filter_ref),
            (value_hbm, value_ref),
            (flags_hbm, flags_ref),
            (table_hbm, table_ref),
            (mask_hbm, mask_ref),
        ),
        sems,
    )
    rows, width = value_ref.shape
    groups = out_ref.shape[0]
    lanes = 128
    stores = []

    def store(which, low, values):
        share = groups * lanes // width
        first = groups * low // width
        part = out_ref.at[pl.ds(first, share), which]
        part[...] = values.T.reshape(part.shape)
        copy = pltpu.make_async_copy(
            part, out_hbm.at[pl.ds(first, share), which], out_sems.at[len(stores)]
        )
        copy.start()
        stores.append(copy)

    steps = width // lanes if groups * lanes % width == 0 else 1
    lanes = width // steps
    loads[0].wait()
    for low in range(0, width, lanes):
        store(1, low, filter_ref[:, low : low + lanes])
    for load in loads[1:]:
        load.wait()
    embed = table_ref[pl.ds(step_ref[0], 1), :]
    mask = mask_ref[...]
    for low in range(0, width, lanes):
        here = slice(low, low + lanes)
        parts = []
        for at in range(rows // FLAGBLK):
            values = value_ref[at * FLAGBLK : (at + 1) * FLAGBLK, here].astype(f32)
            flag = flags_ref[at].astype(f32)
            parts.append((values + embed[:, here] + flag * mask[:, here]).astype(bf16))
        store(0, low, jnp.concatenate(parts, axis=0))
    for copy in stores:
        copy.wait()


def convolve_kernel(
    core_ref,
    both_ref,
    fh_ref,
    fl_ref,
    gh_hbm,
    gl_hbm,
    skip_ref,
    out_ref,
    x_ref,
    h_ref,
    z_ref,
    gh_ref,
    gl_ref,
    sems,
):
    loads = start_loads(((gh_hbm, gh_ref), (gl_hbm, gl_ref)), sems)
    tm, _, chans, rows = both_ref.shape
    block = rows // 2
    half = block // 2
    nb = 2 * tm
    for which, dst in ((0, x_ref), (1, h_ref)):
        for part in range(2):
            data = both_ref[:, which, :, part * block : (part + 1) * block]
            data = data.reshape(tm * chans, block)
            spec = dot(data, fh_ref[...]) + dot(data, fl_ref[...])
            dst[:, part] = spec.reshape(tm, chans, 2 * block)

    def read(ref, at, sub, lanes):
        return ref[at // 2, at % 2, sub, lanes]

    def window(prev_re, prev_im, cur_re, cur_im, odd):
        if odd:
            return prev_re - cur_im, prev_im + cur_re
        return prev_re + cur_im, prev_im - cur_re

    def tile(step, carry):
        sub = pl.ds(pl.multiple_of(step * 8, 8), 8)
        width = min(128, half)
        for odd in range(2):
            for low in range(odd * half, (odd + 1) * half, width):
                re = slice(low, low + width)
                im = slice(block + low, block + low + width)
                zero = jnp.zeros((8, width), f32)

                def put(a, acc):
                    z_ref[a // 2, a % 2, sub, re] = acc[0] - acc[1]
                    z_ref[a // 2, a % 2, sub, im] = acc[2] - acc[0] - acc[1]

                def load(at):
                    xr, xi = read(x_ref, at, sub, re), read(x_ref, at, sub, im)
                    return xr, xi, xr + xi

                if nb <= 16:
                    taps = []
                    prev = (zero, zero)
                    for d in range(nb):
                        cur = read(h_ref, d, sub, re), read(h_ref, d, sub, im)
                        wr, wi = window(*prev, *cur, odd)
                        taps.append((wr, wi, wr + wi))
                        prev = cur
                    values = [load(at) for at in range(nb)]
                    for a in range(nb):
                        acc = None
                        for d in range(a + 1):
                            terms = [v * t for v, t in zip(values[a - d], taps[d])]
                            acc = terms if acc is None else [p + q for p, q in zip(acc, terms)]
                        put(a, acc)
                else:

                    def out_block(a, carry):
                        def pair(d, acc):
                            before = jnp.maximum(d - 1, 0)
                            keep = (d > 0).astype(f32)
                            wr, wi = window(
                                keep * read(h_ref, before, sub, re),
                                keep * read(h_ref, before, sub, im),
                                read(h_ref, d, sub, re),
                                read(h_ref, d, sub, im),
                                odd,
                            )
                            terms = zip(acc, load(a - d), (wr, wi, wr + wi))
                            return tuple(p + v * t for p, v, t in terms)

                        put(a, lax.fori_loop(0, a + 1, pair, (zero, zero, zero)))
                        return carry

                    lax.fori_loop(0, nb, out_block, 0)
        return carry

    lax.fori_loop(0, chans // 8, tile, 0)
    for load in loads:
        load.wait()
    skip = skip_ref[...]
    for part in range(2):
        spec = z_ref[:, part].reshape(tm * chans, 2 * block)
        high = spec.astype(bf16)
        low = (spec - high.astype(f32)).astype(bf16)
        conv = dot(high, gh_ref[...]) + dot(low, gh_ref[...]) + dot(high, gl_ref[...])
        inputs = both_ref[:, 0, :, part * block : (part + 1) * block].astype(f32)
        total = conv.reshape(tm, chans, block) + skip[None] * inputs
        out_ref[:, part ^ core_ref[0]] = total.astype(bf16)


def mix(conv_refs, gate_refs, ats, mixed_ref, ready_ref, gain_ref, square):
    rows, width = gate_refs[0].shape
    for j, (conv_ref, gate_ref, at) in enumerate(zip(conv_refs, gate_refs, ats)):
        conv = conv_ref[...].reshape(width, rows).T.astype(f32)
        mixed = (gate_ref[...].astype(f32) * conv).astype(bf16)
        if j == 0 and mixed_ref is not None:
            mixed_ref[...] = mixed
        wide = mixed.astype(f32)
        square = square + jnp.sum(wide * wide, axis=-1, keepdims=True)
        ready_ref[:, j * width : (j + 1) * width] = (wide * gain_ref[at]).astype(bf16)
    return square


def feed_first_kernel(
    chip_ref,
    core_ref,
    conv0_ref,
    gate0_ref,
    gain_hbm,
    wg0_hbm,
    wu0_hbm,
    wg1_hbm,
    wu1_hbm,
    wd0_hbm,
    wd1_hbm,
    mixed_ref,
    square_ref,
    gain_ref,
    sums_ref,
    straight_ref,
    rest_ref,
    down_ref,
    ready_ref,
    now_ref,
    sems,
):
    here = 2 * chip_ref[0] + core_ref[0]
    rows, width = gate0_ref.shape
    hidden = wd0_hbm.shape[0]
    weights = (wg0_hbm, wu0_hbm, wg1_hbm, wu1_hbm)

    def source(weight, j):
        return weight.at[pl.ds(pl.multiple_of((here ^ j) * width, width), width)]

    loads = start_loads(
        [(gain_hbm, gain_ref)]
        + [(source(weight, 0), now_ref.at[at]) for at, weight in enumerate(weights)]
        + [(source(weight, 2), straight_ref.at[at]) for at, weight in enumerate(weights)]
        + [
            (source(weight, j), rest_ref.at[at, pl.ds(first, width)])
            for j, first in ((1, 0), (3, width))
            for at, weight in enumerate(weights)
        ]
        + [
            (weight, down_ref.at[pl.ds(at * hidden, hidden)])
            for at, weight in enumerate((wd0_hbm, wd1_hbm))
        ],
        sems,
    )
    loads[0].wait()
    square_ref[...] = mix(
        (conv0_ref,),
        (gate0_ref,),
        (here,),
        mixed_ref,
        ready_ref,
        gain_ref,
        jnp.zeros((rows, 1), f32),
    )
    ready = ready_ref[...]
    for at in range(4):
        loads[1 + at].wait()
        sums_ref[at] = dot(ready, now_ref[at])
    for load in loads[5:]:
        load.wait()


def feed_middle_kernel(
    chip_ref,
    core_ref,
    conv2_ref,
    gate2_ref,
    square_ref,
    gain_ref,
    sums_ref,
    straight_ref,
    square_out_ref,
    sums_out_ref,
    ready_ref,
):
    here = 2 * chip_ref[0] + core_ref[0]
    square_out_ref[...] = mix(
        (conv2_ref,), (gate2_ref,), (here ^ 2,), None, ready_ref, gain_ref, square_ref[...]
    )
    ready = ready_ref[...]
    for at in range(4):
        sums_out_ref[at] = sums_ref[at] + dot(ready, straight_ref[at])


def feed_second_kernel(
    chip_ref,
    core_ref,
    conv1_ref,
    conv3_ref,
    gate1_ref,
    gate3_ref,
    square_ref,
    gain_ref,
    sums_ref,
    rest_ref,
    down_ref,
    mixed_ref,
    hidden_ref,
    out2_ref,
    out3_ref,
    ready_ref,
):
    here = 2 * chip_ref[0] + core_ref[0]
    width = gate1_ref.shape[1]
    square = mix(
        (conv1_ref, conv3_ref),
        (gate1_ref, gate3_ref),
        (here ^ 1, here ^ 3),
        mixed_ref,
        ready_ref,
        gain_ref,
        square_ref[...],
    )
    scale = lax.rsqrt(square / (gain_ref.shape[0] * width) + 1e-06)
    ready = ready_ref[...]
    parts = []
    for at in range(2):
        gate = scale * (sums_ref[2 * at] + dot(ready, rest_ref[2 * at]))
        up = scale * (sums_ref[2 * at + 1] + dot(ready, rest_ref[2 * at + 1]))
        parts.append((gate / (1.0 + jnp.exp(-gate)) * up).astype(bf16))
    hidden = jnp.concatenate(parts, axis=1)
    hidden_ref[...] = hidden
    for j, out_ref in ((2, out2_ref), (3, out3_ref)):
        out_ref[...] = piece(hidden, down_ref, here ^ j, width).astype(bf16)


def piece(hidden, down_ref, at, width):
    return dot(hidden, down_ref[:, pl.ds(pl.multiple_of(at * width, width), width)])


def feed_third_kernel(
    chip_ref, core_ref, hidden_ref, down_ref, mixed0_ref, mixed1_ref, out0_ref, out1_ref
):
    here = 2 * chip_ref[0] + core_ref[0]
    width = out0_ref.shape[1]
    hidden = hidden_ref[...]
    for j, mixed_ref, out_ref in ((1, mixed1_ref, out1_ref), (0, mixed0_ref, out0_ref)):
        part = piece(hidden, down_ref, here ^ j, width) + mixed_ref[...].astype(f32)
        out_ref[...] = part.astype(out_ref.dtype)


def finish_kernel(flip, core_ref, base_ref, add_ref, *rest):
    out_hbm, sum_ref, sem = rest[-3:]
    block = base_ref.shape[0]
    first = (core_ref[0] ^ flip) * block
    sum_ref[...] = (base_ref[...].astype(f32) + add_ref[...].astype(f32)).astype(bf16)
    store = pltpu.make_async_copy(
        sum_ref, out_hbm.at[pl.ds(pl.multiple_of(first, block), block)], sem
    )
    store.start()
    store.wait()


def finish(flip, core, base, add, *into):
    block, width = base.shape
    return pl.pallas_call(
        functools.partial(finish_kernel, flip),
        out_shape=jax.ShapeDtypeStruct((2 * block, width), bf16),
        in_specs=[whole(SMEM)] + [whole()] * 2 + [whole(HBM)] * len(into),
        out_specs=whole(HBM),
        scratch_shapes=[pltpu.VMEM((block, width), bf16), pltpu.SemaphoreType.DMA],
        input_output_aliases={3: 0} if into else {},
        compiler_params=params(8),
        name="finish",
    )(core, base, add, *into)


VMEM = pltpu.MemorySpace.VMEM
SMEM = pltpu.MemorySpace.SMEM
HBM = pltpu.MemorySpace.HBM


def whole(space=VMEM):
    return pl.BlockSpec(memory_space=space)


def stay(array):
    return pltpu.with_memory_space_constraint(array, HBM)


def params(mib):
    return pltpu.CompilerParams(vmem_limit_bytes=mib << 20)


def shards(
    series_value,
    series_gate,
    long_filter,
    step_table,
    diffusion_step,
    mask_embed,
    block_flags,
    skip_gain,
    norm_gain,
    w_gate,
    w_up,
    w_down,
):
    tm = lax.axis_size("tm")
    chip, core = lax.axis_index("x"), lax.axis_index("core")
    place = chip.reshape(1).astype(jnp.int32), core.reshape(1).astype(jnp.int32)
    rows, width = series_value.shape
    own = width // tm
    block = rows // 2

    def swap(values, bits):
        return lax.ppermute(values, ("x", "core"), [(at, at ^ bits) for at in range(4)])

    direct = own % 16 == 0
    shape = (tm, 2, own, rows) if direct else (1, 2, width, rows)
    made = pl.pallas_call(
        prepare_kernel,
        out_shape=jax.ShapeDtypeStruct(shape, bf16),
        in_specs=[whole(SMEM)] + [whole(HBM)] * 5,
        out_specs=whole(HBM),
        scratch_shapes=[
            pltpu.SMEM(block_flags.shape, jnp.int32),
            pltpu.VMEM(series_value.shape, bf16),
            pltpu.VMEM(long_filter.shape, bf16),
            pltpu.VMEM(step_table.shape, f32),
            pltpu.VMEM((1, width), f32),
            pltpu.VMEM(shape, bf16),
            pltpu.SemaphoreType.DMA((5,)),
            pltpu.SemaphoreType.DMA((2 * max(1, width // 128),)),
        ],
        compiler_params=params(32),
        name="prepare",
    )(
        diffusion_step,
        *map(stay, (block_flags, series_value, long_filter, step_table)),
        stay(mask_embed.reshape(1, width)),
    )
    if not direct:
        made = made.reshape(2, tm, own, rows).transpose(1, 0, 2, 3)
    both = lax.all_to_all(made, "tm", split_axis=0, concat_axis=0, tiled=True)

    gate_own = lax.dynamic_slice_in_dim(series_gate, core * block, block, 0)
    gate_other = lax.dynamic_slice_in_dim(series_gate, (1 - core) * block, block, 0)
    gates = (gate_own, swap(gate_other, 1), swap(gate_own, 2), swap(gate_other, 3))
    wg1, wu1, wd1 = swap(w_gate, 1), swap(w_up, 1), swap(w_down, 1)

    skip = lax.dynamic_slice_in_dim(skip_gain, lax.axis_index("tm") * own, own, 0)
    skip = skip.reshape(own, 1)
    held = own
    if not direct:
        held = -(-own // 16) * 16
        both = jnp.pad(both, ((0, 0), (0, 0), (0, held - own), (0, 0)))
        skip = jnp.pad(skip, ((0, held - own), (0, 0)))
    both, gates = lax.optimization_barrier((both, gates))
    tables = [jnp.asarray(table) for table in block_tables(block)]
    tables = tables[:2] + [stay(table) for table in tables[2:]]
    conv = pl.pallas_call(
        convolve_kernel,
        out_shape=jax.ShapeDtypeStruct((tm, 2, held, block), bf16),
        in_specs=[whole(SMEM)] + [whole()] * 3 + [whole(HBM)] * 2 + [whole()],
        out_specs=whole(),
        scratch_shapes=[pltpu.VMEM((tm, 2, held, 2 * block), f32)] * 3
        + [pltpu.VMEM(table.shape, bf16) for table in tables[2:]]
        + [pltpu.SemaphoreType.DMA((2,))],
        compiler_params=params(24),
        name="convolve",
    )(place[1], both, *tables, skip)
    if not direct:
        conv = conv[:, :, :own]

    conv = lax.all_to_all(conv, "tm", split_axis=0, concat_axis=0, tiled=True)
    mine, theirs = conv[:, 0], conv[:, 1]
    aside, across = swap(mine, 2), swap(theirs, 3)

    def view(values):
        return values if direct else values.reshape(1, width, block)

    gain = norm_gain.reshape(4, 1, width)
    held = [
        ((block, width), bf16),
        ((block, 1), f32),
        ((4, 1, width), f32),
        ((4, block, w_gate.shape[1]), f32),
        ((4, width, w_gate.shape[1]), bf16),
        ((4, 2 * width, w_gate.shape[1]), bf16),
        ((2 * w_down.shape[0], w_down.shape[1]), bf16),
    ]
    kept = pl.pallas_call(
        feed_first_kernel,
        out_shape=[jax.ShapeDtypeStruct(*spec) for spec in held],
        in_specs=[whole(SMEM)] * 2 + [whole()] * 2 + [whole(HBM)] * 7,
        out_specs=[whole()] * 7,
        scratch_shapes=[
            pltpu.VMEM((block, width), bf16),
            pltpu.VMEM((4, width, w_gate.shape[1]), bf16),
            pltpu.SemaphoreType.DMA((19,)),
        ],
        compiler_params=params(24),
        name="feed_first",
    )(
        *place,
        view(mine),
        gates[0],
        *map(stay, (gain, w_gate, w_up, wg1, wu1, w_down, wd1)),
    )
    theirs, aside, kept = lax.optimization_barrier((theirs, aside, kept))
    beside = swap(theirs, 1)
    mixed0, square, gain, sums, straight, rest, down = kept
    square, sums = pl.pallas_call(
        feed_middle_kernel,
        out_shape=[jax.ShapeDtypeStruct(*held[1]), jax.ShapeDtypeStruct(*held[3])],
        in_specs=[whole(SMEM)] * 2 + [whole()] * 6,
        out_specs=[whole()] * 2,
        scratch_shapes=[pltpu.VMEM((block, width), bf16)],
        compiler_params=params(24),
        name="feed_middle",
    )(*place, view(aside), gates[2], square, gain, sums, straight)
    shape = jax.ShapeDtypeStruct((block, width), bf16)
    mixed1, hidden, *remote = pl.pallas_call(
        feed_second_kernel,
        out_shape=[shape, jax.ShapeDtypeStruct((block, 2 * w_gate.shape[1]), bf16), shape, shape],
        in_specs=[whole(SMEM)] * 2 + [whole()] * 9,
        out_specs=[whole()] * 4,
        scratch_shapes=[pltpu.VMEM((block, 2 * width), bf16)],
        compiler_params=params(24),
        name="feed_second",
    )(
        *place,
        view(beside),
        view(across),
        gates[1],
        gates[3],
        square,
        gain,
        sums,
        rest,
        down,
    )
    side, side1 = swap(remote[0], 2), swap(remote[1], 3)
    local = pl.pallas_call(
        feed_third_kernel,
        out_shape=[jax.ShapeDtypeStruct((block, width), f32), shape],
        in_specs=[whole(SMEM)] * 2 + [whole()] * 4,
        out_specs=[whole()] * 2,
        compiler_params=params(16),
        name="feed_third",
    )(*place, hidden, down, mixed0, mixed1)
    owned, lent = local
    lent, side = lax.optimization_barrier((lent, side))
    half = finish(0, place[1], owned, side)
    return finish(1, place[1], swap(lent, 1), side1, half)


def solution(mesh):
    axes = mesh.devices.reshape(mesh.shape["tm"], mesh.shape["chan"] // 2, 2)
    mesh = jax.sharding.Mesh(axes, ("tm", "x", "core"))
    chan = ("x", "core")
    placed = (
        P("tm", chan),
        P("tm", chan),
        P("tm", chan),
        P(None, chan),
        P(),
        P(chan),
        P("tm"),
        P(chan),
        P(),
        P(None, chan),
        P(None, chan),
        P(chan, None),
    )
    return jax.shard_map(
        shards, mesh=mesh, in_specs=placed, out_specs=P("tm", chan), check_vma=False
    )
```

```python
import functools

import jax
import jax.numpy as jnp
import numpy as np
from jax import lax
from jax.experimental import pallas as pl
from jax.experimental.pallas import tpu as pltpu
from jax.sharding import PartitionSpec as P

FLAGBLK = 64
bf16 = jnp.bfloat16
f32 = jnp.float32


def split_table(table):
    high = table.astype(bf16)
    low = (table - high.astype(np.float64)).astype(bf16)
    return high, low


def block_tables(block):
    freq = np.concatenate([np.arange(0, block, 2), np.arange(1, block, 2)])
    time = np.arange(block)
    turn = np.pi * ((2 * freq[None, :] + 1) * time[:, None] % (4 * block)) / (2 * block)
    forward = np.concatenate([np.cos(turn), -np.sin(turn)], axis=1)
    turn = np.pi * ((2 * freq[:, None] + 1) * (block + time[None, :]) % (4 * block)) / (2 * block)
    inverse = np.concatenate([np.cos(turn), -np.sin(turn)], axis=0) / block
    return split_table(forward) + split_table(inverse)


def dot(left, right):
    return jnp.dot(left, right, preferred_element_type=f32)


def start_loads(pairs, sems):
    loads = [
        pltpu.make_async_copy(src, dst, sems.at[at]) for at, (src, dst) in enumerate(pairs)
    ]
    for load in loads:
        load.start()
    return loads


def prepare_kernel(
    step_ref,
    flags_hbm,
    value_hbm,
    filter_hbm,
    table_hbm,
    mask_hbm,
    out_hbm,
    flags_ref,
    value_ref,
    filter_ref,
    table_ref,
    mask_ref,
    out_ref,
    sems,
    out_sems,
):
    loads = start_loads(
        (
            (filter_hbm, filter_ref),
            (value_hbm, value_ref),
            (flags_hbm, flags_ref),
            (table_hbm, table_ref),
            (mask_hbm, mask_ref),
        ),
        sems,
    )
    rows, width = value_ref.shape
    groups = out_ref.shape[0]
    lanes = 128
    stores = []

    def store(which, low, values):
        share = groups * lanes // width
        first = groups * low // width
        part = out_ref.at[pl.ds(first, share), which]
        part[...] = values.T.reshape(part.shape)
        copy = pltpu.make_async_copy(
            part, out_hbm.at[pl.ds(first, share), which], out_sems.at[len(stores)]
        )
        copy.start()
        stores.append(copy)

    steps = width // lanes if groups * lanes % width == 0 else 1
    lanes = width // steps
    loads[0].wait()
    for low in range(0, width, lanes):
        store(1, low, filter_ref[:, low : low + lanes])
    for load in loads[1:]:
        load.wait()
    embed = table_ref[pl.ds(step_ref[0], 1), :]
    mask = mask_ref[...]
    for low in range(0, width, lanes):
        here = slice(low, low + lanes)
        parts = []
        for at in range(rows // FLAGBLK):
            values = value_ref[at * FLAGBLK : (at + 1) * FLAGBLK, here].astype(f32)
            flag = flags_ref[at].astype(f32)
            parts.append((values + embed[:, here] + flag * mask[:, here]).astype(bf16))
        store(0, low, jnp.concatenate(parts, axis=0))
    for copy in stores:
        copy.wait()


def convolve_kernel(
    core_ref,
    both_ref,
    fh_ref,
    fl_ref,
    gh_hbm,
    gl_hbm,
    skip_ref,
    out_ref,
    x_ref,
    h_ref,
    z_ref,
    gh_ref,
    gl_ref,
    sems,
):
    loads = start_loads(((gh_hbm, gh_ref), (gl_hbm, gl_ref)), sems)
    tm, _, chans, rows = both_ref.shape
    block = rows // 2
    half = block // 2
    nb = 2 * tm
    for which, dst in ((0, x_ref), (1, h_ref)):
        for part in range(2):
            data = both_ref[:, which, :, part * block : (part + 1) * block]
            data = data.reshape(tm * chans, block)
            spec = dot(data, fh_ref[...]) + dot(data, fl_ref[...])
            dst[:, part] = spec.reshape(tm, chans, 2 * block)

    def read(ref, at, sub, lanes):
        return ref[at // 2, at % 2, sub, lanes]

    def window(prev_re, prev_im, cur_re, cur_im, odd):
        if odd:
            return prev_re - cur_im, prev_im + cur_re
        return prev_re + cur_im, prev_im - cur_re

    def tile(step, carry):
        sub = pl.ds(pl.multiple_of(step * 8, 8), 8)
        width = min(128, half)
        for odd in range(2):
            for low in range(odd * half, (odd + 1) * half, width):
                re = slice(low, low + width)
                im = slice(block + low, block + low + width)
                zero = jnp.zeros((8, width), f32)

                def put(a, acc):
                    z_ref[a // 2, a % 2, sub, re] = acc[0] - acc[1]
                    z_ref[a // 2, a % 2, sub, im] = acc[2] - acc[0] - acc[1]

                def load(at):
                    xr, xi = read(x_ref, at, sub, re), read(x_ref, at, sub, im)
                    return xr, xi, xr + xi

                if nb <= 16:
                    taps = []
                    prev = (zero, zero)
                    for d in range(nb):
                        cur = read(h_ref, d, sub, re), read(h_ref, d, sub, im)
                        wr, wi = window(*prev, *cur, odd)
                        taps.append((wr, wi, wr + wi))
                        prev = cur
                    values = [load(at) for at in range(nb)]
                    for a in range(nb):
                        acc = None
                        for d in range(a + 1):
                            terms = [v * t for v, t in zip(values[a - d], taps[d])]
                            acc = terms if acc is None else [p + q for p, q in zip(acc, terms)]
                        put(a, acc)
                else:

                    def out_block(a, carry):
                        def pair(d, acc):
                            before = jnp.maximum(d - 1, 0)
                            keep = (d > 0).astype(f32)
                            wr, wi = window(
                                keep * read(h_ref, before, sub, re),
                                keep * read(h_ref, before, sub, im),
                                read(h_ref, d, sub, re),
                                read(h_ref, d, sub, im),
                                odd,
                            )
                            terms = zip(acc, load(a - d), (wr, wi, wr + wi))
                            return tuple(p + v * t for p, v, t in terms)

                        put(a, lax.fori_loop(0, a + 1, pair, (zero, zero, zero)))
                        return carry

                    lax.fori_loop(0, nb, out_block, 0)
        return carry

    lax.fori_loop(0, chans // 8, tile, 0)
    for load in loads:
        load.wait()
    skip = skip_ref[...]
    for part in range(2):
        spec = z_ref[:, part].reshape(tm * chans, 2 * block)
        high = spec.astype(bf16)
        low = (spec - high.astype(f32)).astype(bf16)
        conv = dot(high, gh_ref[...]) + dot(low, gh_ref[...]) + dot(high, gl_ref[...])
        inputs = both_ref[:, 0, :, part * block : (part + 1) * block].astype(f32)
        total = conv.reshape(tm, chans, block) + skip[None] * inputs
        out_ref[:, part ^ core_ref[0]] = total.astype(bf16)


def mix(conv_refs, gate_refs, ats, mixed_ref, ready_ref, gain_ref, square):
    rows, width = gate_refs[0].shape
    for j, (conv_ref, gate_ref, at) in enumerate(zip(conv_refs, gate_refs, ats)):
        conv = conv_ref[...].reshape(width, rows).T.astype(f32)
        mixed = (gate_ref[...].astype(f32) * conv).astype(bf16)
        if j == 0 and mixed_ref is not None:
            mixed_ref[...] = mixed
        wide = mixed.astype(f32)
        square = square + jnp.sum(wide * wide, axis=-1, keepdims=True)
        ready_ref[:, j * width : (j + 1) * width] = (wide * gain_ref[at]).astype(bf16)
    return square


def feed_first_kernel(
    chip_ref,
    core_ref,
    conv0_ref,
    gate0_ref,
    gain_hbm,
    wg0_hbm,
    wu0_hbm,
    wg1_hbm,
    wu1_hbm,
    wd0_hbm,
    wd1_hbm,
    mixed_ref,
    square_ref,
    gain_ref,
    sums_ref,
    straight_ref,
    rest_ref,
    down_ref,
    ready_ref,
    now_ref,
    sems,
):
    here = 2 * chip_ref[0] + core_ref[0]
    rows, width = gate0_ref.shape
    hidden = wd0_hbm.shape[0]
    weights = (wg0_hbm, wu0_hbm, wg1_hbm, wu1_hbm)

    def source(weight, j):
        return weight.at[pl.ds(pl.multiple_of((here ^ j) * width, width), width)]

    loads = start_loads(
        [(gain_hbm, gain_ref)]
        + [(source(weight, 0), now_ref.at[at]) for at, weight in enumerate(weights)]
        + [(source(weight, 2), straight_ref.at[at]) for at, weight in enumerate(weights)]
        + [
            (source(weight, j), rest_ref.at[at, pl.ds(first, width)])
            for j, first in ((1, 0), (3, width))
            for at, weight in enumerate(weights)
        ]
        + [
            (weight, down_ref.at[pl.ds(at * hidden, hidden)])
            for at, weight in enumerate((wd0_hbm, wd1_hbm))
        ],
        sems,
    )
    loads[0].wait()
    square_ref[...] = mix(
        (conv0_ref,),
        (gate0_ref,),
        (here,),
        mixed_ref,
        ready_ref,
        gain_ref,
        jnp.zeros((rows, 1), f32),
    )
    ready = ready_ref[...]
    for at in range(4):
        loads[1 + at].wait()
        sums_ref[at] = dot(ready, now_ref[at])
    for load in loads[5:]:
        load.wait()


def feed_middle_kernel(
    chip_ref,
    core_ref,
    conv2_ref,
    gate2_ref,
    square_ref,
    gain_ref,
    sums_ref,
    straight_ref,
    square_out_ref,
    sums_out_ref,
    ready_ref,
):
    here = 2 * chip_ref[0] + core_ref[0]
    square_out_ref[...] = mix(
        (conv2_ref,), (gate2_ref,), (here ^ 2,), None, ready_ref, gain_ref, square_ref[...]
    )
    ready = ready_ref[...]
    for at in range(4):
        sums_out_ref[at] = sums_ref[at] + dot(ready, straight_ref[at])


def feed_second_kernel(
    chip_ref,
    core_ref,
    conv1_ref,
    conv3_ref,
    gate1_ref,
    gate3_ref,
    square_ref,
    gain_ref,
    sums_ref,
    rest_ref,
    down_ref,
    mixed_ref,
    hidden_ref,
    out2_ref,
    out3_ref,
    ready_ref,
):
    here = 2 * chip_ref[0] + core_ref[0]
    width = gate1_ref.shape[1]
    square = mix(
        (conv1_ref, conv3_ref),
        (gate1_ref, gate3_ref),
        (here ^ 1, here ^ 3),
        mixed_ref,
        ready_ref,
        gain_ref,
        square_ref[...],
    )
    scale = lax.rsqrt(square / (gain_ref.shape[0] * width) + 1e-06)
    ready = ready_ref[...]
    parts = []
    for at in range(2):
        gate = scale * (sums_ref[2 * at] + dot(ready, rest_ref[2 * at]))
        up = scale * (sums_ref[2 * at + 1] + dot(ready, rest_ref[2 * at + 1]))
        parts.append((gate / (1.0 + jnp.exp(-gate)) * up).astype(bf16))
    size = parts[0].shape[1]
    for at, values in enumerate(parts):
        hidden_ref[:, at * size : (at + 1) * size] = values
    away = pl.ds(pl.multiple_of((1 - chip_ref[0]) * 2 * width, 2 * width), 2 * width)
    both = dot(parts[0], down_ref[:size, away]) + dot(parts[1], down_ref[size:, away])
    low, high = both[:, :width].astype(bf16), both[:, width:].astype(bf16)
    first = core_ref[0] == 0
    out2_ref[...] = jnp.where(first, low, high)
    out3_ref[...] = jnp.where(first, high, low)


def piece(hidden, down_ref, at, width):
    return dot(hidden, down_ref[:, pl.ds(pl.multiple_of(at * width, width), width)])


def feed_third_kernel(
    chip_ref, core_ref, hidden_ref, down_ref, mixed0_ref, mixed1_ref, out0_ref, out1_ref
):
    here = 2 * chip_ref[0] + core_ref[0]
    width = out0_ref.shape[1]
    hidden = hidden_ref[...]
    for j, mixed_ref, out_ref in ((1, mixed1_ref, out1_ref), (0, mixed0_ref, out0_ref)):
        part = piece(hidden, down_ref, here ^ j, width) + mixed_ref[...].astype(f32)
        out_ref[...] = part.astype(out_ref.dtype)


def finish_kernel(flip, core_ref, base_ref, add_ref, *rest):
    out_hbm, sum_ref, sem = rest[-3:]
    block = base_ref.shape[0]
    first = (core_ref[0] ^ flip) * block
    sum_ref[...] = (base_ref[...].astype(f32) + add_ref[...].astype(f32)).astype(bf16)
    store = pltpu.make_async_copy(
        sum_ref, out_hbm.at[pl.ds(pl.multiple_of(first, block), block)], sem
    )
    store.start()
    store.wait()


def finish(flip, core, base, add, *into):
    block, width = base.shape
    return pl.pallas_call(
        functools.partial(finish_kernel, flip),
        out_shape=jax.ShapeDtypeStruct((2 * block, width), bf16),
        in_specs=[whole(SMEM)] + [whole()] * 2 + [whole(HBM)] * len(into),
        out_specs=whole(HBM),
        scratch_shapes=[pltpu.VMEM((block, width), bf16), pltpu.SemaphoreType.DMA],
        input_output_aliases={3: 0} if into else {},
        compiler_params=params(8),
        name="finish",
    )(core, base, add, *into)


VMEM = pltpu.MemorySpace.VMEM
SMEM = pltpu.MemorySpace.SMEM
HBM = pltpu.MemorySpace.HBM


def whole(space=VMEM):
    return pl.BlockSpec(memory_space=space)


def stay(array):
    return pltpu.with_memory_space_constraint(array, HBM)


def params(mib):
    return pltpu.CompilerParams(vmem_limit_bytes=mib << 20)


def shards(
    series_value,
    series_gate,
    long_filter,
    step_table,
    diffusion_step,
    mask_embed,
    block_flags,
    skip_gain,
    norm_gain,
    w_gate,
    w_up,
    w_down,
):
    tm = lax.axis_size("tm")
    chip, core = lax.axis_index("x"), lax.axis_index("core")
    place = chip.reshape(1).astype(jnp.int32), core.reshape(1).astype(jnp.int32)
    rows, width = series_value.shape
    own = width // tm
    block = rows // 2

    def swap(values, bits):
        return lax.ppermute(values, ("x", "core"), [(at, at ^ bits) for at in range(4)])

    direct = own % 16 == 0
    shape = (tm, 2, own, rows) if direct else (1, 2, width, rows)
    made = pl.pallas_call(
        prepare_kernel,
        out_shape=jax.ShapeDtypeStruct(shape, bf16),
        in_specs=[whole(SMEM)] + [whole(HBM)] * 5,
        out_specs=whole(HBM),
        scratch_shapes=[
            pltpu.SMEM(block_flags.shape, jnp.int32),
            pltpu.VMEM(series_value.shape, bf16),
            pltpu.VMEM(long_filter.shape, bf16),
            pltpu.VMEM(step_table.shape, f32),
            pltpu.VMEM((1, width), f32),
            pltpu.VMEM(shape, bf16),
            pltpu.SemaphoreType.DMA((5,)),
            pltpu.SemaphoreType.DMA((2 * max(1, width // 128),)),
        ],
        compiler_params=params(32),
        name="prepare",
    )(
        diffusion_step,
        *map(stay, (block_flags, series_value, long_filter, step_table)),
        stay(mask_embed.reshape(1, width)),
    )
    if not direct:
        made = made.reshape(2, tm, own, rows).transpose(1, 0, 2, 3)
    both = lax.all_to_all(made, "tm", split_axis=0, concat_axis=0, tiled=True)

    gate_own = lax.dynamic_slice_in_dim(series_gate, core * block, block, 0)
    gate_other = lax.dynamic_slice_in_dim(series_gate, (1 - core) * block, block, 0)
    gates = (gate_own, swap(gate_other, 1), swap(gate_own, 2), swap(gate_other, 3))
    wg1, wu1, wd1 = swap(w_gate, 1), swap(w_up, 1), swap(w_down, 1)

    skip = lax.dynamic_slice_in_dim(skip_gain, lax.axis_index("tm") * own, own, 0)
    skip = skip.reshape(own, 1)
    held = own
    if not direct:
        held = -(-own // 16) * 16
        both = jnp.pad(both, ((0, 0), (0, 0), (0, held - own), (0, 0)))
        skip = jnp.pad(skip, ((0, held - own), (0, 0)))
    both, gates = lax.optimization_barrier((both, gates))
    tables = [jnp.asarray(table) for table in block_tables(block)]
    tables = tables[:2] + [stay(table) for table in tables[2:]]
    conv = pl.pallas_call(
        convolve_kernel,
        out_shape=jax.ShapeDtypeStruct((tm, 2, held, block), bf16),
        in_specs=[whole(SMEM)] + [whole()] * 3 + [whole(HBM)] * 2 + [whole()],
        out_specs=whole(),
        scratch_shapes=[pltpu.VMEM((tm, 2, held, 2 * block), f32)] * 3
        + [pltpu.VMEM(table.shape, bf16) for table in tables[2:]]
        + [pltpu.SemaphoreType.DMA((2,))],
        compiler_params=params(24),
        name="convolve",
    )(place[1], both, *tables, skip)
    if not direct:
        conv = conv[:, :, :own]

    conv = lax.all_to_all(conv, "tm", split_axis=0, concat_axis=0, tiled=True)
    mine, theirs = conv[:, 0], conv[:, 1]
    aside, across = swap(mine, 2), swap(theirs, 3)

    def view(values):
        return values if direct else values.reshape(1, width, block)

    gain = norm_gain.reshape(4, 1, width)
    held = [
        ((block, width), bf16),
        ((block, 1), f32),
        ((4, 1, width), f32),
        ((4, block, w_gate.shape[1]), f32),
        ((4, width, w_gate.shape[1]), bf16),
        ((4, 2 * width, w_gate.shape[1]), bf16),
        ((2 * w_down.shape[0], w_down.shape[1]), bf16),
    ]
    kept = pl.pallas_call(
        feed_first_kernel,
        out_shape=[jax.ShapeDtypeStruct(*spec) for spec in held],
        in_specs=[whole(SMEM)] * 2 + [whole()] * 2 + [whole(HBM)] * 7,
        out_specs=[whole()] * 7,
        scratch_shapes=[
            pltpu.VMEM((block, width), bf16),
            pltpu.VMEM((4, width, w_gate.shape[1]), bf16),
            pltpu.SemaphoreType.DMA((19,)),
        ],
        compiler_params=params(24),
        name="feed_first",
    )(
        *place,
        view(mine),
        gates[0],
        *map(stay, (gain, w_gate, w_up, wg1, wu1, w_down, wd1)),
    )
    theirs, aside, kept = lax.optimization_barrier((theirs, aside, kept))
    beside = swap(theirs, 1)
    mixed0, square, gain, sums, straight, rest, down = kept
    square, sums = pl.pallas_call(
        feed_middle_kernel,
        out_shape=[jax.ShapeDtypeStruct(*held[1]), jax.ShapeDtypeStruct(*held[3])],
        in_specs=[whole(SMEM)] * 2 + [whole()] * 6,
        out_specs=[whole()] * 2,
        scratch_shapes=[pltpu.VMEM((block, width), bf16)],
        compiler_params=params(24),
        name="feed_middle",
    )(*place, view(aside), gates[2], square, gain, sums, straight)
    shape = jax.ShapeDtypeStruct((block, width), bf16)
    mixed1, hidden, *remote = pl.pallas_call(
        feed_second_kernel,
        out_shape=[shape, jax.ShapeDtypeStruct((block, 2 * w_gate.shape[1]), bf16), shape, shape],
        in_specs=[whole(SMEM)] * 2 + [whole()] * 9,
        out_specs=[whole()] * 4,
        scratch_shapes=[pltpu.VMEM((block, 2 * width), bf16)],
        compiler_params=params(24),
        name="feed_second",
    )(
        *place,
        view(beside),
        view(across),
        gates[1],
        gates[3],
        square,
        gain,
        sums,
        rest,
        down,
    )
    side, side1 = swap(remote[0], 2), swap(remote[1], 3)
    local = pl.pallas_call(
        feed_third_kernel,
        out_shape=[jax.ShapeDtypeStruct((block, width), f32), shape],
        in_specs=[whole(SMEM)] * 2 + [whole()] * 4,
        out_specs=[whole()] * 2,
        compiler_params=params(16),
        name="feed_third",
    )(*place, hidden, down, mixed0, mixed1)
    owned, lent = local
    lent, side = lax.optimization_barrier((lent, side))
    half = finish(0, place[1], owned, side)
    return finish(1, place[1], swap(lent, 1), side1, half)


def solution(mesh):
    axes = mesh.devices.reshape(mesh.shape["tm"], mesh.shape["chan"] // 2, 2)
    mesh = jax.sharding.Mesh(axes, ("tm", "x", "core"))
    chan = ("x", "core")
    placed = (
        P("tm", chan),
        P("tm", chan),
        P("tm", chan),
        P(None, chan),
        P(),
        P(chan),
        P("tm"),
        P(chan),
        P(),
        P(None, chan),
        P(None, chan),
        P(chan, None),
    )
    return jax.shard_map(
        shards, mesh=mesh, in_specs=placed, out_specs=P("tm", chan), check_vma=False
    )
```

```python
import functools

import jax
import jax.numpy as jnp
import numpy as np
from jax import lax
from jax.experimental import pallas as pl
from jax.experimental.pallas import tpu as pltpu
from jax.sharding import PartitionSpec as P

FLAGBLK = 64
bf16 = jnp.bfloat16
f32 = jnp.float32


def split_table(table):
    high = table.astype(bf16)
    low = (table - high.astype(np.float64)).astype(bf16)
    return high, low


def block_tables(block):
    freq = np.concatenate([np.arange(0, block, 2), np.arange(1, block, 2)])
    time = np.arange(block)
    turn = np.pi * ((2 * freq[None, :] + 1) * time[:, None] % (4 * block)) / (2 * block)
    forward = np.concatenate([np.cos(turn), -np.sin(turn)], axis=1)
    turn = np.pi * ((2 * freq[:, None] + 1) * (block + time[None, :]) % (4 * block)) / (2 * block)
    inverse = np.concatenate([np.cos(turn), -np.sin(turn)], axis=0) / block
    return split_table(forward) + split_table(inverse)


def dot(left, right):
    return jnp.dot(left, right, preferred_element_type=f32)


def start_loads(pairs, sems):
    loads = [
        pltpu.make_async_copy(src, dst, sems.at[at]) for at, (src, dst) in enumerate(pairs)
    ]
    for load in loads:
        load.start()
    return loads


def prepare_kernel(
    step_ref,
    flags_hbm,
    value_hbm,
    filter_hbm,
    table_hbm,
    mask_hbm,
    out_hbm,
    flags_ref,
    value_ref,
    filter_ref,
    table_ref,
    mask_ref,
    out_ref,
    sems,
    out_sems,
):
    loads = start_loads(
        (
            (filter_hbm, filter_ref),
            (value_hbm, value_ref),
            (flags_hbm, flags_ref),
            (table_hbm, table_ref),
            (mask_hbm, mask_ref),
        ),
        sems,
    )
    rows, width = value_ref.shape
    groups = out_ref.shape[0]
    lanes = 128
    stores = []

    def store(which, low, values):
        share = groups * lanes // width
        first = groups * low // width
        part = out_ref.at[pl.ds(first, share), which]
        part[...] = values.T.reshape(part.shape)
        copy = pltpu.make_async_copy(
            part, out_hbm.at[pl.ds(first, share), which], out_sems.at[len(stores)]
        )
        copy.start()
        stores.append(copy)

    steps = width // lanes if groups * lanes % width == 0 else 1
    lanes = width // steps
    loads[0].wait()
    for low in range(0, width, lanes):
        store(1, low, filter_ref[:, low : low + lanes])
    for load in loads[1:]:
        load.wait()
    embed = table_ref[pl.ds(step_ref[0], 1), :]
    mask = mask_ref[...]
    for low in range(0, width, lanes):
        here = slice(low, low + lanes)
        parts = []
        for at in range(rows // FLAGBLK):
            values = value_ref[at * FLAGBLK : (at + 1) * FLAGBLK, here].astype(f32)
            flag = flags_ref[at].astype(f32)
            parts.append((values + embed[:, here] + flag * mask[:, here]).astype(bf16))
        store(0, low, jnp.concatenate(parts, axis=0))
    for copy in stores:
        copy.wait()


def convolve_kernel(
    core_ref,
    both_ref,
    fh_ref,
    fl_ref,
    gh_hbm,
    gl_hbm,
    skip_ref,
    out_ref,
    x_ref,
    h_ref,
    z_ref,
    gh_ref,
    gl_ref,
    sems,
):
    loads = start_loads(((gh_hbm, gh_ref), (gl_hbm, gl_ref)), sems)
    tm, _, chans, rows = both_ref.shape
    block = rows // 2
    half = block // 2
    nb = 2 * tm
    for which, dst in ((0, x_ref), (1, h_ref)):
        for part in range(2):
            data = both_ref[:, which, :, part * block : (part + 1) * block]
            data = data.reshape(tm * chans, block)
            spec = dot(data, fh_ref[...]) + dot(data, fl_ref[...])
            dst[:, part] = spec.reshape(tm, chans, 2 * block)

    def read(ref, at, sub, lanes):
        return ref[at // 2, at % 2, sub, lanes]

    def window(prev_re, prev_im, cur_re, cur_im, odd):
        if odd:
            return prev_re - cur_im, prev_im + cur_re
        return prev_re + cur_im, prev_im - cur_re

    def tile(step, carry):
        sub = pl.ds(pl.multiple_of(step * 8, 8), 8)
        width = min(128, half)
        for odd in range(2):
            for low in range(odd * half, (odd + 1) * half, width):
                re = slice(low, low + width)
                im = slice(block + low, block + low + width)
                zero = jnp.zeros((8, width), f32)

                def put(a, acc):
                    z_ref[a // 2, a % 2, sub, re] = acc[0] - acc[1]
                    z_ref[a // 2, a % 2, sub, im] = acc[2] - acc[0] - acc[1]

                def load(at):
                    xr, xi = read(x_ref, at, sub, re), read(x_ref, at, sub, im)
                    return xr, xi, xr + xi

                if nb <= 16:
                    taps = []
                    prev = (zero, zero)
                    for d in range(nb):
                        cur = read(h_ref, d, sub, re), read(h_ref, d, sub, im)
                        wr, wi = window(*prev, *cur, odd)
                        taps.append((wr, wi, wr + wi))
                        prev = cur
                    values = [load(at) for at in range(nb)]
                    for a in range(nb):
                        acc = None
                        for d in range(a + 1):
                            terms = [v * t for v, t in zip(values[a - d], taps[d])]
                            acc = terms if acc is None else [p + q for p, q in zip(acc, terms)]
                        put(a, acc)
                else:

                    def out_block(a, carry):
                        def pair(d, acc):
                            before = jnp.maximum(d - 1, 0)
                            keep = (d > 0).astype(f32)
                            wr, wi = window(
                                keep * read(h_ref, before, sub, re),
                                keep * read(h_ref, before, sub, im),
                                read(h_ref, d, sub, re),
                                read(h_ref, d, sub, im),
                                odd,
                            )
                            terms = zip(acc, load(a - d), (wr, wi, wr + wi))
                            return tuple(p + v * t for p, v, t in terms)

                        put(a, lax.fori_loop(0, a + 1, pair, (zero, zero, zero)))
                        return carry

                    lax.fori_loop(0, nb, out_block, 0)
        return carry

    lax.fori_loop(0, chans // 8, tile, 0)
    for load in loads:
        load.wait()
    skip = skip_ref[...]
    spec = z_ref[...].reshape(nb * chans, 2 * block)
    high = spec.astype(bf16)
    low = (spec - high.astype(f32)).astype(bf16)
    conv = dot(high, gh_ref[...]) + dot(low, gh_ref[...]) + dot(high, gl_ref[...])
    conv = conv.reshape(tm, 2, chans, block)
    for part in range(2):
        inputs = both_ref[:, 0, :, part * block : (part + 1) * block].astype(f32)
        total = conv[:, part] + skip[None] * inputs
        out_ref[:, part ^ core_ref[0]] = total.astype(bf16)


def mix(conv_refs, gate_refs, ats, mixed_ref, ready_ref, gain_ref, square):
    rows, width = gate_refs[0].shape
    for j, (conv_ref, gate_ref, at) in enumerate(zip(conv_refs, gate_refs, ats)):
        conv = conv_ref[...].reshape(width, rows).T.astype(f32)
        mixed = (gate_ref[...].astype(f32) * conv).astype(bf16)
        if j == 0 and mixed_ref is not None:
            mixed_ref[...] = mixed
        wide = mixed.astype(f32)
        square = square + jnp.sum(wide * wide, axis=-1, keepdims=True)
        ready_ref[:, j * width : (j + 1) * width] = (wide * gain_ref[at]).astype(bf16)
    return square


def feed_first_kernel(
    chip_ref,
    core_ref,
    conv0_ref,
    gate0_ref,
    gain_hbm,
    wg0_hbm,
    wu0_hbm,
    wg1_hbm,
    wu1_hbm,
    wd0_hbm,
    wd1_hbm,
    mixed_ref,
    square_ref,
    gain_ref,
    sums_ref,
    straight_ref,
    rest_ref,
    down_ref,
    ready_ref,
    now_ref,
    sems,
):
    here = 2 * chip_ref[0] + core_ref[0]
    rows, width = gate0_ref.shape
    hidden = wd0_hbm.shape[0]
    weights = (wg0_hbm, wu0_hbm, wg1_hbm, wu1_hbm)

    def source(weight, j):
        return weight.at[pl.ds(pl.multiple_of((here ^ j) * width, width), width)]

    loads = start_loads(
        [(gain_hbm, gain_ref)]
        + [(source(weight, 0), now_ref.at[at]) for at, weight in enumerate(weights)]
        + [(source(weight, 2), straight_ref.at[at]) for at, weight in enumerate(weights)]
        + [
            (source(weight, j), rest_ref.at[at, pl.ds(first, width)])
            for j, first in ((1, 0), (3, width))
            for at, weight in enumerate(weights)
        ]
        + [
            (weight, down_ref.at[pl.ds(at * hidden, hidden)])
            for at, weight in enumerate((wd0_hbm, wd1_hbm))
        ],
        sems,
    )
    loads[0].wait()
    square_ref[...] = mix(
        (conv0_ref,),
        (gate0_ref,),
        (here,),
        mixed_ref,
        ready_ref,
        gain_ref,
        jnp.zeros((rows, 1), f32),
    )
    ready = ready_ref[...]
    for at in range(4):
        loads[1 + at].wait()
        sums_ref[at] = dot(ready, now_ref[at])
    for load in loads[5:]:
        load.wait()


def feed_middle_kernel(
    chip_ref,
    core_ref,
    conv2_ref,
    gate2_ref,
    square_ref,
    gain_ref,
    sums_ref,
    straight_ref,
    square_out_ref,
    sums_out_ref,
    ready_ref,
):
    here = 2 * chip_ref[0] + core_ref[0]
    square_out_ref[...] = mix(
        (conv2_ref,), (gate2_ref,), (here ^ 2,), None, ready_ref, gain_ref, square_ref[...]
    )
    ready = ready_ref[...]
    for at in range(4):
        sums_out_ref[at] = sums_ref[at] + dot(ready, straight_ref[at])


def feed_second_kernel(
    chip_ref,
    core_ref,
    conv1_ref,
    conv3_ref,
    gate1_ref,
    gate3_ref,
    square_ref,
    gain_ref,
    sums_ref,
    rest_ref,
    down_ref,
    mixed_ref,
    hidden_ref,
    out2_ref,
    out3_ref,
    ready_ref,
):
    here = 2 * chip_ref[0] + core_ref[0]
    width = gate1_ref.shape[1]
    square = mix(
        (conv1_ref, conv3_ref),
        (gate1_ref, gate3_ref),
        (here ^ 1, here ^ 3),
        mixed_ref,
        ready_ref,
        gain_ref,
        square_ref[...],
    )
    scale = lax.rsqrt(square / (gain_ref.shape[0] * width) + 1e-06)
    ready = ready_ref[...]
    parts = []
    for at in range(2):
        gate = scale * (sums_ref[2 * at] + dot(ready, rest_ref[2 * at]))
        up = scale * (sums_ref[2 * at + 1] + dot(ready, rest_ref[2 * at + 1]))
        parts.append((gate / (1.0 + jnp.exp(-gate)) * up).astype(bf16))
    size = parts[0].shape[1]
    for at, values in enumerate(parts):
        hidden_ref[:, at * size : (at + 1) * size] = values
    away = pl.ds(pl.multiple_of((1 - chip_ref[0]) * 2 * width, 2 * width), 2 * width)
    both = dot(parts[0], down_ref[:size, away]) + dot(parts[1], down_ref[size:, away])
    low, high = both[:, :width].astype(bf16), both[:, width:].astype(bf16)
    first = core_ref[0] == 0
    out2_ref[...] = jnp.where(first, low, high)
    out3_ref[...] = jnp.where(first, high, low)


def piece(hidden, down_ref, at, width):
    return dot(hidden, down_ref[:, pl.ds(pl.multiple_of(at * width, width), width)])


def feed_third_kernel(
    chip_ref, core_ref, hidden_ref, down_ref, mixed0_ref, mixed1_ref, out0_ref, out1_ref
):
    here = 2 * chip_ref[0] + core_ref[0]
    width = out0_ref.shape[1]
    hidden = hidden_ref[...]
    for j, mixed_ref, out_ref in ((1, mixed1_ref, out1_ref), (0, mixed0_ref, out0_ref)):
        part = piece(hidden, down_ref, here ^ j, width) + mixed_ref[...].astype(f32)
        out_ref[...] = part.astype(out_ref.dtype)


def finish_kernel(flip, core_ref, base_ref, add_ref, *rest):
    out_hbm, sum_ref, sem = rest[-3:]
    block = base_ref.shape[0]
    first = (core_ref[0] ^ flip) * block
    sum_ref[...] = (base_ref[...].astype(f32) + add_ref[...].astype(f32)).astype(bf16)
    store = pltpu.make_async_copy(
        sum_ref, out_hbm.at[pl.ds(pl.multiple_of(first, block), block)], sem
    )
    store.start()
    store.wait()


def finish(flip, core, base, add, *into):
    block, width = base.shape
    return pl.pallas_call(
        functools.partial(finish_kernel, flip),
        out_shape=jax.ShapeDtypeStruct((2 * block, width), bf16),
        in_specs=[whole(SMEM)] + [whole()] * 2 + [whole(HBM)] * len(into),
        out_specs=whole(HBM),
        scratch_shapes=[pltpu.VMEM((block, width), bf16), pltpu.SemaphoreType.DMA],
        input_output_aliases={3: 0} if into else {},
        compiler_params=params(8),
        name="finish",
    )(core, base, add, *into)


VMEM = pltpu.MemorySpace.VMEM
SMEM = pltpu.MemorySpace.SMEM
HBM = pltpu.MemorySpace.HBM


def whole(space=VMEM):
    return pl.BlockSpec(memory_space=space)


def stay(array):
    return pltpu.with_memory_space_constraint(array, HBM)


def params(mib):
    return pltpu.CompilerParams(vmem_limit_bytes=mib << 20)


def shards(
    series_value,
    series_gate,
    long_filter,
    step_table,
    diffusion_step,
    mask_embed,
    block_flags,
    skip_gain,
    norm_gain,
    w_gate,
    w_up,
    w_down,
):
    tm = lax.axis_size("tm")
    chip, core = lax.axis_index("x"), lax.axis_index("core")
    place = chip.reshape(1).astype(jnp.int32), core.reshape(1).astype(jnp.int32)
    rows, width = series_value.shape
    own = width // tm
    block = rows // 2

    def swap(values, bits):
        return lax.ppermute(values, ("x", "core"), [(at, at ^ bits) for at in range(4)])

    direct = own % 16 == 0
    shape = (tm, 2, own, rows) if direct else (1, 2, width, rows)
    made = pl.pallas_call(
        prepare_kernel,
        out_shape=jax.ShapeDtypeStruct(shape, bf16),
        in_specs=[whole(SMEM)] + [whole(HBM)] * 5,
        out_specs=whole(HBM),
        scratch_shapes=[
            pltpu.SMEM(block_flags.shape, jnp.int32),
            pltpu.VMEM(series_value.shape, bf16),
            pltpu.VMEM(long_filter.shape, bf16),
            pltpu.VMEM(step_table.shape, f32),
            pltpu.VMEM((1, width), f32),
            pltpu.VMEM(shape, bf16),
            pltpu.SemaphoreType.DMA((5,)),
            pltpu.SemaphoreType.DMA((2 * max(1, width // 128),)),
        ],
        compiler_params=params(32),
        name="prepare",
    )(
        diffusion_step,
        *map(stay, (block_flags, series_value, long_filter, step_table)),
        stay(mask_embed.reshape(1, width)),
    )
    if not direct:
        made = made.reshape(2, tm, own, rows).transpose(1, 0, 2, 3)
    both = lax.all_to_all(made, "tm", split_axis=0, concat_axis=0, tiled=True)

    gate_own = lax.dynamic_slice_in_dim(series_gate, core * block, block, 0)
    gate_other = lax.dynamic_slice_in_dim(series_gate, (1 - core) * block, block, 0)
    gates = (gate_own, swap(gate_other, 1), swap(gate_own, 2), swap(gate_other, 3))
    wg1, wu1, wd1 = swap(w_gate, 1), swap(w_up, 1), swap(w_down, 1)

    skip = lax.dynamic_slice_in_dim(skip_gain, lax.axis_index("tm") * own, own, 0)
    skip = skip.reshape(own, 1)
    held = own
    if not direct:
        held = -(-own // 16) * 16
        both = jnp.pad(both, ((0, 0), (0, 0), (0, held - own), (0, 0)))
        skip = jnp.pad(skip, ((0, held - own), (0, 0)))
    both, gates = lax.optimization_barrier((both, gates))
    tables = [jnp.asarray(table) for table in block_tables(block)]
    tables = tables[:2] + [stay(table) for table in tables[2:]]
    conv = pl.pallas_call(
        convolve_kernel,
        out_shape=jax.ShapeDtypeStruct((tm, 2, held, block), bf16),
        in_specs=[whole(SMEM)] + [whole()] * 3 + [whole(HBM)] * 2 + [whole()],
        out_specs=whole(),
        scratch_shapes=[pltpu.VMEM((tm, 2, held, 2 * block), f32)] * 3
        + [pltpu.VMEM(table.shape, bf16) for table in tables[2:]]
        + [pltpu.SemaphoreType.DMA((2,))],
        compiler_params=params(24),
        name="convolve",
    )(place[1], both, *tables, skip)
    if not direct:
        conv = conv[:, :, :own]

    conv = lax.all_to_all(conv, "tm", split_axis=0, concat_axis=0, tiled=True)
    mine, theirs = conv[:, 0], conv[:, 1]
    aside, across = swap(mine, 2), swap(theirs, 3)

    def view(values):
        return values if direct else values.reshape(1, width, block)

    gain = norm_gain.reshape(4, 1, width)
    held = [
        ((block, width), bf16),
        ((block, 1), f32),
        ((4, 1, width), f32),
        ((4, block, w_gate.shape[1]), f32),
        ((4, width, w_gate.shape[1]), bf16),
        ((4, 2 * width, w_gate.shape[1]), bf16),
        ((2 * w_down.shape[0], w_down.shape[1]), bf16),
    ]
    kept = pl.pallas_call(
        feed_first_kernel,
        out_shape=[jax.ShapeDtypeStruct(*spec) for spec in held],
        in_specs=[whole(SMEM)] * 2 + [whole()] * 2 + [whole(HBM)] * 7,
        out_specs=[whole()] * 7,
        scratch_shapes=[
            pltpu.VMEM((block, width), bf16),
            pltpu.VMEM((4, width, w_gate.shape[1]), bf16),
            pltpu.SemaphoreType.DMA((19,)),
        ],
        compiler_params=params(24),
        name="feed_first",
    )(
        *place,
        view(mine),
        gates[0],
        *map(stay, (gain, w_gate, w_up, wg1, wu1, w_down, wd1)),
    )
    theirs, aside, kept = lax.optimization_barrier((theirs, aside, kept))
    beside = swap(theirs, 1)
    mixed0, square, gain, sums, straight, rest, down = kept
    square, sums = pl.pallas_call(
        feed_middle_kernel,
        out_shape=[jax.ShapeDtypeStruct(*held[1]), jax.ShapeDtypeStruct(*held[3])],
        in_specs=[whole(SMEM)] * 2 + [whole()] * 6,
        out_specs=[whole()] * 2,
        scratch_shapes=[pltpu.VMEM((block, width), bf16)],
        compiler_params=params(24),
        name="feed_middle",
    )(*place, view(aside), gates[2], square, gain, sums, straight)
    shape = jax.ShapeDtypeStruct((block, width), bf16)
    mixed1, hidden, *remote = pl.pallas_call(
        feed_second_kernel,
        out_shape=[shape, jax.ShapeDtypeStruct((block, 2 * w_gate.shape[1]), bf16), shape, shape],
        in_specs=[whole(SMEM)] * 2 + [whole()] * 9,
        out_specs=[whole()] * 4,
        scratch_shapes=[pltpu.VMEM((block, 2 * width), bf16)],
        compiler_params=params(24),
        name="feed_second",
    )(
        *place,
        view(beside),
        view(across),
        gates[1],
        gates[3],
        square,
        gain,
        sums,
        rest,
        down,
    )
    side, side1 = swap(remote[0], 2), swap(remote[1], 3)
    local = pl.pallas_call(
        feed_third_kernel,
        out_shape=[jax.ShapeDtypeStruct((block, width), f32), shape],
        in_specs=[whole(SMEM)] * 2 + [whole()] * 4,
        out_specs=[whole()] * 2,
        compiler_params=params(16),
        name="feed_third",
    )(*place, hidden, down, mixed0, mixed1)
    owned, lent = local
    lent, side = lax.optimization_barrier((lent, side))
    half = finish(0, place[1], owned, side)
    return finish(1, place[1], swap(lent, 1), side1, half)


def solution(mesh):
    axes = mesh.devices.reshape(mesh.shape["tm"], mesh.shape["chan"] // 2, 2)
    mesh = jax.sharding.Mesh(axes, ("tm", "x", "core"))
    chan = ("x", "core")
    placed = (
        P("tm", chan),
        P("tm", chan),
        P("tm", chan),
        P(None, chan),
        P(),
        P(chan),
        P("tm"),
        P(chan),
        P(),
        P(None, chan),
        P(None, chan),
        P(chan, None),
    )
    return jax.shard_map(
        shards, mesh=mesh, in_specs=placed, out_specs=P("tm", chan), check_vma=False
    )
```
